32 devices in a mesh: groups: 2 (over y), node: 4 (over z), rep: 4 (over x, core).
Axes of the slice: x: 2, y: 2, z: 4, core: 2. Of those that a mesh axis runs over, the one named last changes fastest.
Arguments:
- node_states: bfloat16 [8, 512, 512], P(('groups', 'rep'), 'node'), parts along dimension 0, may hold values from -6 to 6
- cotangent: bfloat16 [8, 512, 512], P(('groups', 'rep'), 'node'), parts along dimension 0, may hold values from -1.1953125 to 1.1953125
- reach_blocks: int32 [8, 8, 8], P(('groups', 'rep'), 'node'), parts along dimension 0, may hold values from 0 to 7, as said below
- reach_count: int32 [8, 8], P(('groups', 'rep'), 'node'), parts along dimension 0, may hold values from 1 to 8, as said below
- level_start: int32 [8, 17], P(('groups', 'rep')), parts along dimension 0, may hold values from 0 to 512, as said below
- query_weight: bfloat16 [512, 256], replicated, may hold values from -0.25 to 0.25
- key_weight: bfloat16 [512, 256], replicated, may hold values from -0.25 to 0.25
- value_weight: bfloat16 [512, 256], replicated, may hold values from -0.25 to 0.25
- out_weight: bfloat16 [256, 512], replicated, may hold values from -0.375 to 0.375
- bias_table: float32 [4, 32], replicated, may hold values from -4 to 412
Outputs:
- updated: bfloat16 [8, 512, 512], P(('groups', 'rep'), 'node'), parts along dimension 0
- node_state_gradient: bfloat16 [8, 512, 512], P(('groups', 'rep'), 'node'), parts along dimension 0
- grad_query: float32 [1024, 256], P('groups'), parts along dimension 0
- grad_key: float32 [1024, 256], P('groups'), parts along dimension 0
- grad_value: float32 [1024, 256], P('groups'), parts along dimension 0
- grad_out: float32 [512, 512], P('groups'), parts along dimension 0
The draws below stay inside these ranges and needn't reach their ends.
There are 2 independent parts, one for each index of `groups`. The reference program is written for one: setup_inputs(seed, part) draws one part's arguments, and reference() takes and returns one part's arrays. A program takes and returns all parts, laid end to end along the dimension named above; an argument that names none is the same for every part. Nothing has to cross between parts.
Inputs may be any that keep to these rules, and one draw needn't show every extreme that they name: `reach_blocks`: in row b of a graph, entry 0 is b, entries 1 to min(b, 7) are distinct blocks below b, and any later entries are b. `reach_count`: row b holds at most b + 1; row 7 of every graph holds 8. `level_start`: strictly increasing; entry 0 is 0 and entry 16 is 512.
All inputs are finite; a program needn't handle non-finite values.
Results may differ from the reference program's by a relative error of at most 0.011.
Values may be sent and summed in bfloat16 or wider, within the bound.
No kernel may reach another device: no remote copies, remote signals or barrier semaphores. Data moves between devices by JAX's collectives and lax.ppermute only.
A program may use at most 64 MiB of HBM per device.

```python
import jax
import jax.numpy as jnp
from jax import lax

D = 512
HEADS = 4
HEAD = 64
BLOCK = 64
DIST = 32
NODE_DEV = 128
HD = 256
NODES = 512
KBLOCKS = 8
MOST = 8
LEVELS = 16
GRAPHS = 4


def draw_reach_blocks(key, part):
    base = jax.random.fold_in(key, 11)
    index = jnp.arange(KBLOCKS, dtype=jnp.int32)
    slots = jnp.arange(MOST, dtype=jnp.int32)

    def one_graph(graph_key):

        def one_row(block):
            ranks = jax.random.permutation(jax.random.fold_in(graph_key, 100 + block), KBLOCKS).astype(jnp.int32)
            score = jnp.where(index < block, ranks, KBLOCKS + index)
            order = jnp.argsort(score, stable=True).astype(jnp.int32)
            picked = order[jnp.maximum(slots - 1, 0)]
            below = (slots >= 1) & (slots - 1 < block)
            return jnp.where(below, picked, block).astype(jnp.int32)
        return jax.vmap(one_row)(index)
    return jax.vmap(one_graph)(jax.random.split(base, GRAPHS))


def draw_reach_count(key, part):
    base = jax.random.fold_in(key, 13)
    index = jnp.arange(KBLOCKS, dtype=jnp.int32)

    def one_graph(graph_key):
        first_draw = jax.random.randint(jax.random.fold_in(graph_key, 1), (KBLOCKS,), 1, MOST + 1)
        second_draw = jax.random.randint(jax.random.fold_in(graph_key, 2), (KBLOCKS,), 1, MOST + 1)
        raw = jnp.maximum(first_draw * second_draw // MOST, 1)
        count = jnp.minimum(raw, index + 1)
        return jnp.where(index == KBLOCKS - 1, MOST, count).astype(jnp.int32)
    return jax.vmap(one_graph)(jax.random.split(base, GRAPHS))


def draw_level_start(key, part):

    def one_graph(graph_key):
        cuts = jax.random.permutation(graph_key, NODES - 1)[:LEVELS - 1].astype(jnp.int32) + 1
        cuts = jnp.sort(cuts)
        return jnp.concatenate([jnp.zeros((1,), jnp.int32), cuts, jnp.full((1,), NODES, jnp.int32)])
    return jax.vmap(one_graph)(jax.random.split(jax.random.fold_in(key, 3), GRAPHS))


def draw_bias_table(key, part):
    base = jnp.clip(jax.random.normal(jax.random.fold_in(key, 5), (HEADS, DIST), jnp.float32) * 1.5, -4.0, 4.0)
    return base


def block_levels(own_key, shape, cuts, smallest, top_value):
    loudness = 1.0
    for position, blocks in cuts:
        draws = jax.random.uniform(jax.random.fold_in(jax.random.fold_in(own_key, 6), position), (blocks,), jnp.float32, smallest / len(cuts), top_value / len(cuts))
        loudness = loudness * jnp.repeat(jnp.exp(draws), shape[position] // blocks).reshape((-1,) + (1,) * (len(shape) - 1 - position))
    return loudness


def noise(rng, shape, scale, most, shards=(), held_as=jnp.bfloat16):
    gain = block_levels(rng, shape, shards, -0.22, 0.18) if shards else 1.0
    entries = jax.random.normal(rng, shape, jnp.float32) * scale * gain
    return jnp.minimum(jnp.maximum(entries, -most), most).astype(held_as)


def setup_inputs(seed: int = 0, part: int = 0) -> dict:
    splits = jax.random.split(jax.random.key(seed), 11)
    part_keys = jax.random.split(jax.random.fold_in(splits[10], part), 11)
    node_states = noise(part_keys[0], (GRAPHS, NODES, D), 1.0, 6.0, ((0, 4), (1, 4)))
    cotangent = noise(part_keys[1], (GRAPHS, NODES, D), 0.2, 1.1953125, ((0, 4), (1, 4)))
    reach_blocks = draw_reach_blocks(jax.random.fold_in(jax.random.fold_in(splits[10], part), 71), part)
    reach_count = draw_reach_count(jax.random.fold_in(jax.random.fold_in(splits[10], part), 71), part)
    level_start = draw_level_start(jax.random.fold_in(jax.random.fold_in(splits[10], part), 71), part)
    query_weight = noise(splits[5], (D, HD), D ** -0.5, 0.25)
    key_weight = noise(splits[6], (D, HD), D ** -0.5, 0.25)
    value_weight = noise(splits[7], (D, HD), D ** -0.5, 0.25)
    out_weight = noise(splits[8], (HD, D), HD ** -0.5, 0.375)
    bias_table = draw_bias_table(jax.random.fold_in(splits[10], 71), part)
    return dict(node_states=node_states, cotangent=cotangent, reach_blocks=reach_blocks, reach_count=reach_count, level_start=level_start, query_weight=query_weight, key_weight=key_weight, value_weight=value_weight, out_weight=out_weight, bias_table=bias_table)


EPS = 1e-05
NEG = -1e+30

def node_levels(starts):
    places = jnp.arange(NODES, dtype=jnp.int32)
    inner = starts[1:LEVELS]
    return lax.optimization_barrier(jnp.sum((places[:, None] >= inner[None, :]).astype(jnp.int32), axis=1))

def block_table(blocks, counts):
    slots = jnp.arange(MOST, dtype=jnp.int32)
    live = slots[None, :] < counts[:, None]
    kinds = jnp.arange(KBLOCKS, dtype=jnp.int32)
    hits = (blocks[:, :, None] == kinds[None, None, :]) & live[:, :, None]
    return jnp.any(hits, axis=1)

def graph_pass(states, cotangent, blocks, counts, starts, query_weight, key_weight, value_weight, out_weight, bias_table):
    single_float_type = jnp.float32
    brain_float_sixteen = jnp.bfloat16
    scale = HEAD ** (-0.5)
    states_single_float = states.astype(single_float_type)
    inverse_norm_scale = lax.rsqrt(lax.optimization_barrier(jnp.mean(states_single_float * states_single_float, axis=1, keepdims=True)) + EPS)
    centered_states = states_single_float * inverse_norm_scale
    normalized_states = centered_states.astype(brain_float_sixteen)
    queries = jnp.dot(normalized_states, query_weight, preferred_element_type=single_float_type).astype(brain_float_sixteen)
    keys = jnp.dot(normalized_states, key_weight, preferred_element_type=single_float_type).astype(brain_float_sixteen)
    values = jnp.dot(normalized_states, value_weight, preferred_element_type=single_float_type).astype(brain_float_sixteen)
    levels = node_levels(starts)
    table = block_table(blocks, counts)
    positions = jnp.arange(NODES, dtype=jnp.int32)
    key_heads = keys.astype(single_float_type).reshape(NODES, HEADS, HEAD)
    value_heads = values.astype(single_float_type).reshape(NODES, HEADS, HEAD)

    def one_shard(carry, index):
        lower = index * NODE_DEV
        rows = lower + jnp.arange(NODE_DEV, dtype=jnp.int32)
        query_rows = lax.dynamic_slice_in_dim(queries, lower, NODE_DEV, 0).astype(single_float_type).reshape(NODE_DEV, HEADS, HEAD)
        state_rows = lax.dynamic_slice_in_dim(states_single_float, lower, NODE_DEV, 0)
        grad_rows = lax.dynamic_slice_in_dim(cotangent, lower, NODE_DEV, 0)
        row_levels = levels[rows]
        block_rows = table[rows // BLOCK][:, positions // BLOCK]
        visible = block_rows & ((levels[None, :] < row_levels[:, None]) | (positions[None, :] == rows[:, None]))
        distance = jnp.clip(row_levels[:, None] - levels[None, :], 0, DIST - 1)
        scores = jnp.einsum('qhe,khe->hqk', query_rows, key_heads) * scale + bias_table[:, distance]
        scores = jnp.where(visible[None], scores, NEG)
        peak = lax.optimization_barrier(jnp.max(scores, axis=2, keepdims=True))
        mass = lax.optimization_barrier(jnp.sum(jnp.where(visible[None], jnp.exp(scores - peak), 0.0), axis=2, keepdims=True))
        lse = peak + jnp.log(mass)
        probs = jnp.where(visible[None], jnp.exp(scores - lse), 0.0).astype(brain_float_sixteen)
        probs_f = probs.astype(single_float_type)
        mixed = jnp.einsum('hqk,khe->qhe', probs_f, value_heads).reshape(NODE_DEV, HD).astype(brain_float_sixteen)
        updated = (state_rows + jnp.dot(mixed, out_weight, preferred_element_type=single_float_type)).astype(brain_float_sixteen)
        d_mixed = jnp.dot(grad_rows, out_weight.T, preferred_element_type=single_float_type).astype(brain_float_sixteen)
        mixed_grad = d_mixed.astype(single_float_type).reshape(NODE_DEV, HEADS, HEAD)
        delta = jnp.einsum('qhe,qhe->hq', mixed_grad, mixed.astype(single_float_type).reshape(NODE_DEV, HEADS, HEAD))
        d_probs = jnp.einsum('qhe,khe->hqk', mixed_grad, value_heads)
        d_scores = (probs_f * (d_probs - delta[:, :, None])).astype(brain_float_sixteen)
        score_grad = d_scores.astype(single_float_type)
        d_queries = (jnp.einsum('hqk,khe->qhe', score_grad, key_heads) * scale).reshape(NODE_DEV, HD).astype(brain_float_sixteen)
        key_part = (jnp.einsum('hqk,qhe->khe', score_grad, query_rows) * scale).reshape(NODES, HD)
        value_part = jnp.einsum('hqk,qhe->khe', probs_f, mixed_grad).reshape(NODES, HD)
        key_part = lax.optimization_barrier(key_part.astype(brain_float_sixteen)).astype(single_float_type)
        value_part = lax.optimization_barrier(value_part.astype(brain_float_sixteen)).astype(single_float_type)
        return ((carry[0] + key_part, carry[1] + value_part), (updated, mixed, d_queries))
    start = (jnp.zeros((NODES, HD), single_float_type), jnp.zeros((NODES, HD), single_float_type))
    shard_ids = jnp.arange(NODES // NODE_DEV, dtype=jnp.int32)
    sums, outputs = lax.scan(one_shard, start, shard_ids)
    updated = outputs[0].reshape(NODES, D)
    mixed = outputs[1].reshape(NODES, HD)
    d_queries = outputs[2].reshape(NODES, HD)
    d_keys = sums[0].astype(brain_float_sixteen)
    d_values = sums[1].astype(brain_float_sixteen)
    normalized_gradient = jnp.dot(d_queries, query_weight.T, preferred_element_type=single_float_type) + jnp.dot(d_keys, key_weight.T, preferred_element_type=single_float_type) + jnp.dot(d_values, value_weight.T, preferred_element_type=single_float_type)
    node_state_gradient = (cotangent.astype(single_float_type) + inverse_norm_scale * (normalized_gradient - centered_states * lax.optimization_barrier(jnp.mean(normalized_gradient * centered_states, axis=1, keepdims=True)))).astype(brain_float_sixteen)
    grad_query = jnp.dot(normalized_states.T, d_queries, preferred_element_type=single_float_type)
    grad_key = jnp.dot(normalized_states.T, d_keys, preferred_element_type=single_float_type)
    grad_value = jnp.dot(normalized_states.T, d_values, preferred_element_type=single_float_type)
    grad_out = jnp.dot(mixed.T, cotangent, preferred_element_type=single_float_type)
    return (updated, node_state_gradient, grad_query, grad_key, grad_value, grad_out)

def reference(node_states, cotangent, reach_blocks, reach_count, level_start, query_weight, key_weight, value_weight, out_weight, bias_table):
    updated_list = []
    grad_list = []
    totals = None
    for graph in range(GRAPHS):
        result = graph_pass(node_states[graph], cotangent[graph], reach_blocks[graph], reach_count[graph], level_start[graph], query_weight, key_weight, value_weight, out_weight, bias_table)
        updated_list.append(result[0])
        grad_list.append(result[1])
        if totals is None:
            totals = list(result[2:])
        else:
            totals = [left + right for left, right in zip(totals, result[2:])]
    return (jnp.stack(updated_list), jnp.stack(grad_list), totals[0], totals[1], totals[2], totals[3])
```

```python
import jax
import jax.numpy as jnp
from jax import lax
from jax.experimental import pallas as pl
from jax.experimental.pallas import tpu as pltpu
from jax.sharding import PartitionSpec as P

HEADS = 4
HEAD = 64
BLOCK = 64
DIST = 32


EPS = 1e-05
NEG = -1e30
HIGH = lax.Precision.HIGHEST
CONTRACT_ROWS = (((0,), (0,)), ((), ()))
CONTRACT_COLS = (((1,), (1,)), ((), ()))


def rows_product(left, right):
    return lax.dot_general(left, right, CONTRACT_ROWS, preferred_element_type=jnp.float32)


def cols_product(left, right):
    return lax.dot_general(left, right, CONTRACT_COLS, preferred_element_type=jnp.float32)


def expand(listed):
    return jnp.repeat(jnp.repeat(listed, BLOCK, axis=0), BLOCK, axis=1)


def level_tables(starts, total, bias_table):
    level_count = starts.shape[0] - 1
    places = jnp.arange(total, dtype=jnp.int32)
    inner = starts[1:level_count]
    levels = jnp.sum((places[:, None] >= inner[None, :]).astype(jnp.int32), axis=1)
    marks = jnp.arange(level_count, dtype=jnp.int32)
    onehot = (levels[:, None] == marks[None, :]).astype(jnp.float32)
    spread = jnp.clip(marks[:, None] - marks[None, :], 0, DIST - 1)
    picks = (spread[:, :, None] == jnp.arange(DIST, dtype=jnp.int32)[None, None, :]).astype(
        jnp.float32
    )
    level_bias = jnp.einsum("hd,abd->hab", bias_table, picks, precision=HIGH)
    return (levels, onehot, level_bias)


def bias_block(row_onehot, head_bias, col_onehot):
    row_part = jnp.dot(row_onehot, head_bias, precision=HIGH)
    return lax.dot_general(row_part, col_onehot, CONTRACT_COLS, precision=HIGH)


def on_device_general(
    node_states,
    cotangent,
    reach_blocks,
    reach_count,
    level_start,
    query_weight,
    key_weight,
    value_weight,
    out_weight,
    bias_table,
):
    states = node_states[0]
    grads_in = cotangent[0]
    blocks = reach_blocks[0]
    counts = reach_count[0]
    starts = level_start[0]
    rows_dev = states.shape[0]
    width = query_weight.shape[1]
    total = rows_dev * lax.axis_size("node")
    offset = lax.axis_index("node") * rows_dev
    scale = HEAD ** (-0.5)
    key_blocks = total // BLOCK
    states_single_float = states.astype(jnp.float32)
    inverse_norm_scale = lax.rsqrt(
        jnp.mean(states_single_float * states_single_float, axis=1, keepdims=True) + EPS
    )
    centered_states = states_single_float * inverse_norm_scale
    normalized_states = centered_states.astype(jnp.bfloat16)
    queries = jnp.dot(normalized_states, query_weight, preferred_element_type=jnp.float32).astype(
        jnp.bfloat16
    )
    keys = jnp.dot(normalized_states, key_weight, preferred_element_type=jnp.float32).astype(
        jnp.bfloat16
    )
    values = jnp.dot(normalized_states, value_weight, preferred_element_type=jnp.float32).astype(
        jnp.bfloat16
    )
    keys_all, values_all = (
        lax.all_gather(keys, "node", axis=0, tiled=True),
        lax.all_gather(values, "node", axis=0, tiled=True),
    )
    levels, onehot, level_bias = level_tables(starts, total, bias_table)
    positions = jnp.arange(total, dtype=jnp.int32)
    local = jnp.arange(rows_dev, dtype=jnp.int32)
    row_ids = offset + local
    row_levels = lax.dynamic_slice_in_dim(levels, offset, rows_dev, 0)
    row_onehot = lax.dynamic_slice_in_dim(onehot, offset, rows_dev, 0)
    slots = jnp.arange(blocks.shape[1], dtype=jnp.int32)
    live = slots[None, :] < counts[:, None]
    kinds = jnp.arange(key_blocks, dtype=jnp.int32)
    listed = jnp.any((blocks[:, :, None] == kinds[None, None, :]) & live[:, :, None], axis=1)
    visible = expand(listed) & (
        (levels[None, :] < row_levels[:, None]) | (positions[None, :] == row_ids[:, None])
    )
    prob_list = []
    lse_list = []
    mixed_list = []
    for head in range(HEADS):
        lower = head * HEAD
        scores = (
            cols_product(queries[:, lower : lower + HEAD], keys_all[:, lower : lower + HEAD])
            * scale
        )
        scores = scores + bias_block(row_onehot, level_bias[head], onehot)
        scores = jnp.where(visible, scores, NEG)
        peak = jnp.max(scores, axis=1, keepdims=True)
        mass = jnp.sum(jnp.where(visible, jnp.exp(scores - peak), 0.0), axis=1, keepdims=True)
        lse = peak + jnp.log(mass)
        probs = jnp.where(visible, jnp.exp(scores - lse), 0.0).astype(jnp.bfloat16)
        prob_list.append(probs)
        lse_list.append(lse)
        mixed_list.append(
            jnp.dot(probs, values_all[:, lower : lower + HEAD], preferred_element_type=jnp.float32)
        )
    mixed = jnp.concatenate(mixed_list, axis=1).astype(jnp.bfloat16)
    updated = (
        states_single_float + jnp.dot(mixed, out_weight, preferred_element_type=jnp.float32)
    ).astype(jnp.bfloat16)
    partial_out = rows_product(mixed, grads_in)
    d_mixed = cols_product(grads_in, out_weight).astype(jnp.bfloat16)
    score_grads = []
    delta_list = []
    query_grads = []
    for head in range(HEADS):
        lower = head * HEAD
        mixed_head = d_mixed[:, lower : lower + HEAD]
        delta = jnp.sum(
            mixed_head.astype(jnp.float32) * mixed[:, lower : lower + HEAD].astype(jnp.float32),
            axis=1,
            keepdims=True,
        )
        d_probs = cols_product(mixed_head, values_all[:, lower : lower + HEAD])
        d_scores = (prob_list[head].astype(jnp.float32) * (d_probs - delta)).astype(jnp.bfloat16)
        score_grads.append(d_scores)
        delta_list.append(delta)
        query_grads.append(
            jnp.dot(d_scores, keys_all[:, lower : lower + HEAD], preferred_element_type=jnp.float32)
            * scale
        )
    d_queries = jnp.concatenate(query_grads, axis=1).astype(jnp.bfloat16)
    key_pieces = []
    value_pieces = []
    for head in range(HEADS):
        lower = head * HEAD
        score_part = score_grads[head]
        prob_part = prob_list[head]
        key_pieces.append(rows_product(score_part, queries[:, lower : lower + HEAD]) * scale)
        value_pieces.append(rows_product(prob_part, d_mixed[:, lower : lower + HEAD]))
    key_value_grads = lax.psum_scatter(
        jnp.concatenate(key_pieces + value_pieces, axis=1).astype(jnp.bfloat16),
        "node",
        scatter_dimension=0,
        tiled=True,
    ).astype(jnp.float32)
    d_keys = key_value_grads[:, :width].astype(jnp.bfloat16)
    d_values = key_value_grads[:, width:].astype(jnp.bfloat16)
    normalized_gradient = (
        cols_product(d_queries, query_weight)
        + cols_product(d_keys, key_weight)
        + cols_product(d_values, value_weight)
    )
    node_state_gradient = (
        grads_in.astype(jnp.float32)
        + inverse_norm_scale
        * (
            normalized_gradient
            - centered_states
            * jnp.mean(normalized_gradient * centered_states, axis=1, keepdims=True)
        )
    ).astype(jnp.bfloat16)
    partial_query = rows_product(normalized_states, d_queries)
    partial_key = rows_product(normalized_states, d_keys)
    partial_value = rows_product(normalized_states, d_values)
    total_query, total_key, total_value, total_out = lax.psum(
        (partial_query, partial_key, partial_value, partial_out), ("node", "rep")
    )
    return (
        updated[None],
        node_state_gradient[None],
        total_query,
        total_key,
        total_value,
        total_out,
    )

LANES = 128
SLOTS = 16
LEVEL_PARTS = 3
VMEM_LIMIT = 48 * 1024 * 1024


def transposed_product(left, right):
    return lax.dot_general(left, right, CONTRACT_ROWS, preferred_element_type=jnp.float32)


def pair_product(left, right):
    return lax.dot_general(left, right, CONTRACT_COLS, preferred_element_type=jnp.float32)


def plain_product(left, right):
    return jnp.dot(left, right, preferred_element_type=jnp.float32)


def head_lanes(rows, half):
    lanes = lax.broadcasted_iota(jnp.int32, (rows, LANES), 1)
    return (lanes >= HEAD) if half else (lanes < HEAD)


def keep_lanes(array, mask):
    return jnp.where(mask, array, jnp.zeros_like(array))


def normalize(states):
    wide = states.astype(jnp.float32)
    inverse = lax.rsqrt(jnp.mean(wide * wide, axis=1, keepdims=True) + EPS)
    return wide, inverse, wide * inverse


def score_tables(starts, bias, hidden, total):
    levels = starts.shape[0] - 1
    columns = lax.broadcasted_iota(jnp.int32, (SLOTS, total), 1)
    slots = lax.broadcasted_iota(jnp.int32, (SLOTS, total), 0)
    level = jnp.zeros((SLOTS, total), jnp.int32)
    for entry in range(1, levels):
        level += (columns >= starts[entry]).astype(jnp.int32)
    features = jnp.concatenate(
        [
            (level == slots).astype(jnp.float32),
            ((columns >> 6) == slots).astype(jnp.float32),
        ],
        axis=0,
    ).astype(jnp.bfloat16)
    own = lax.broadcasted_iota(jnp.int32, (SLOTS, LANES), 0)
    lanes = lax.broadcasted_iota(jnp.int32, (SLOTS, LANES), 1)
    part = lanes >> 4
    distance = own - (lanes & (SLOTS - 1))
    tables = []
    for head in range(HEADS):
        table = jnp.full((SLOTS, LANES), NEG, jnp.float32)
        for step in range(1, min(levels, DIST)):
            table = jnp.where(distance == step, bias[head, step], table)
        high = table.astype(jnp.bfloat16).astype(jnp.float32)
        middle = (table - high).astype(jnp.bfloat16).astype(jnp.float32)
        low = table - high - middle
        split = jnp.where(part == 0, high, jnp.where(part == 1, middle, low))
        tables.append(jnp.where(part < LEVEL_PARTS, split, 0.0))
    table = jnp.concatenate(tables, axis=1).astype(jnp.bfloat16)
    table = jnp.concatenate([table, hidden], axis=0)
    picks_row = lax.broadcasted_iota(jnp.int32, (2 * SLOTS, LANES), 0)
    picks_lane = lax.broadcasted_iota(jnp.int32, (2 * SLOTS, LANES), 1)
    wanted = jnp.where(
        picks_lane < LEVEL_PARTS * SLOTS,
        picks_lane & (SLOTS - 1),
        picks_lane - (LEVEL_PARTS - 1) * SLOTS,
    )
    picks = wanted == picks_row
    rows = transposed_product(features, table).astype(jnp.bfloat16)
    cols = transposed_product(features, picks.astype(jnp.float32).astype(jnp.bfloat16))
    return rows, cols.astype(jnp.bfloat16)


def forward_kernel(
    place, starts, bias, own, near, far, last, hidden, query_w, key_w, value_w, out_w,
    normed, queries, keys, values, probs, mixed, updated,
    row_table, key_table,
):
    rows = own.shape[0]
    total = normed.shape[0]
    scale = HEAD ** (-0.5)
    for index, chunk in enumerate((own, near, far, last)):
        at = pl.ds(pl.multiple_of((place[0] ^ index) * rows, rows), rows)
        unit = normalize(chunk[...])[2].astype(jnp.bfloat16)
        normed[at, :] = unit
        queries[at, :] = plain_product(unit, query_w[...]).astype(jnp.bfloat16)
        keys[at, :] = plain_product(unit, key_w[...]).astype(jnp.bfloat16)
        values[at, :] = plain_product(unit, value_w[...]).astype(jnp.bfloat16)
    coefficients, features = score_tables(starts, bias, hidden[...], total)
    row_table[...] = coefficients
    for pair in range(HEADS // 2):
        lanes = slice(pair * LANES, (pair + 1) * LANES)
        key_table[pair, :, :LANES] = keys[:, lanes]
        key_table[pair, :, LANES:] = features
    for tile in range(total // LANES):
        low, high = tile * LANES, (tile + 1) * LANES
        same = lax.broadcasted_iota(jnp.int32, (LANES, high), 1) == (
            lax.broadcasted_iota(jnp.int32, (LANES, high), 0) + low
        )
        for pair in range(HEADS // 2):
            lanes = slice(pair * LANES, (pair + 1) * LANES)
            query = queries[low:high, lanes] * jnp.asarray(scale, jnp.bfloat16)
            product = query.astype(jnp.float32) * keys[low:high, lanes].astype(jnp.float32)
            parts = []
            for half in range(2):
                head = 2 * pair + half
                mask = head_lanes(LANES, half)
                left = jnp.concatenate(
                    [
                        keep_lanes(query, mask),
                        row_table[low:high, head * LANES : (head + 1) * LANES],
                    ],
                    axis=1,
                )
                scores = pair_product(left, key_table[pair, :high, :])
                self_score = jnp.sum(keep_lanes(product, mask), axis=1, keepdims=True)
                scores = jnp.where(same, self_score + bias[head, 0], scores)
                peak = jnp.max(scores, axis=1, keepdims=True)
                weight = jnp.exp(scores - peak)
                mass = jnp.sum(weight, axis=1, keepdims=True)
                prob = (weight * (1.0 / mass)).astype(jnp.bfloat16)
                probs[head, low:high, :high] = prob
                parts.append(plain_product(prob, values[:high, lanes]))
            mixed[low:high, lanes] = jnp.where(
                head_lanes(LANES, 0), parts[0], parts[1]
            ).astype(jnp.bfloat16)
    here = pl.ds(pl.multiple_of(place[0] * rows, rows), rows)
    updated[...] = (
        own[...].astype(jnp.float32) + plain_product(mixed[here, :], out_w[...])
    ).astype(jnp.bfloat16)


def store_halves(place, value, keep, send, full):
    half = keep.shape[0]
    full[...] = value
    keep[...] = full[pl.ds(pl.multiple_of(place[1] * half, half), half), :]
    send[...] = full[pl.ds(pl.multiple_of((1 - place[1]) * half, half), half), :].astype(
        jnp.bfloat16
    )


def output_kernel(place, own, near, far, last, mixed, out_w, d_mixed, keep, send, gathered, full):
    rows = own.shape[0]
    for index, chunk in enumerate((own, near, far, last)):
        at = pl.ds(pl.multiple_of((place[0] ^ index) * rows, rows), rows)
        gathered[at, :] = chunk[...]
    d_mixed[...] = pair_product(gathered[...], out_w[...]).astype(jnp.bfloat16)
    store_halves(place, transposed_product(mixed[...], gathered[...]), keep, send, full)


def backward_kernel(
    place, normed, queries, keys, values, probs, mixed, d_mixed,
    d_all, query_keep, query_send, key_keep, key_send, value_keep, value_send,
    d_queries, d_keys, d_values, key_sum, value_sum, full,
):
    total = normed.shape[0]
    rows = d_all.shape[0]
    width = queries.shape[1]
    scale = HEAD ** (-0.5)
    for pair in range(HEADS // 2):
        lanes = slice(pair * LANES, (pair + 1) * LANES)
        for tile in reversed(range(total // LANES)):
            low, high = tile * LANES, (tile + 1) * LANES
            query = queries[low:high, lanes]
            mix_grad = d_mixed[low:high, lanes]
            product = mix_grad.astype(jnp.float32) * mixed[low:high, lanes].astype(jnp.float32)
            score_grads, prob_list, query_list, mix_list, query_parts = [], [], [], [], []
            for half in range(2):
                head = 2 * pair + half
                mask = head_lanes(LANES, half)
                delta = jnp.sum(keep_lanes(product, mask), axis=1, keepdims=True)
                mix_head = keep_lanes(mix_grad, mask)
                prob = probs[head, low:high, :high]
                d_probs = pair_product(mix_head, values[:high, lanes])
                score_grad = (prob.astype(jnp.float32) * (d_probs - delta)).astype(jnp.bfloat16)
                query_parts.append(plain_product(score_grad, keys[:high, lanes]))
                score_grads.append(score_grad)
                prob_list.append(prob)
                query_list.append(keep_lanes(query, mask))
                mix_list.append(mix_head)
            d_queries[low:high, lanes] = (
                jnp.where(head_lanes(LANES, 0), query_parts[0], query_parts[1]) * scale
            ).astype(jnp.bfloat16)
            key_term = transposed_product(
                jnp.concatenate(score_grads, axis=0), jnp.concatenate(query_list, axis=0)
            )
            value_term = transposed_product(
                jnp.concatenate(prob_list, axis=0), jnp.concatenate(mix_list, axis=0)
            )
            if high == total:
                key_sum[...] = key_term
                value_sum[...] = value_term
            else:
                key_sum[:high, :] += key_term
                value_sum[:high, :] += value_term
        d_keys[:, lanes] = (key_sum[...] * scale).astype(jnp.bfloat16)
        d_values[:, lanes] = value_sum[...].astype(jnp.bfloat16)
    here = pl.ds(pl.multiple_of(place[0] * rows, rows), rows)
    for index, (grad, keep, send) in enumerate(
        (
            (d_queries, query_keep, query_send),
            (d_keys, key_keep, key_send),
            (d_values, value_keep, value_send),
        )
    ):
        d_all[:, index * width : (index + 1) * width] = grad[here, :]
        store_halves(place, transposed_product(normed[...], grad[...]), keep, send, full)


def input_kernel(own, grads_in, d_all, query_w, key_w, value_w, gradient):
    width = query_w.shape[1]
    unit = normalize(own[...])
    inner = (
        pair_product(d_all[:, :width], query_w[...])
        + pair_product(d_all[:, width : 2 * width], key_w[...])
        + pair_product(d_all[:, 2 * width :], value_w[...])
    )
    gradient[...] = (
        grads_in[...].astype(jnp.float32)
        + unit[1] * (inner - unit[2] * jnp.mean(inner * unit[2], axis=1, keepdims=True))
    ).astype(jnp.bfloat16)


def add_kernel(keep, other, total):
    total[...] = (keep[...] + other[...].astype(jnp.float32)).astype(jnp.bfloat16)


def join_kernel(place, mine, other, total):
    half = mine.shape[0]
    total[pl.ds(pl.multiple_of(place[1] * half, half), half), :] = mine[...].astype(jnp.float32)
    total[pl.ds(pl.multiple_of((1 - place[1]) * half, half), half), :] = other[...].astype(
        jnp.float32
    )


def run(kernel, outs, smem, arrays, scratch=(), flops=0):
    out_shape = tuple(jax.ShapeDtypeStruct(shape, dtype) for shape, dtype in outs)
    moved = sum(array.size * array.dtype.itemsize for array in arrays)
    return pl.pallas_call(
        kernel,
        out_shape=out_shape,
        in_specs=[pl.BlockSpec(memory_space=pltpu.SMEM)] * len(smem)
        + [pl.BlockSpec(memory_space=pltpu.VMEM)] * len(arrays),
        out_specs=tuple([pl.BlockSpec(memory_space=pltpu.VMEM)] * len(outs)),
        scratch_shapes=list(scratch),
        compiler_params=pltpu.CompilerParams(vmem_limit_bytes=VMEM_LIMIT),
        cost_estimate=pl.CostEstimate(flops=flops, bytes_accessed=moved, transcendentals=0),
    )(*smem, *arrays)


def swap(array, axis, flip):
    return lax.ppermute(array, axis, [(i, i ^ flip) for i in range(lax.axis_size(axis))])


def sum_over_rep(keep, send, place):
    half, columns = keep.shape
    other = swap(send, "rep", 1)
    local = (keep + other.astype(jnp.float32)).astype(jnp.bfloat16)
    across = swap(local, "rep", 2)
    mine = (local.astype(jnp.float32) + across.astype(jnp.float32)).astype(jnp.bfloat16)
    other = swap(mine, "rep", 1)
    return run(join_kernel, [((2 * half, columns), jnp.float32)], [place], [mine, other])[0]


def on_device_whole(
    node_states,
    cotangent,
    reach_blocks,
    reach_count,
    level_start,
    query_weight,
    key_weight,
    value_weight,
    out_weight,
    bias_table,
):
    states = node_states[0]
    grads_in = cotangent[0]
    blocks = reach_blocks[0]
    counts = reach_count[0]
    starts = level_start[0]
    rows, model = states.shape
    width = query_weight.shape[1]
    total = rows * lax.axis_size("node")
    place = jnp.stack([lax.axis_index("node"), lax.axis_index("rep") & 1]).astype(jnp.int32)

    far = swap(states, "node", 2)
    near = swap(states, "node", 1)
    last = swap(far, "node", 1)
    grads_far = swap(grads_in, "node", 2)
    grads_near = swap(grads_in, "node", 1)
    grads_last = swap(grads_far, "node", 1)

    local_blocks = blocks.shape[0]
    slots = jnp.arange(blocks.shape[1], dtype=jnp.int32)
    live = slots[None, :] < counts[:, None]
    kinds = jnp.arange(SLOTS, dtype=jnp.int32)
    listed = jnp.any((blocks[:, :, None] == kinds[None, None, :]) & live[:, :, None], axis=1)
    hidden = jnp.where(listed, 0.0, NEG).astype(jnp.bfloat16)
    hidden = jnp.pad(
        hidden, ((0, 0), (LEVEL_PARTS * SLOTS, LANES - (LEVEL_PARTS + 1) * SLOTS))
    )
    hidden = lax.dynamic_update_slice(
        jnp.zeros((SLOTS, HEADS * LANES), jnp.bfloat16),
        jnp.tile(hidden, (1, HEADS)),
        (place[0] * local_blocks, jnp.int32(0)),
    )
    hidden = hidden + swap(hidden, "node", 1)
    hidden = hidden + swap(hidden, "node", 2)

    half = jnp.bfloat16
    wide = jnp.float32
    normed, queries, keys, values, probs, mixed, updated = run(
        forward_kernel,
        [
            ((total, model), half),
            ((total, width), half),
            ((total, width), half),
            ((total, width), half),
            ((HEADS, total, total), half),
            ((total, width), half),
            ((rows, model), half),
        ],
        [place, starts, bias_table],
        [
            states, near, far, last, hidden,
            query_weight, key_weight, value_weight, out_weight,
        ],
        [
            pltpu.VMEM((total, HEADS * LANES), half),
            pltpu.VMEM((HEADS // 2, total, 2 * LANES), half),
        ],
        flops=2 * total * model * width * 6,
    )
    d_mixed, out_keep, out_send = run(
        output_kernel,
        [
            ((total, width), half),
            ((width // 2, model), wide),
            ((width // 2, model), half),
        ],
        [place],
        [grads_in, grads_near, grads_far, grads_last, mixed, out_weight],
        [pltpu.VMEM((total, model), half), pltpu.VMEM((width, model), wide)],
        flops=2 * total * model * width * 2,
    )
    halves = [((model // 2, width), wide), ((model // 2, width), half)]
    d_all, query_keep, query_send, key_keep, key_send, value_keep, value_send = run(
        backward_kernel,
        [((rows, 3 * width), half)] + halves * 3,
        [place],
        [normed, queries, keys, values, probs, mixed, d_mixed],
        [pltpu.VMEM((total, width), half)] * 3
        + [pltpu.VMEM((total, LANES), wide)] * 2
        + [pltpu.VMEM((model, width), wide)],
        flops=2 * total * model * width * 8,
    )
    total_out = sum_over_rep(out_keep, out_send, place)
    total_query = sum_over_rep(query_keep, query_send, place)
    total_key = sum_over_rep(key_keep, key_send, place)
    total_value = sum_over_rep(value_keep, value_send, place)
    node_state_gradient = run(
        input_kernel,
        [((rows, model), half)],
        [],
        [states, grads_in, d_all, query_weight, key_weight, value_weight],
        flops=2 * rows * model * width * 3,
    )[0]
    return (
        updated[None],
        node_state_gradient[None],
        total_query,
        total_key,
        total_value,
        total_out,
    )


def on_device(node_states, cotangent, reach_blocks, reach_count, level_start, *rest):
    nodes = lax.axis_size("node")
    total = node_states.shape[1] * nodes
    small = (
        nodes == 4
        and lax.axis_size("rep") == 4
        and node_states.shape[1] == LANES
        and total // BLOCK <= SLOTS
        and level_start.shape[1] - 1 <= SLOTS
    )
    path = on_device_whole if small else on_device_general
    return path(node_states, cotangent, reach_blocks, reach_count, level_start, *rest)


def solution(mesh):
    in_specs = (
        P(("groups", "rep"), "node", None),
        P(("groups", "rep"), "node", None),
        P(("groups", "rep"), "node", None),
        P(("groups", "rep"), "node"),
        P(("groups", "rep"), None),
        P(),
        P(),
        P(),
        P(),
        P(),
    )
    out_specs = (
        P(("groups", "rep"), "node", None),
        P(("groups", "rep"), "node", None),
        P("groups", None),
        P("groups", None),
        P("groups", None),
        P("groups", None),
    )
    return jax.shard_map(
        on_device, mesh=mesh, in_specs=in_specs, out_specs=out_specs, check_vma=False
    )
```

```python
import functools

import jax
import jax.numpy as jnp
from jax import lax
from jax.experimental import pallas as pl
from jax.experimental.pallas import tpu as pltpu
from jax.sharding import PartitionSpec as P

HEADS = 4
HEAD = 64
BLOCK = 64
DIST = 32


EPS = 1e-05
NEG = -1e30
HIGH = lax.Precision.HIGHEST
CONTRACT_ROWS = (((0,), (0,)), ((), ()))
CONTRACT_COLS = (((1,), (1,)), ((), ()))


def rows_product(left, right):
    return lax.dot_general(left, right, CONTRACT_ROWS, preferred_element_type=jnp.float32)


def cols_product(left, right):
    return lax.dot_general(left, right, CONTRACT_COLS, preferred_element_type=jnp.float32)


def expand(listed):
    return jnp.repeat(jnp.repeat(listed, BLOCK, axis=0), BLOCK, axis=1)


def level_tables(starts, total, bias_table):
    level_count = starts.shape[0] - 1
    places = jnp.arange(total, dtype=jnp.int32)
    inner = starts[1:level_count]
    levels = jnp.sum((places[:, None] >= inner[None, :]).astype(jnp.int32), axis=1)
    marks = jnp.arange(level_count, dtype=jnp.int32)
    onehot = (levels[:, None] == marks[None, :]).astype(jnp.float32)
    spread = jnp.clip(marks[:, None] - marks[None, :], 0, DIST - 1)
    picks = (spread[:, :, None] == jnp.arange(DIST, dtype=jnp.int32)[None, None, :]).astype(
        jnp.float32
    )
    level_bias = jnp.einsum("hd,abd->hab", bias_table, picks, precision=HIGH)
    return (levels, onehot, level_bias)


def bias_block(row_onehot, head_bias, col_onehot):
    row_part = jnp.dot(row_onehot, head_bias, precision=HIGH)
    return lax.dot_general(row_part, col_onehot, CONTRACT_COLS, precision=HIGH)


def on_device_general(
    node_states,
    cotangent,
    reach_blocks,
    reach_count,
    level_start,
    query_weight,
    key_weight,
    value_weight,
    out_weight,
    bias_table,
):
    states = node_states[0]
    grads_in = cotangent[0]
    blocks = reach_blocks[0]
    counts = reach_count[0]
    starts = level_start[0]
    rows_dev = states.shape[0]
    width = query_weight.shape[1]
    total = rows_dev * lax.axis_size("node")
    offset = lax.axis_index("node") * rows_dev
    scale = HEAD ** (-0.5)
    key_blocks = total // BLOCK
    states_single_float = states.astype(jnp.float32)
    inverse_norm_scale = lax.rsqrt(
        jnp.mean(states_single_float * states_single_float, axis=1, keepdims=True) + EPS
    )
    centered_states = states_single_float * inverse_norm_scale
    normalized_states = centered_states.astype(jnp.bfloat16)
    queries = jnp.dot(normalized_states, query_weight, preferred_element_type=jnp.float32).astype(
        jnp.bfloat16
    )
    keys = jnp.dot(normalized_states, key_weight, preferred_element_type=jnp.float32).astype(
        jnp.bfloat16
    )
    values = jnp.dot(normalized_states, value_weight, preferred_element_type=jnp.float32).astype(
        jnp.bfloat16
    )
    keys_all, values_all = (
        lax.all_gather(keys, "node", axis=0, tiled=True),
        lax.all_gather(values, "node", axis=0, tiled=True),
    )
    levels, onehot, level_bias = level_tables(starts, total, bias_table)
    positions = jnp.arange(total, dtype=jnp.int32)
    local = jnp.arange(rows_dev, dtype=jnp.int32)
    row_ids = offset + local
    row_levels = lax.dynamic_slice_in_dim(levels, offset, rows_dev, 0)
    row_onehot = lax.dynamic_slice_in_dim(onehot, offset, rows_dev, 0)
    slots = jnp.arange(blocks.shape[1], dtype=jnp.int32)
    live = slots[None, :] < counts[:, None]
    kinds = jnp.arange(key_blocks, dtype=jnp.int32)
    listed = jnp.any((blocks[:, :, None] == kinds[None, None, :]) & live[:, :, None], axis=1)
    visible = expand(listed) & (
        (levels[None, :] < row_levels[:, None]) | (positions[None, :] == row_ids[:, None])
    )
    prob_list = []
    lse_list = []
    mixed_list = []
    for head in range(HEADS):
        lower = head * HEAD
        scores = (
            cols_product(queries[:, lower : lower + HEAD], keys_all[:, lower : lower + HEAD])
            * scale
        )
        scores = scores + bias_block(row_onehot, level_bias[head], onehot)
        scores = jnp.where(visible, scores, NEG)
        peak = jnp.max(scores, axis=1, keepdims=True)
        mass = jnp.sum(jnp.where(visible, jnp.exp(scores - peak), 0.0), axis=1, keepdims=True)
        lse = peak + jnp.log(mass)
        probs = jnp.where(visible, jnp.exp(scores - lse), 0.0).astype(jnp.bfloat16)
        prob_list.append(probs)
        lse_list.append(lse)
        mixed_list.append(
            jnp.dot(probs, values_all[:, lower : lower + HEAD], preferred_element_type=jnp.float32)
        )
    mixed = jnp.concatenate(mixed_list, axis=1).astype(jnp.bfloat16)
    updated = (
        states_single_float + jnp.dot(mixed, out_weight, preferred_element_type=jnp.float32)
    ).astype(jnp.bfloat16)
    partial_out = rows_product(mixed, grads_in)
    d_mixed = cols_product(grads_in, out_weight).astype(jnp.bfloat16)
    score_grads = []
    delta_list = []
    query_grads = []
    for head in range(HEADS):
        lower = head * HEAD
        mixed_head = d_mixed[:, lower : lower + HEAD]
        delta = jnp.sum(
            mixed_head.astype(jnp.float32) * mixed[:, lower : lower + HEAD].astype(jnp.float32),
            axis=1,
            keepdims=True,
        )
        d_probs = cols_product(mixed_head, values_all[:, lower : lower + HEAD])
        d_scores = (prob_list[head].astype(jnp.float32) * (d_probs - delta)).astype(jnp.bfloat16)
        score_grads.append(d_scores)
        delta_list.append(delta)
        query_grads.append(
            jnp.dot(d_scores, keys_all[:, lower : lower + HEAD], preferred_element_type=jnp.float32)
            * scale
        )
    d_queries = jnp.concatenate(query_grads, axis=1).astype(jnp.bfloat16)
    key_pieces = []
    value_pieces = []
    for head in range(HEADS):
        lower = head * HEAD
        score_part = score_grads[head]
        prob_part = prob_list[head]
        key_pieces.append(rows_product(score_part, queries[:, lower : lower + HEAD]) * scale)
        value_pieces.append(rows_product(prob_part, d_mixed[:, lower : lower + HEAD]))
    key_value_grads = lax.psum_scatter(
        jnp.concatenate(key_pieces + value_pieces, axis=1).astype(jnp.bfloat16),
        "node",
        scatter_dimension=0,
        tiled=True,
    ).astype(jnp.float32)
    d_keys = key_value_grads[:, :width].astype(jnp.bfloat16)
    d_values = key_value_grads[:, width:].astype(jnp.bfloat16)
    normalized_gradient = (
        cols_product(d_queries, query_weight)
        + cols_product(d_keys, key_weight)
        + cols_product(d_values, value_weight)
    )
    node_state_gradient = (
        grads_in.astype(jnp.float32)
        + inverse_norm_scale
        * (
            normalized_gradient
            - centered_states
            * jnp.mean(normalized_gradient * centered_states, axis=1, keepdims=True)
        )
    ).astype(jnp.bfloat16)
    partial_query = rows_product(normalized_states, d_queries)
    partial_key = rows_product(normalized_states, d_keys)
    partial_value = rows_product(normalized_states, d_values)
    total_query, total_key, total_value, total_out = lax.psum(
        (partial_query, partial_key, partial_value, partial_out), ("node", "rep")
    )
    return (
        updated[None],
        node_state_gradient[None],
        total_query,
        total_key,
        total_value,
        total_out,
    )

LANES = 128
SLOTS = 16
LEVEL_PARTS = 3
VMEM_LIMIT = 48 * 1024 * 1024


def transposed_product(left, right):
    return lax.dot_general(left, right, CONTRACT_ROWS, preferred_element_type=jnp.float32)


def pair_product(left, right):
    return lax.dot_general(left, right, CONTRACT_COLS, preferred_element_type=jnp.float32)


def plain_product(left, right):
    return jnp.dot(left, right, preferred_element_type=jnp.float32)


def head_lanes(rows, half):
    lanes = lax.broadcasted_iota(jnp.int32, (rows, LANES), 1)
    return (lanes >= HEAD) if half else (lanes < HEAD)


def keep_lanes(array, mask):
    return jnp.where(mask, array, jnp.zeros_like(array))


def split_heads(array):
    rows = array.shape[0]
    return jnp.concatenate(
        [keep_lanes(array, head_lanes(rows, 0)), keep_lanes(array, head_lanes(rows, 1))], axis=0
    )


def merge_heads(array):
    rows = array.shape[0] // 2
    return jnp.where(head_lanes(rows, 0), array[:rows], array[rows:])


def normalize(states):
    wide = states.astype(jnp.float32)
    inverse = lax.rsqrt(jnp.mean(wide * wide, axis=1, keepdims=True) + EPS)
    return wide, inverse, wide * inverse


def level_tables_whole(scalars, levels, total):
    columns = lax.broadcasted_iota(jnp.int32, (SLOTS, total), 1)
    places = columns.astype(jnp.float32)
    slots = lax.broadcasted_iota(jnp.int32, (SLOTS, total), 0)
    level = jnp.zeros((SLOTS, total), jnp.int32)
    for entry in range(1, levels):
        level += (places >= scalars[HEADS * DIST + entry]).astype(jnp.int32)
    features = jnp.concatenate(
        [
            (level == slots).astype(jnp.float32),
            ((columns >> 6) == slots).astype(jnp.float32),
        ],
        axis=0,
    ).astype(jnp.bfloat16)
    own = lax.broadcasted_iota(jnp.int32, (SLOTS, LANES), 0)
    lanes = lax.broadcasted_iota(jnp.int32, (SLOTS, LANES), 1)
    part = lanes >> 4
    distance = own - (lanes & (SLOTS - 1))
    tables = []
    for head in range(HEADS):
        table = jnp.full((SLOTS, LANES), NEG, jnp.float32)
        for step in range(1, min(levels, DIST)):
            table = jnp.where(distance == step, scalars[head * DIST + step], table)
        high = table.astype(jnp.bfloat16).astype(jnp.float32)
        middle = (table - high).astype(jnp.bfloat16).astype(jnp.float32)
        low = table - high - middle
        split = jnp.where(part == 0, high, jnp.where(part == 1, middle, low))
        tables.append(jnp.where(part < LEVEL_PARTS, split, 0.0))
    table = jnp.concatenate(tables, axis=1).astype(jnp.bfloat16)
    picks_row = lax.broadcasted_iota(jnp.int32, (2 * SLOTS, LANES), 0)
    picks_lane = lax.broadcasted_iota(jnp.int32, (2 * SLOTS, LANES), 1)
    wanted = jnp.where(
        picks_lane < LEVEL_PARTS * SLOTS,
        picks_lane & (SLOTS - 1),
        picks_lane - (LEVEL_PARTS - 1) * SLOTS,
    )
    picks = (wanted == picks_row).astype(jnp.float32).astype(jnp.bfloat16)
    return features, table, transposed_product(features, picks).astype(jnp.bfloat16)


def project(chunk, weights, unit_t, projected):
    unit = normalize(chunk[...])[2]
    unit_t[...] = unit.T.astype(jnp.bfloat16)
    projected[...] = plain_product(unit.astype(jnp.bfloat16), weights[...]).astype(jnp.bfloat16)


def first_kernel(
    levels, scalars, own, in_weights, features, table, column_features, unit_t, projected
):
    rows, level_bias, columns = level_tables_whole(scalars, levels, features.shape[1])
    features[...] = rows
    table[...] = level_bias
    column_features[...] = columns
    project(own, in_weights, unit_t, projected)


def project_kernel(chunk, in_weights, unit_t, projected):
    project(chunk, in_weights, unit_t, projected)


def forward_kernel(
    place, scalars, own_t, own, near_t, near, far_t, far, last_states, in_weights,
    hidden, features, table, column_features,
    normed_t, projected, probs, mixed, mixed_t,
    row_table, key_table, last_t, last,
):
    total, width = mixed.shape
    rows = own.shape[0]
    scale = HEAD ** (-0.5)
    project(last_states, in_weights, last_t, last)
    chunks = ((own_t, own), (near_t, near), (far_t, far), (last_t, last))
    for index, (unit_t, chunk) in enumerate(chunks):
        at = pl.ds(pl.multiple_of((place[0] ^ index) * rows, rows), rows)
        normed_t[:, at] = unit_t[...]
        projected[at, :] = chunk[...]
    row_table[...] = transposed_product(
        features[...], jnp.concatenate([table[...], hidden[...]], axis=0)
    ).astype(jnp.bfloat16)
    for pair in range(HEADS // 2):
        key_table[pair, :, :LANES] = projected[:, width + pair * LANES : width + (pair + 1) * LANES]
        key_table[pair, :, LANES:] = column_features[...]
    same = lax.broadcasted_iota(jnp.int32, (2 * LANES, LANES), 1) == (
        lax.broadcasted_iota(jnp.int32, (2 * LANES, LANES), 0) & (LANES - 1)
    )
    first_half = lax.broadcasted_iota(jnp.int32, (2 * LANES, 1), 0) < LANES
    for pair in range(HEADS // 2):
        lanes = slice(pair * LANES, (pair + 1) * LANES)
        values = slice(2 * width + pair * LANES, 2 * width + (pair + 1) * LANES)
        self_bias = jnp.where(
            first_half, scalars[2 * pair * DIST], scalars[(2 * pair + 1) * DIST]
        )
        for tile in range(total // LANES):
            low, high = tile * LANES, (tile + 1) * LANES
            stacked = slice(2 * low, 2 * high)
            query = split_heads(projected[low:high, lanes] * jnp.asarray(scale, jnp.bfloat16))
            key = key_table[pair, low:high, :LANES].astype(jnp.float32)
            self_score = jnp.sum(
                query.astype(jnp.float32) * jnp.concatenate([key, key], axis=0),
                axis=1,
                keepdims=True,
            )
            rest = jnp.concatenate(
                [
                    row_table[low:high, (2 * pair) * LANES : (2 * pair + 1) * LANES],
                    row_table[low:high, (2 * pair + 1) * LANES : (2 * pair + 2) * LANES],
                ],
                axis=0,
            )
            scores = pair_product(
                jnp.concatenate([query, rest], axis=1), key_table[pair, :high, :]
            )
            corner = jnp.where(same, self_score + self_bias, scores[:, low:])
            peak = jnp.max(corner, axis=1, keepdims=True)
            if low:
                peak = jnp.maximum(peak, jnp.max(scores[:, :low], axis=1, keepdims=True))
            corner = jnp.exp(corner - peak)
            mass = jnp.sum(corner, axis=1, keepdims=True)
            if low:
                weight = jnp.exp(scores[:, :low] - peak)
                mass += jnp.sum(weight, axis=1, keepdims=True)
                inverse = 1.0 / mass
                probs[pair, stacked, :low] = (weight * inverse).astype(jnp.bfloat16)
            else:
                inverse = 1.0 / mass
            probs[pair, stacked, low:high] = (corner * inverse).astype(jnp.bfloat16)
            both = merge_heads(
                plain_product(probs[pair, stacked, :high], projected[:high, values])
            )
            mixed[low:high, lanes] = both.astype(jnp.bfloat16)
            mixed_t[lanes, low:high] = both.T.astype(jnp.bfloat16)


def store_halves(place, value, keep, send, full):
    half = keep.shape[0]
    full[...] = value
    keep[...] = full[pl.ds(pl.multiple_of(place[1] * half, half), half), :]
    send[...] = full[pl.ds(pl.multiple_of((1 - place[1]) * half, half), half), :].astype(
        jnp.bfloat16
    )


def output_kernel(
    place, own, near, far, last, mixed_t, out_w, d_mixed, keep, send, gathered, full
):
    rows = own.shape[0]
    for index, chunk in enumerate((own, near, far, last)):
        at = pl.ds(pl.multiple_of((place[0] ^ index) * rows, rows), rows)
        gathered[at, :] = chunk[...]
    store_halves(place, plain_product(mixed_t[...], gathered[...]), keep, send, full)
    d_mixed[...] = pair_product(gathered[...], out_w[...]).astype(jnp.bfloat16)


def backward_kernel(
    pair, place, normed_t, projected, probs, mixed, d_mixed,
    d_own, keep, send,
    grads, key_sum, value_sum, full,
):
    total, width = mixed.shape
    rows = d_own.shape[0]
    scale = HEAD ** (-0.5)
    lanes, key_lanes, value_lanes = (
        slice(i * width + pair * LANES, i * width + (pair + 1) * LANES) for i in range(3)
    )
    for tile in reversed(range(total // LANES)):
        low, high = tile * LANES, (tile + 1) * LANES
        query = split_heads(projected[low:high, lanes])
        mix_grad = split_heads(d_mixed[low:high, lanes])
        mix = mixed[low:high, lanes].astype(jnp.float32)
        delta = jnp.sum(
            mix_grad.astype(jnp.float32) * jnp.concatenate([mix, mix], axis=0),
            axis=1,
            keepdims=True,
        )
        prob = probs[pair, 2 * low : 2 * high, :high]
        d_probs = pair_product(mix_grad, projected[:high, value_lanes])
        score_grad = (prob.astype(jnp.float32) * (d_probs - delta)).astype(jnp.bfloat16)
        grads[low:high, :LANES] = (
            merge_heads(plain_product(score_grad, projected[:high, key_lanes])) * scale
        ).astype(jnp.bfloat16)
        key_term = transposed_product(score_grad, query)
        value_term = transposed_product(prob, mix_grad)
        if high == total:
            key_sum[...] = key_term
            value_sum[...] = value_term
        else:
            key_sum[:high, :] += key_term
            value_sum[:high, :] += value_term
    grads[:, LANES : 2 * LANES] = (key_sum[...] * scale).astype(jnp.bfloat16)
    grads[:, 2 * LANES :] = value_sum[...].astype(jnp.bfloat16)
    store_halves(place, plain_product(normed_t[...], grads[...]), keep, send, full)
    d_own[...] = grads[pl.ds(pl.multiple_of(place[0] * rows, rows), rows), :]


def rows_kernel(place, own, grads_in, mixed, in_weights, out_w, *rest):
    *d_own, updated, gradient = rest
    rows = own.shape[0]
    width = mixed.shape[1]
    states, inverse, unit = normalize(own[...])
    here = pl.ds(pl.multiple_of(place[0] * rows, rows), rows)
    updated[...] = (states + plain_product(mixed[here, :], out_w[...])).astype(jnp.bfloat16)
    inner = jnp.zeros(own.shape, jnp.float32)
    for pair, piece in enumerate(d_own):
        for i in range(3):
            lanes = slice(i * width + pair * LANES, i * width + (pair + 1) * LANES)
            inner += pair_product(piece[:, i * LANES : (i + 1) * LANES], in_weights[:, lanes])
    gradient[...] = (
        grads_in[...].astype(jnp.float32)
        + inverse * (inner - unit * jnp.mean(inner * unit, axis=1, keepdims=True))
    ).astype(jnp.bfloat16)


def join_kernel(place, *refs):
    mine, other = refs[0:3], refs[3:6]
    total_query, total_key, total_value, total_out = refs[6:]
    for pieces, slot in ((mine, place[1]), (other, 1 - place[1])):
        half = pieces[0].shape[0]
        total_out[pl.ds(pl.multiple_of(slot * half, half), half), :] = pieces[0][...].astype(
            jnp.float32
        )
        half = pieces[1].shape[0]
        at = pl.ds(pl.multiple_of(slot * half, half), half)
        for pair, piece in enumerate(pieces[1:]):
            for i, total in enumerate((total_query, total_key, total_value)):
                total[at, pair * LANES : (pair + 1) * LANES] = piece[
                    :, i * LANES : (i + 1) * LANES
                ].astype(jnp.float32)


def run(kernel, outs, smem, arrays, scratch=(), cost=0):
    out_shape = tuple(jax.ShapeDtypeStruct(shape, dtype) for shape, dtype in outs)
    return pl.pallas_call(
        kernel,
        out_shape=out_shape,
        in_specs=[pl.BlockSpec(memory_space=pltpu.SMEM)] * len(smem)
        + [pl.BlockSpec(memory_space=pltpu.VMEM)] * len(arrays),
        out_specs=tuple([pl.BlockSpec(memory_space=pltpu.VMEM)] * len(outs)),
        scratch_shapes=list(scratch),
        compiler_params=pltpu.CompilerParams(vmem_limit_bytes=VMEM_LIMIT),
        cost_estimate=pl.CostEstimate(
            flops=cost * 1000000000, bytes_accessed=0, transcendentals=0
        ),
    )(*smem, *arrays)


def swap(array, axis, flip):
    return lax.ppermute(array, axis, [(i, i ^ flip) for i in range(lax.axis_size(axis))])


def sum_over_chips(keep, send):
    local = (keep + swap(send, "rep", 1).astype(jnp.float32)).astype(jnp.bfloat16)
    across = swap(local, "rep", 2)
    return local, across


def on_device_whole(
    node_states,
    cotangent,
    reach_blocks,
    reach_count,
    level_start,
    query_weight,
    key_weight,
    value_weight,
    out_weight,
    bias_table,
):
    states = node_states[0]
    grads_in = cotangent[0]
    blocks = reach_blocks[0]
    counts = reach_count[0]
    starts = level_start[0]
    rows, model = states.shape
    width = query_weight.shape[1]
    total = rows * lax.axis_size("node")
    place = jnp.stack([lax.axis_index("node"), lax.axis_index("rep") & 1]).astype(jnp.int32)
    half = jnp.bfloat16
    wide = jnp.float32

    far = swap(states, "node", 2)
    near = swap(states, "node", 1)

    local_blocks = blocks.shape[0]
    slots = jnp.arange(blocks.shape[1], dtype=jnp.int32)
    live = slots[None, :] < counts[:, None]
    kinds = jnp.arange(SLOTS, dtype=jnp.int32)
    listed = jnp.any((blocks[:, :, None] == kinds[None, None, :]) & live[:, :, None], axis=1)
    hidden = jnp.where(listed, 0.0, NEG).astype(jnp.bfloat16)
    hidden = jnp.pad(
        hidden, ((0, 0), (LEVEL_PARTS * SLOTS, LANES - (LEVEL_PARTS + 1) * SLOTS))
    )
    hidden = lax.dynamic_update_slice(
        jnp.zeros((SLOTS, HEADS * LANES), jnp.bfloat16),
        jnp.tile(hidden, (1, HEADS)),
        (place[0] * local_blocks, jnp.int32(0)),
    )
    hidden = hidden + swap(hidden, "node", 1)
    hidden = hidden + swap(hidden, "node", 2)

    last = swap(far, "node", 1)
    grads_far = swap(grads_in, "node", 2)
    grads_near = swap(grads_in, "node", 1)
    scalars = jnp.concatenate([bias_table.reshape(-1), starts.astype(wide)])
    in_weights = jnp.concatenate([query_weight, key_weight, value_weight], axis=1)
    loaded, far = lax.optimization_barrier((states, far))
    features, table, columns, own_t, own_p = run(
        functools.partial(first_kernel, starts.shape[0] - 1),
        [
            ((2 * SLOTS, total), half),
            ((SLOTS, HEADS * LANES), half),
            ((total, LANES), half),
            ((model, rows), half),
            ((rows, 3 * width), half),
        ],
        [scalars],
        [loaded, in_weights],
    )
    chunk_outs = [((model, rows), half), ((rows, 3 * width), half)]
    near_t, near_p = run(project_kernel, chunk_outs, [], [near, in_weights])
    far_t, far_p = run(project_kernel, chunk_outs, [], [far, in_weights])
    grads_far, own_p, near_p, far_p = lax.optimization_barrier((grads_far, own_p, near_p, far_p))
    grads_last = swap(grads_far, "node", 1)
    normed_t, projected, probs, mixed, mixed_t = run(
        forward_kernel,
        [
            ((model, total), half),
            ((total, 3 * width), half),
            ((HEADS // 2, 2 * total, total), half),
            ((total, width), half),
            ((width, total), half),
        ],
        [place, scalars],
        [
            own_t, own_p, near_t, near_p, far_t, far_p, last, in_weights,
            hidden, features, table, columns,
        ],
        [
            pltpu.VMEM((total, HEADS * LANES), half),
            pltpu.VMEM((HEADS // 2, total, 2 * LANES), half),
            pltpu.VMEM((model, rows), half),
            pltpu.VMEM((rows, 3 * width), half),
        ],
    )
    d_mixed, out_keep, out_send = run(
        output_kernel,
        [
            ((total, width), half),
            ((width // 2, model), wide),
            ((width // 2, model), half),
        ],
        [place],
        [grads_in, grads_near, grads_far, grads_last, mixed_t, out_weight],
        [pltpu.VMEM((total, model), half), pltpu.VMEM((width, model), wide)],
    )
    local, across = sum_over_chips(out_keep, out_send)
    halves = [(local, across)]
    d_own = []
    for pair in range(HEADS // 2):
        if pair:
            d_mixed, local = lax.optimization_barrier((d_mixed, local))
            halves[0] = (local, halves[0][1])
        own_grads, keep, send = run(
            functools.partial(backward_kernel, pair),
            [
                ((rows, 3 * LANES), half),
                ((model // 2, 3 * LANES), wide),
                ((model // 2, 3 * LANES), half),
            ],
            [place],
            [normed_t, projected, probs, mixed, d_mixed],
            [
                pltpu.VMEM((total, 3 * LANES), half),
                pltpu.VMEM((total, LANES), wide),
                pltpu.VMEM((total, LANES), wide),
                pltpu.VMEM((model, 3 * LANES), wide),
            ],
        )
        d_own.append(own_grads)
        halves.append(sum_over_chips(keep, send))
    d_own[-1], _ = lax.optimization_barrier((d_own[-1], halves[-1][0]))
    updated, node_state_gradient = run(
        rows_kernel,
        [((rows, model), half)] * 2,
        [place],
        [loaded, grads_in, mixed, in_weights, out_weight, *d_own],
    )
    first, node_state_gradient = lax.optimization_barrier((halves[0][1], node_state_gradient))
    halves[0] = (halves[0][0], first)
    mine = [
        (near_sum.astype(wide) + far_sum.astype(wide)).astype(half) for near_sum, far_sum in halves
    ]
    other = [swap(piece, "rep", 1) for piece in mine]
    total_query, total_key, total_value, total_out = run(
        join_kernel,
        [((model, width), wide)] * 3 + [((width, model), wide)],
        [place],
        [*mine, *other],
    )
    return (
        updated[None],
        node_state_gradient[None],
        total_query,
        total_key,
        total_value,
        total_out,
    )


def on_device(node_states, cotangent, reach_blocks, reach_count, level_start, *rest):
    nodes = lax.axis_size("node")
    total = node_states.shape[1] * nodes
    small = (
        nodes == 4
        and lax.axis_size("rep") == 4
        and node_states.shape[1] == LANES
        and total // BLOCK <= SLOTS
        and level_start.shape[1] - 1 <= SLOTS
    )
    path = on_device_whole if small else on_device_general
    return path(node_states, cotangent, reach_blocks, reach_count, level_start, *rest)


def solution(mesh):
    in_specs = (
        P(("groups", "rep"), "node", None),
        P(("groups", "rep"), "node", None),
        P(("groups", "rep"), "node", None),
        P(("groups", "rep"), "node"),
        P(("groups", "rep"), None),
        P(),
        P(),
        P(),
        P(),
        P(),
    )
    out_specs = (
        P(("groups", "rep"), "node", None),
        P(("groups", "rep"), "node", None),
        P("groups", None),
        P("groups", None),
        P("groups", None),
        P("groups", None),
    )
    return jax.shard_map(
        on_device, mesh=mesh, in_specs=in_specs, out_specs=out_specs, check_vma=False
    )
```

```python
import functools

import jax
import jax.numpy as jnp
from jax import lax
from jax.experimental import pallas as pl
from jax.experimental.pallas import tpu as pltpu
from jax.sharding import PartitionSpec as P

HEADS = 4
HEAD = 64
BLOCK = 64
DIST = 32


EPS = 1e-05
NEG = -1e30
HIGH = lax.Precision.HIGHEST
CONTRACT_ROWS = (((0,), (0,)), ((), ()))
CONTRACT_COLS = (((1,), (1,)), ((), ()))


def rows_product(left, right):
    return lax.dot_general(left, right, CONTRACT_ROWS, preferred_element_type=jnp.float32)


def cols_product(left, right):
    return lax.dot_general(left, right, CONTRACT_COLS, preferred_element_type=jnp.float32)


def expand(listed):
    return jnp.repeat(jnp.repeat(listed, BLOCK, axis=0), BLOCK, axis=1)


def level_tables(starts, total, bias_table):
    level_count = starts.shape[0] - 1
    places = jnp.arange(total, dtype=jnp.int32)
    inner = starts[1:level_count]
    levels = jnp.sum((places[:, None] >= inner[None, :]).astype(jnp.int32), axis=1)
    marks = jnp.arange(level_count, dtype=jnp.int32)
    onehot = (levels[:, None] == marks[None, :]).astype(jnp.float32)
    spread = jnp.clip(marks[:, None] - marks[None, :], 0, DIST - 1)
    picks = (spread[:, :, None] == jnp.arange(DIST, dtype=jnp.int32)[None, None, :]).astype(
        jnp.float32
    )
    level_bias = jnp.einsum("hd,abd->hab", bias_table, picks, precision=HIGH)
    return (levels, onehot, level_bias)


def bias_block(row_onehot, head_bias, col_onehot):
    row_part = jnp.dot(row_onehot, head_bias, precision=HIGH)
    return lax.dot_general(row_part, col_onehot, CONTRACT_COLS, precision=HIGH)


def on_device_general(
    node_states,
    cotangent,
    reach_blocks,
    reach_count,
    level_start,
    query_weight,
    key_weight,
    value_weight,
    out_weight,
    bias_table,
):
    states = node_states[0]
    grads_in = cotangent[0]
    blocks = reach_blocks[0]
    counts = reach_count[0]
    starts = level_start[0]
    rows_dev = states.shape[0]
    width = query_weight.shape[1]
    total = rows_dev * lax.axis_size("node")
    offset = lax.axis_index("node") * rows_dev
    scale = HEAD ** (-0.5)
    key_blocks = total // BLOCK
    states_single_float = states.astype(jnp.float32)
    inverse_norm_scale = lax.rsqrt(
        jnp.mean(states_single_float * states_single_float, axis=1, keepdims=True) + EPS
    )
    centered_states = states_single_float * inverse_norm_scale
    normalized_states = centered_states.astype(jnp.bfloat16)
    queries = jnp.dot(normalized_states, query_weight, preferred_element_type=jnp.float32).astype(
        jnp.bfloat16
    )
    keys = jnp.dot(normalized_states, key_weight, preferred_element_type=jnp.float32).astype(
        jnp.bfloat16
    )
    values = jnp.dot(normalized_states, value_weight, preferred_element_type=jnp.float32).astype(
        jnp.bfloat16
    )
    keys_all, values_all = (
        lax.all_gather(keys, "node", axis=0, tiled=True),
        lax.all_gather(values, "node", axis=0, tiled=True),
    )
    levels, onehot, level_bias = level_tables(starts, total, bias_table)
    positions = jnp.arange(total, dtype=jnp.int32)
    local = jnp.arange(rows_dev, dtype=jnp.int32)
    row_ids = offset + local
    row_levels = lax.dynamic_slice_in_dim(levels, offset, rows_dev, 0)
    row_onehot = lax.dynamic_slice_in_dim(onehot, offset, rows_dev, 0)
    slots = jnp.arange(blocks.shape[1], dtype=jnp.int32)
    live = slots[None, :] < counts[:, None]
    kinds = jnp.arange(key_blocks, dtype=jnp.int32)
    listed = jnp.any((blocks[:, :, None] == kinds[None, None, :]) & live[:, :, None], axis=1)
    visible = expand(listed) & (
        (levels[None, :] < row_levels[:, None]) | (positions[None, :] == row_ids[:, None])
    )
    prob_list = []
    lse_list = []
    mixed_list = []
    for head in range(HEADS):
        lower = head * HEAD
        scores = (
            cols_product(queries[:, lower : lower + HEAD], keys_all[:, lower : lower + HEAD])
            * scale
        )
        scores = scores + bias_block(row_onehot, level_bias[head], onehot)
        scores = jnp.where(visible, scores, NEG)
        peak = jnp.max(scores, axis=1, keepdims=True)
        mass = jnp.sum(jnp.where(visible, jnp.exp(scores - peak), 0.0), axis=1, keepdims=True)
        lse = peak + jnp.log(mass)
        probs = jnp.where(visible, jnp.exp(scores - lse), 0.0).astype(jnp.bfloat16)
        prob_list.append(probs)
        lse_list.append(lse)
        mixed_list.append(
            jnp.dot(probs, values_all[:, lower : lower + HEAD], preferred_element_type=jnp.float32)
        )
    mixed = jnp.concatenate(mixed_list, axis=1).astype(jnp.bfloat16)
    updated = (
        states_single_float + jnp.dot(mixed, out_weight, preferred_element_type=jnp.float32)
    ).astype(jnp.bfloat16)
    partial_out = rows_product(mixed, grads_in)
    d_mixed = cols_product(grads_in, out_weight).astype(jnp.bfloat16)
    score_grads = []
    delta_list = []
    query_grads = []
    for head in range(HEADS):
        lower = head * HEAD
        mixed_head = d_mixed[:, lower : lower + HEAD]
        delta = jnp.sum(
            mixed_head.astype(jnp.float32) * mixed[:, lower : lower + HEAD].astype(jnp.float32),
            axis=1,
            keepdims=True,
        )
        d_probs = cols_product(mixed_head, values_all[:, lower : lower + HEAD])
        d_scores = (prob_list[head].astype(jnp.float32) * (d_probs - delta)).astype(jnp.bfloat16)
        score_grads.append(d_scores)
        delta_list.append(delta)
        query_grads.append(
            jnp.dot(d_scores, keys_all[:, lower : lower + HEAD], preferred_element_type=jnp.float32)
            * scale
        )
    d_queries = jnp.concatenate(query_grads, axis=1).astype(jnp.bfloat16)
    key_pieces = []
    value_pieces = []
    for head in range(HEADS):
        lower = head * HEAD
        score_part = score_grads[head]
        prob_part = prob_list[head]
        key_pieces.append(rows_product(score_part, queries[:, lower : lower + HEAD]) * scale)
        value_pieces.append(rows_product(prob_part, d_mixed[:, lower : lower + HEAD]))
    key_value_grads = lax.psum_scatter(
        jnp.concatenate(key_pieces + value_pieces, axis=1).astype(jnp.bfloat16),
        "node",
        scatter_dimension=0,
        tiled=True,
    ).astype(jnp.float32)
    d_keys = key_value_grads[:, :width].astype(jnp.bfloat16)
    d_values = key_value_grads[:, width:].astype(jnp.bfloat16)
    normalized_gradient = (
        cols_product(d_queries, query_weight)
        + cols_product(d_keys, key_weight)
        + cols_product(d_values, value_weight)
    )
    node_state_gradient = (
        grads_in.astype(jnp.float32)
        + inverse_norm_scale
        * (
            normalized_gradient
            - centered_states
            * jnp.mean(normalized_gradient * centered_states, axis=1, keepdims=True)
        )
    ).astype(jnp.bfloat16)
    partial_query = rows_product(normalized_states, d_queries)
    partial_key = rows_product(normalized_states, d_keys)
    partial_value = rows_product(normalized_states, d_values)
    total_query, total_key, total_value, total_out = lax.psum(
        (partial_query, partial_key, partial_value, partial_out), ("node", "rep")
    )
    return (
        updated[None],
        node_state_gradient[None],
        total_query,
        total_key,
        total_value,
        total_out,
    )

LANES = 128
SLOTS = 16
LEVEL_PARTS = 3
VMEM_LIMIT = 24 * 1024 * 1024


def transposed_product(left, right):
    return lax.dot_general(left, right, CONTRACT_ROWS, preferred_element_type=jnp.float32)


def pair_product(left, right):
    return lax.dot_general(left, right, CONTRACT_COLS, preferred_element_type=jnp.float32)


def plain_product(left, right):
    return jnp.dot(left, right, preferred_element_type=jnp.float32)


def head_lanes(rows, half):
    lanes = lax.broadcasted_iota(jnp.int32, (rows, LANES), 1)
    return (lanes >= HEAD) if half else (lanes < HEAD)


def keep_lanes(array, mask):
    return jnp.where(mask, array, jnp.zeros_like(array))


def split_heads(array):
    rows = array.shape[0]
    return jnp.concatenate(
        [keep_lanes(array, head_lanes(rows, 0)), keep_lanes(array, head_lanes(rows, 1))], axis=0
    )


def merge_heads(array):
    rows = array.shape[0] // 2
    return jnp.where(head_lanes(rows, 0), array[:rows], array[rows:])


def normalize(states):
    wide = states.astype(jnp.float32)
    inverse = lax.rsqrt(jnp.mean(wide * wide, axis=1, keepdims=True) + EPS)
    return wide, inverse, wide * inverse


def level_tables_whole(scalars, levels, total):
    columns = lax.broadcasted_iota(jnp.int32, (SLOTS, total), 1)
    places = columns.astype(jnp.float32)
    slots = lax.broadcasted_iota(jnp.int32, (SLOTS, total), 0)
    level = jnp.zeros((SLOTS, total), jnp.int32)
    for entry in range(1, levels):
        level += (places >= scalars[HEADS, entry]).astype(jnp.int32)
    features = jnp.concatenate(
        [
            (level == slots).astype(jnp.float32),
            ((columns >> 6) == slots).astype(jnp.float32),
        ],
        axis=0,
    ).astype(jnp.bfloat16)
    own = lax.broadcasted_iota(jnp.int32, (SLOTS, LANES), 0)
    lanes = lax.broadcasted_iota(jnp.int32, (SLOTS, LANES), 1)
    part = lanes >> 4
    distance = own - (lanes & (SLOTS - 1))
    tables = []
    for head in range(HEADS):
        table = jnp.full((SLOTS, LANES), NEG, jnp.float32)
        for step in range(1, min(levels, DIST)):
            table = jnp.where(distance == step, scalars[head, step], table)
        high = table.astype(jnp.bfloat16).astype(jnp.float32)
        middle = (table - high).astype(jnp.bfloat16).astype(jnp.float32)
        low = table - high - middle
        split = jnp.where(part == 0, high, jnp.where(part == 1, middle, low))
        tables.append(jnp.where(part < LEVEL_PARTS, split, 0.0))
    table = jnp.concatenate(tables, axis=1).astype(jnp.bfloat16)
    picks_row = lax.broadcasted_iota(jnp.int32, (2 * SLOTS, LANES), 0)
    picks_lane = lax.broadcasted_iota(jnp.int32, (2 * SLOTS, LANES), 1)
    wanted = jnp.where(
        picks_lane < LEVEL_PARTS * SLOTS,
        picks_lane & (SLOTS - 1),
        picks_lane - (LEVEL_PARTS - 1) * SLOTS,
    )
    picks = (wanted == picks_row).astype(jnp.float32).astype(jnp.bfloat16)
    return features, table, transposed_product(features, picks).astype(jnp.bfloat16)


def project(chunk, weights, unit_t, projected):
    unit = normalize(chunk[: projected.shape[0], :])[2]
    unit_t[...] = unit.T.astype(jnp.bfloat16)
    unit = unit.astype(jnp.bfloat16)
    width = projected.shape[1] // 3
    for i, weight in enumerate(weights):
        projected[:, i * width : (i + 1) * width] = plain_product(unit, weight[...]).astype(
            jnp.bfloat16
        )


def tables_kernel(levels, scalars, features, table, column_features):
    rows, level_bias, columns = level_tables_whole(scalars, levels, features.shape[1])
    features[...] = rows
    table[...] = level_bias
    column_features[...] = columns


def project_kernel(chunk, query_w, key_w, value_w, unit_t, projected):
    project(chunk, (query_w, key_w, value_w), unit_t, projected)


def forward_kernel(
    place, scalars, own_states, own_t, own, near_states, near_t, near,
    far_states, far_t, far, last_states, query_w, key_w, value_w, features, table, column_features,
    normed_t, projected, probs, mixed, mixed_t,
    row_table, key_table, last_t, last,
):
    total, width = mixed.shape
    rows = own.shape[0]
    scale = HEAD ** (-0.5)
    project(last_states, (query_w, key_w, value_w), last_t, last)
    chunks = ((own_t, own), (near_t, near), (far_t, far), (last_t, last))
    for index, (unit_t, chunk) in enumerate(chunks):
        at = pl.ds(pl.multiple_of((place[0] ^ index) * rows, rows), rows)
        normed_t[:, at] = unit_t[...]
        projected[at, :] = chunk[...]
    slots = lax.broadcasted_iota(jnp.int32, (SLOTS, HEADS * LANES), 0)
    hidden = jnp.zeros((SLOTS, HEADS * LANES), jnp.float32)
    for index, part in enumerate((own_states, near_states, far_states, last_states)):
        tile = part[rows:, :].astype(jnp.float32)
        for block in range(rows // BLOCK):
            at = (place[0] ^ index) * (rows // BLOCK) + block
            hidden = jnp.where(slots == at, tile[block : block + 1, :], hidden)
    row_table[...] = transposed_product(
        features[...], jnp.concatenate([table[...], hidden.astype(jnp.bfloat16)], axis=0)
    ).astype(jnp.bfloat16)
    for pair in range(HEADS // 2):
        key_table[pair, :, :LANES] = projected[:, width + pair * LANES : width + (pair + 1) * LANES]
        key_table[pair, :, LANES:] = column_features[...]
    same = lax.broadcasted_iota(jnp.int32, (2 * LANES, LANES), 1) == (
        lax.broadcasted_iota(jnp.int32, (2 * LANES, LANES), 0) & (LANES - 1)
    )
    first_half = lax.broadcasted_iota(jnp.int32, (2 * LANES, 1), 0) < LANES
    for pair in range(HEADS // 2):
        lanes = slice(pair * LANES, (pair + 1) * LANES)
        values = slice(2 * width + pair * LANES, 2 * width + (pair + 1) * LANES)
        self_bias = jnp.where(
            first_half, scalars[2 * pair, 0], scalars[2 * pair + 1, 0]
        )
        for tile in range(total // LANES):
            low, high = tile * LANES, (tile + 1) * LANES
            stacked = slice(2 * low, 2 * high)
            query = split_heads(projected[low:high, lanes] * jnp.asarray(scale, jnp.bfloat16))
            key = key_table[pair, low:high, :LANES].astype(jnp.float32)
            self_score = jnp.sum(
                query.astype(jnp.float32) * jnp.concatenate([key, key], axis=0),
                axis=1,
                keepdims=True,
            )
            rest = jnp.concatenate(
                [
                    row_table[low:high, (2 * pair) * LANES : (2 * pair + 1) * LANES],
                    row_table[low:high, (2 * pair + 1) * LANES : (2 * pair + 2) * LANES],
                ],
                axis=0,
            )
            scores = pair_product(
                jnp.concatenate([query, rest], axis=1), key_table[pair, :high, :]
            )
            corner = jnp.where(same, self_score + self_bias, scores[:, low:])
            peak = jnp.max(corner, axis=1, keepdims=True)
            if low:
                peak = jnp.maximum(peak, jnp.max(scores[:, :low], axis=1, keepdims=True))
            corner = jnp.exp(corner - peak)
            mass = jnp.sum(corner, axis=1, keepdims=True)
            if low:
                weight = jnp.exp(scores[:, :low] - peak)
                mass += jnp.sum(weight, axis=1, keepdims=True)
                inverse = 1.0 / mass
                probs[pair, stacked, :low] = (weight * inverse).astype(jnp.bfloat16)
            else:
                inverse = 1.0 / mass
            probs[pair, stacked, low:high] = (corner * inverse).astype(jnp.bfloat16)
            both = merge_heads(
                plain_product(probs[pair, stacked, :high], projected[:high, values])
            )
            mixed[low:high, lanes] = both.astype(jnp.bfloat16)
            mixed_t[lanes, low:high] = both.T.astype(jnp.bfloat16)


def store_halves(place, value, keep, send, full):
    half = keep.shape[0]
    full[...] = value
    keep[...] = full[pl.ds(pl.multiple_of(place[1] * half, half), half), :]
    send[...] = full[pl.ds(pl.multiple_of((1 - place[1]) * half, half), half), :].astype(
        jnp.bfloat16
    )


def output_kernel(
    place, own, near, far, last, mixed_t, out_w, d_mixed, keep, send, gathered, full
):
    rows = own.shape[0]
    for index, chunk in enumerate((own, near, far, last)):
        at = pl.ds(pl.multiple_of((place[0] ^ index) * rows, rows), rows)
        gathered[at, :] = chunk[...]
    store_halves(place, plain_product(mixed_t[...], gathered[...]), keep, send, full)
    d_mixed[...] = pair_product(gathered[...], out_w[...]).astype(jnp.bfloat16)


def backward_kernel(
    pair, place, normed_t, projected, probs, mixed, d_mixed,
    d_own, keep, send,
    grads, key_sum, value_sum, full,
):
    total, width = mixed.shape
    rows = d_own.shape[0]
    scale = HEAD ** (-0.5)
    lanes, key_lanes, value_lanes = (
        slice(i * width + pair * LANES, i * width + (pair + 1) * LANES) for i in range(3)
    )
    for tile in reversed(range(total // LANES)):
        low, high = tile * LANES, (tile + 1) * LANES
        query = split_heads(projected[low:high, lanes])
        mix_grad = split_heads(d_mixed[low:high, lanes])
        mix = mixed[low:high, lanes].astype(jnp.float32)
        delta = jnp.sum(
            mix_grad.astype(jnp.float32) * jnp.concatenate([mix, mix], axis=0),
            axis=1,
            keepdims=True,
        )
        prob = probs[pair, 2 * low : 2 * high, :high]
        d_probs = pair_product(mix_grad, projected[:high, value_lanes])
        score_grad = (prob.astype(jnp.float32) * (d_probs - delta)).astype(jnp.bfloat16)
        grads[low:high, :LANES] = (
            merge_heads(plain_product(score_grad, projected[:high, key_lanes])) * scale
        ).astype(jnp.bfloat16)
        key_term = transposed_product(score_grad, query)
        value_term = transposed_product(prob, mix_grad)
        if high == total:
            key_sum[...] = key_term
            value_sum[...] = value_term
        else:
            key_sum[:high, :] += key_term
            value_sum[:high, :] += value_term
    grads[:, LANES : 2 * LANES] = (key_sum[...] * scale).astype(jnp.bfloat16)
    grads[:, 2 * LANES :] = value_sum[...].astype(jnp.bfloat16)
    store_halves(place, plain_product(normed_t[...], grads[...]), keep, send, full)
    d_own[...] = grads[pl.ds(pl.multiple_of(place[0] * rows, rows), rows), :]


def rows_kernel(place, own, grads_in, mixed, query_w, key_w, value_w, out_w, *rest):
    *d_own, updated, gradient = rest
    rows = updated.shape[0]
    width = mixed.shape[1]
    states, inverse, unit = normalize(own[:rows, :])
    here = pl.ds(pl.multiple_of(place[0] * rows, rows), rows)
    updated[...] = (states + plain_product(mixed[here, :], out_w[...])).astype(jnp.bfloat16)
    inner = jnp.zeros(updated.shape, jnp.float32)
    for pair, piece in enumerate(d_own):
        lanes = slice(pair * LANES, (pair + 1) * LANES)
        for i, weight in enumerate((query_w, key_w, value_w)):
            inner += pair_product(piece[:, i * LANES : (i + 1) * LANES], weight[:, lanes])
    gradient[...] = (
        grads_in[...].astype(jnp.float32)
        + inverse * (inner - unit * jnp.mean(inner * unit, axis=1, keepdims=True))
    ).astype(jnp.bfloat16)


def join_kernel(place, *refs):
    mine, other = refs[0:3], refs[3:6]
    total_query, total_key, total_value, total_out = refs[6:]
    for pieces, slot in ((mine, place[1]), (other, 1 - place[1])):
        half = pieces[0].shape[0]
        total_out[pl.ds(pl.multiple_of(slot * half, half), half), :] = pieces[0][...].astype(
            jnp.float32
        )
        half = pieces[1].shape[0]
        at = pl.ds(pl.multiple_of(slot * half, half), half)
        for pair, piece in enumerate(pieces[1:]):
            for i, total in enumerate((total_query, total_key, total_value)):
                total[at, pair * LANES : (pair + 1) * LANES] = piece[
                    :, i * LANES : (i + 1) * LANES
                ].astype(jnp.float32)


def run(kernel, outs, smem, arrays, scratch=(), cost=0):
    out_shape = tuple(jax.ShapeDtypeStruct(shape, dtype) for shape, dtype in outs)
    return pl.pallas_call(
        kernel,
        out_shape=out_shape,
        in_specs=[pl.BlockSpec(memory_space=pltpu.SMEM)] * len(smem)
        + [pl.BlockSpec(memory_space=pltpu.VMEM)] * len(arrays),
        out_specs=tuple([pl.BlockSpec(memory_space=pltpu.VMEM)] * len(outs)),
        scratch_shapes=list(scratch),
        compiler_params=pltpu.CompilerParams(vmem_limit_bytes=VMEM_LIMIT),
        cost_estimate=pl.CostEstimate(
            flops=cost * 1000000000, bytes_accessed=0, transcendentals=0
        ),
    )(*smem, *arrays)


def swap(array, axis, flip):
    return lax.ppermute(array, axis, [(i, i ^ flip) for i in range(lax.axis_size(axis))])


def sum_over_chips(keep, send):
    local = (keep + swap(send, "rep", 1).astype(jnp.float32)).astype(jnp.bfloat16)
    across = swap(local, "rep", 2)
    return local, across


def on_device_whole(
    node_states,
    cotangent,
    reach_blocks,
    reach_count,
    level_start,
    query_weight,
    key_weight,
    value_weight,
    out_weight,
    bias_table,
):
    states = node_states[0]
    grads_in = cotangent[0]
    blocks = reach_blocks[0]
    counts = reach_count[0]
    starts = level_start[0]
    rows, model = states.shape
    width = query_weight.shape[1]
    total = rows * lax.axis_size("node")
    place = jnp.stack([lax.axis_index("node"), lax.axis_index("rep") & 1]).astype(jnp.int32)
    half = jnp.bfloat16
    wide = jnp.float32

    local_blocks = blocks.shape[0]
    shape = (local_blocks, blocks.shape[1], HEADS * LANES)
    kinds = (lax.broadcasted_iota(jnp.int32, shape, 2) & (LANES - 1)) - LEVEL_PARTS * SLOTS
    slots = lax.broadcasted_iota(jnp.int32, shape, 1)
    match = (blocks[:, :, None] == kinds) & (slots < counts[:, None, None])
    match |= (kinds < 0) | (kinds >= SLOTS)
    hidden = (1.0 - jnp.max(match.astype(wide), axis=1)) * NEG
    own = jnp.concatenate(
        [states, jnp.pad(hidden.astype(half), ((0, SLOTS - local_blocks), (0, 0)))], axis=0
    )
    far = swap(own, "node", 2)
    near = swap(own, "node", 1)
    last = swap(far, "node", 1)
    grads_sent, near = lax.optimization_barrier((grads_in, near))
    grads_far = swap(grads_sent, "node", 2)
    grads_near = swap(grads_sent, "node", 1)
    scalars = jnp.pad(bias_table, ((0, HEADS), (0, LANES - DIST))) + jnp.pad(
        starts.astype(wide)[None, :], ((HEADS, HEADS - 1), (0, LANES - starts.shape[0]))
    )
    features, table, columns = run(
        functools.partial(tables_kernel, starts.shape[0] - 1),
        [
            ((2 * SLOTS, total), half),
            ((SLOTS, HEADS * LANES), half),
            ((total, LANES), half),
        ],
        [scalars],
        [],
        cost=10,
    )
    weights = [query_weight, key_weight, value_weight]
    table, *weights = lax.optimization_barrier((table, *weights))
    chunk_outs = [((model, rows), half), ((rows, 3 * width), half)]
    own_t, own_p = run(project_kernel, chunk_outs, [], [own, *weights])
    near_t, near_p = run(project_kernel, chunk_outs, [], [near, *weights])
    far_t, far_p = run(project_kernel, chunk_outs, [], [far, *weights])
    grads_far, own_p, near_p, far_p = lax.optimization_barrier((grads_far, own_p, near_p, far_p))
    grads_last = swap(grads_far, "node", 1)
    normed_t, projected, probs, mixed, mixed_t = run(
        forward_kernel,
        [
            ((model, total), half),
            ((total, 3 * width), half),
            ((HEADS // 2, 2 * total, total), half),
            ((total, width), half),
            ((width, total), half),
        ],
        [place, scalars],
        [
            own, own_t, own_p, near, near_t, near_p, far, far_t, far_p, last, *weights,
            features, table, columns,
        ],
        [
            pltpu.VMEM((total, HEADS * LANES), half),
            pltpu.VMEM((HEADS // 2, total, 2 * LANES), half),
            pltpu.VMEM((model, rows), half),
            pltpu.VMEM((rows, 3 * width), half),
        ],
        cost=5,
    )
    d_mixed, out_keep, out_send = run(
        output_kernel,
        [
            ((total, width), half),
            ((width // 2, model), wide),
            ((width // 2, model), half),
        ],
        [place],
        [grads_in, grads_near, grads_far, grads_last, mixed_t, out_weight],
        [pltpu.VMEM((total, model), half), pltpu.VMEM((width, model), wide)],
    )
    local, across = sum_over_chips(out_keep, out_send)
    halves = [(local, across)]
    d_own = []
    for pair in range(HEADS // 2):
        if pair:
            d_mixed, local = lax.optimization_barrier((d_mixed, local))
            halves[0] = (local, halves[0][1])
        own_grads, keep, send = run(
            functools.partial(backward_kernel, pair),
            [
                ((rows, 3 * LANES), half),
                ((model // 2, 3 * LANES), wide),
                ((model // 2, 3 * LANES), half),
            ],
            [place],
            [normed_t, projected, probs, mixed, d_mixed],
            [
                pltpu.VMEM((total, 3 * LANES), half),
                pltpu.VMEM((total, LANES), wide),
                pltpu.VMEM((total, LANES), wide),
                pltpu.VMEM((model, 3 * LANES), wide),
            ],
        )
        d_own.append(own_grads)
        halves.append(sum_over_chips(keep, send))
    d_own[-1], _ = lax.optimization_barrier((d_own[-1], halves[-1][0]))
    updated, node_state_gradient = run(
        rows_kernel,
        [((rows, model), half)] * 2,
        [place],
        [own, grads_in, mixed, *weights, out_weight, *d_own],
    )
    first, node_state_gradient = lax.optimization_barrier((halves[0][1], node_state_gradient))
    halves[0] = (halves[0][0], first)
    mine = [
        (near_sum.astype(wide) + far_sum.astype(wide)).astype(half) for near_sum, far_sum in halves
    ]
    other = [swap(piece, "rep", 1) for piece in mine]
    total_query, total_key, total_value, total_out = run(
        join_kernel,
        [((model, width), wide)] * 3 + [((width, model), wide)],
        [place],
        [*mine, *other],
    )
    return (
        updated[None],
        node_state_gradient[None],
        total_query,
        total_key,
        total_value,
        total_out,
    )


def on_device(node_states, cotangent, reach_blocks, reach_count, level_start, *rest):
    nodes = lax.axis_size("node")
    total = node_states.shape[1] * nodes
    small = (
        nodes == 4
        and lax.axis_size("rep") == 4
        and node_states.shape[1] == LANES
        and total // BLOCK <= SLOTS
        and level_start.shape[1] - 1 <= SLOTS
    )
    path = on_device_whole if small else on_device_general
    return path(node_states, cotangent, reach_blocks, reach_count, level_start, *rest)


def solution(mesh):
    in_specs = (
        P(("groups", "rep"), "node", None),
        P(("groups", "rep"), "node", None),
        P(("groups", "rep"), "node", None),
        P(("groups", "rep"), "node"),
        P(("groups", "rep"), None),
        P(),
        P(),
        P(),
        P(),
        P(),
    )
    out_specs = (
        P(("groups", "rep"), "node", None),
        P(("groups", "rep"), "node", None),
        P("groups", None),
        P("groups", None),
        P("groups", None),
        P("groups", None),
    )
    return jax.shard_map(
        on_device, mesh=mesh, in_specs=in_specs, out_specs=out_specs, check_vma=False
    )
```

```python
import functools

import jax
import jax.numpy as jnp
from jax import lax
from jax.experimental import pallas as pl
from jax.experimental.pallas import tpu as pltpu
from jax.sharding import PartitionSpec as P

HEADS = 4
HEAD = 64
BLOCK = 64
DIST = 32


EPS = 1e-05
NEG = -1e30
HIGH = lax.Precision.HIGHEST
CONTRACT_ROWS = (((0,), (0,)), ((), ()))
CONTRACT_COLS = (((1,), (1,)), ((), ()))


def rows_product(left, right):
    return lax.dot_general(left, right, CONTRACT_ROWS, preferred_element_type=jnp.float32)


def cols_product(left, right):
    return lax.dot_general(left, right, CONTRACT_COLS, preferred_element_type=jnp.float32)


def expand(listed):
    return jnp.repeat(jnp.repeat(listed, BLOCK, axis=0), BLOCK, axis=1)


def level_tables(starts, total, bias_table):
    level_count = starts.shape[0] - 1
    places = jnp.arange(total, dtype=jnp.int32)
    inner = starts[1:level_count]
    levels = jnp.sum((places[:, None] >= inner[None, :]).astype(jnp.int32), axis=1)
    marks = jnp.arange(level_count, dtype=jnp.int32)
    onehot = (levels[:, None] == marks[None, :]).astype(jnp.float32)
    spread = jnp.clip(marks[:, None] - marks[None, :], 0, DIST - 1)
    picks = (spread[:, :, None] == jnp.arange(DIST, dtype=jnp.int32)[None, None, :]).astype(
        jnp.float32
    )
    level_bias = jnp.einsum("hd,abd->hab", bias_table, picks, precision=HIGH)
    return (levels, onehot, level_bias)


def bias_block(row_onehot, head_bias, col_onehot):
    row_part = jnp.dot(row_onehot, head_bias, precision=HIGH)
    return lax.dot_general(row_part, col_onehot, CONTRACT_COLS, precision=HIGH)


def on_device_general(
    node_states,
    cotangent,
    reach_blocks,
    reach_count,
    level_start,
    query_weight,
    key_weight,
    value_weight,
    out_weight,
    bias_table,
):
    states = node_states[0]
    grads_in = cotangent[0]
    blocks = reach_blocks[0]
    counts = reach_count[0]
    starts = level_start[0]
    rows_dev = states.shape[0]
    width = query_weight.shape[1]
    total = rows_dev * lax.axis_size("node")
    offset = lax.axis_index("node") * rows_dev
    scale = HEAD ** (-0.5)
    key_blocks = total // BLOCK
    states_single_float = states.astype(jnp.float32)
    inverse_norm_scale = lax.rsqrt(
        jnp.mean(states_single_float * states_single_float, axis=1, keepdims=True) + EPS
    )
    centered_states = states_single_float * inverse_norm_scale
    normalized_states = centered_states.astype(jnp.bfloat16)
    queries = jnp.dot(normalized_states, query_weight, preferred_element_type=jnp.float32).astype(
        jnp.bfloat16
    )
    keys = jnp.dot(normalized_states, key_weight, preferred_element_type=jnp.float32).astype(
        jnp.bfloat16
    )
    values = jnp.dot(normalized_states, value_weight, preferred_element_type=jnp.float32).astype(
        jnp.bfloat16
    )
    keys_all, values_all = (
        lax.all_gather(keys, "node", axis=0, tiled=True),
        lax.all_gather(values, "node", axis=0, tiled=True),
    )
    levels, onehot, level_bias = level_tables(starts, total, bias_table)
    positions = jnp.arange(total, dtype=jnp.int32)
    local = jnp.arange(rows_dev, dtype=jnp.int32)
    row_ids = offset + local
    row_levels = lax.dynamic_slice_in_dim(levels, offset, rows_dev, 0)
    row_onehot = lax.dynamic_slice_in_dim(onehot, offset, rows_dev, 0)
    slots = jnp.arange(blocks.shape[1], dtype=jnp.int32)
    live = slots[None, :] < counts[:, None]
    kinds = jnp.arange(key_blocks, dtype=jnp.int32)
    listed = jnp.any((blocks[:, :, None] == kinds[None, None, :]) & live[:, :, None], axis=1)
    visible = expand(listed) & (
        (levels[None, :] < row_levels[:, None]) | (positions[None, :] == row_ids[:, None])
    )
    prob_list = []
    lse_list = []
    mixed_list = []
    for head in range(HEADS):
        lower = head * HEAD
        scores = (
            cols_product(queries[:, lower : lower + HEAD], keys_all[:, lower : lower + HEAD])
            * scale
        )
        scores = scores + bias_block(row_onehot, level_bias[head], onehot)
        scores = jnp.where(visible, scores, NEG)
        peak = jnp.max(scores, axis=1, keepdims=True)
        mass = jnp.sum(jnp.where(visible, jnp.exp(scores - peak), 0.0), axis=1, keepdims=True)
        lse = peak + jnp.log(mass)
        probs = jnp.where(visible, jnp.exp(scores - lse), 0.0).astype(jnp.bfloat16)
        prob_list.append(probs)
        lse_list.append(lse)
        mixed_list.append(
            jnp.dot(probs, values_all[:, lower : lower + HEAD], preferred_element_type=jnp.float32)
        )
    mixed = jnp.concatenate(mixed_list, axis=1).astype(jnp.bfloat16)
    updated = (
        states_single_float + jnp.dot(mixed, out_weight, preferred_element_type=jnp.float32)
    ).astype(jnp.bfloat16)
    partial_out = rows_product(mixed, grads_in)
    d_mixed = cols_product(grads_in, out_weight).astype(jnp.bfloat16)
    score_grads = []
    delta_list = []
    query_grads = []
    for head in range(HEADS):
        lower = head * HEAD
        mixed_head = d_mixed[:, lower : lower + HEAD]
        delta = jnp.sum(
            mixed_head.astype(jnp.float32) * mixed[:, lower : lower + HEAD].astype(jnp.float32),
            axis=1,
            keepdims=True,
        )
        d_probs = cols_product(mixed_head, values_all[:, lower : lower + HEAD])
        d_scores = (prob_list[head].astype(jnp.float32) * (d_probs - delta)).astype(jnp.bfloat16)
        score_grads.append(d_scores)
        delta_list.append(delta)
        query_grads.append(
            jnp.dot(d_scores, keys_all[:, lower : lower + HEAD], preferred_element_type=jnp.float32)
            * scale
        )
    d_queries = jnp.concatenate(query_grads, axis=1).astype(jnp.bfloat16)
    key_pieces = []
    value_pieces = []
    for head in range(HEADS):
        lower = head * HEAD
        score_part = score_grads[head]
        prob_part = prob_list[head]
        key_pieces.append(rows_product(score_part, queries[:, lower : lower + HEAD]) * scale)
        value_pieces.append(rows_product(prob_part, d_mixed[:, lower : lower + HEAD]))
    key_value_grads = lax.psum_scatter(
        jnp.concatenate(key_pieces + value_pieces, axis=1).astype(jnp.bfloat16),
        "node",
        scatter_dimension=0,
        tiled=True,
    ).astype(jnp.float32)
    d_keys = key_value_grads[:, :width].astype(jnp.bfloat16)
    d_values = key_value_grads[:, width:].astype(jnp.bfloat16)
    normalized_gradient = (
        cols_product(d_queries, query_weight)
        + cols_product(d_keys, key_weight)
        + cols_product(d_values, value_weight)
    )
    node_state_gradient = (
        grads_in.astype(jnp.float32)
        + inverse_norm_scale
        * (
            normalized_gradient
            - centered_states
            * jnp.mean(normalized_gradient * centered_states, axis=1, keepdims=True)
        )
    ).astype(jnp.bfloat16)
    partial_query = rows_product(normalized_states, d_queries)
    partial_key = rows_product(normalized_states, d_keys)
    partial_value = rows_product(normalized_states, d_values)
    total_query, total_key, total_value, total_out = lax.psum(
        (partial_query, partial_key, partial_value, partial_out), ("node", "rep")
    )
    return (
        updated[None],
        node_state_gradient[None],
        total_query,
        total_key,
        total_value,
        total_out,
    )

LANES = 128
SLOTS = 16
LEVEL_PARTS = 3
VMEM_LIMIT = 24 * 1024 * 1024


def transposed_product(left, right):
    return lax.dot_general(left, right, CONTRACT_ROWS, preferred_element_type=jnp.float32)


def pair_product(left, right):
    return lax.dot_general(left, right, CONTRACT_COLS, preferred_element_type=jnp.float32)


def plain_product(left, right):
    return jnp.dot(left, right, preferred_element_type=jnp.float32)


def head_lanes(rows, half):
    lanes = lax.broadcasted_iota(jnp.int32, (rows, LANES), 1)
    return (lanes >= HEAD) if half else (lanes < HEAD)


def keep_lanes(array, mask):
    return jnp.where(mask, array, jnp.zeros_like(array))


def split_heads(array):
    rows = array.shape[0]
    return jnp.concatenate(
        [keep_lanes(array, head_lanes(rows, 0)), keep_lanes(array, head_lanes(rows, 1))], axis=0
    )


def merge_heads(array):
    rows = array.shape[0] // 2
    return jnp.where(head_lanes(rows, 0), array[:rows], array[rows:])


def normalize(states):
    wide = states.astype(jnp.float32)
    inverse = lax.rsqrt(jnp.mean(wide * wide, axis=1, keepdims=True) + EPS)
    return wide, inverse, wide * inverse


def level_tables_whole(scalars, levels, total):
    columns = lax.broadcasted_iota(jnp.int32, (SLOTS, total), 1)
    places = columns.astype(jnp.float32)
    slots = lax.broadcasted_iota(jnp.int32, (SLOTS, total), 0)
    level = jnp.zeros((SLOTS, total), jnp.int32)
    for entry in range(1, levels):
        level += (places >= scalars[HEADS, entry]).astype(jnp.int32)
    features = jnp.concatenate(
        [
            (level == slots).astype(jnp.float32),
            ((columns >> 6) == slots).astype(jnp.float32),
        ],
        axis=0,
    ).astype(jnp.bfloat16)
    own = lax.broadcasted_iota(jnp.int32, (SLOTS, LANES), 0)
    lanes = lax.broadcasted_iota(jnp.int32, (SLOTS, LANES), 1)
    part = lanes >> 4
    distance = own - (lanes & (SLOTS - 1))
    tables = []
    for head in range(HEADS):
        table = jnp.full((SLOTS, LANES), NEG, jnp.float32)
        for step in range(1, min(levels, DIST)):
            table = jnp.where(distance == step, scalars[head, step], table)
        high = table.astype(jnp.bfloat16).astype(jnp.float32)
        middle = (table - high).astype(jnp.bfloat16).astype(jnp.float32)
        low = table - high - middle
        split = jnp.where(part == 0, high, jnp.where(part == 1, middle, low))
        tables.append(jnp.where(part < LEVEL_PARTS, split, 0.0))
    table = jnp.concatenate(tables, axis=1).astype(jnp.bfloat16)
    picks_row = lax.broadcasted_iota(jnp.int32, (2 * SLOTS, LANES), 0)
    picks_lane = lax.broadcasted_iota(jnp.int32, (2 * SLOTS, LANES), 1)
    wanted = jnp.where(
        picks_lane < LEVEL_PARTS * SLOTS,
        picks_lane & (SLOTS - 1),
        picks_lane - (LEVEL_PARTS - 1) * SLOTS,
    )
    picks = (wanted == picks_row).astype(jnp.float32).astype(jnp.bfloat16)
    return features, table, transposed_product(features, picks).astype(jnp.bfloat16)


def project(chunk, weights, unit_t, projected):
    unit = normalize(chunk[: projected.shape[0], :])[2]
    unit_t[...] = unit.T.astype(jnp.bfloat16)
    unit = unit.astype(jnp.bfloat16)
    width = projected.shape[1] // 3
    for i, weight in enumerate(weights):
        projected[:, i * width : (i + 1) * width] = plain_product(unit, weight[...]).astype(
            jnp.bfloat16
        )


def tables_kernel(levels, scalars, features, table, column_features):
    rows, level_bias, columns = level_tables_whole(scalars, levels, features.shape[1])
    features[...] = rows
    table[...] = level_bias
    column_features[...] = columns


def project_kernel(chunk, query_w, key_w, value_w, unit_t, projected):
    project(chunk, (query_w, key_w, value_w), unit_t, projected)


def forward_kernel(
    place, scalars, own_states, own_t, own, near_states, near_t, near,
    far_states, far_t, far, last_states, query_w, key_w, value_w, features, table, column_features,
    normed_t, projected, probs, mixed, mixed_t,
    row_table, key_table, last_t, last,
):
    total, width = mixed.shape
    rows = own.shape[0]
    scale = HEAD ** (-0.5)
    project(last_states, (query_w, key_w, value_w), last_t, last)
    chunks = ((own_t, own), (near_t, near), (far_t, far), (last_t, last))
    for index, (unit_t, chunk) in enumerate(chunks):
        at = pl.ds(pl.multiple_of((place[0] ^ index) * rows, rows), rows)
        normed_t[:, at] = unit_t[...]
        projected[at, :] = chunk[...]
    slots = lax.broadcasted_iota(jnp.int32, (SLOTS, HEADS * LANES), 0)
    hidden = jnp.zeros((SLOTS, HEADS * LANES), jnp.float32)
    for index, part in enumerate((own_states, near_states, far_states, last_states)):
        tile = part[rows:, :].astype(jnp.float32)
        for block in range(rows // BLOCK):
            at = (place[0] ^ index) * (rows // BLOCK) + block
            hidden = jnp.where(slots == at, tile[block : block + 1, :], hidden)
    row_table[...] = transposed_product(
        features[...], jnp.concatenate([table[...], hidden.astype(jnp.bfloat16)], axis=0)
    ).astype(jnp.bfloat16)
    for pair in range(HEADS // 2):
        key_table[pair, :, :LANES] = projected[:, width + pair * LANES : width + (pair + 1) * LANES]
        key_table[pair, :, LANES:] = column_features[...]
    same = lax.broadcasted_iota(jnp.int32, (2 * LANES, LANES), 1) == (
        lax.broadcasted_iota(jnp.int32, (2 * LANES, LANES), 0) & (LANES - 1)
    )
    first_half = lax.broadcasted_iota(jnp.int32, (2 * LANES, 1), 0) < LANES
    for pair in range(HEADS // 2):
        lanes = slice(pair * LANES, (pair + 1) * LANES)
        values = slice(2 * width + pair * LANES, 2 * width + (pair + 1) * LANES)
        self_bias = jnp.where(
            first_half, scalars[2 * pair, 0], scalars[2 * pair + 1, 0]
        )
        for tile in range(total // LANES):
            low, high = tile * LANES, (tile + 1) * LANES
            stacked = slice(2 * low, 2 * high)
            query = split_heads(projected[low:high, lanes] * jnp.asarray(scale, jnp.bfloat16))
            key = key_table[pair, low:high, :LANES].astype(jnp.float32)
            self_score = jnp.sum(
                query.astype(jnp.float32) * jnp.concatenate([key, key], axis=0),
                axis=1,
                keepdims=True,
            )
            rest = jnp.concatenate(
                [
                    row_table[low:high, (2 * pair) * LANES : (2 * pair + 1) * LANES],
                    row_table[low:high, (2 * pair + 1) * LANES : (2 * pair + 2) * LANES],
                ],
                axis=0,
            )
            scores = pair_product(
                jnp.concatenate([query, rest], axis=1), key_table[pair, :high, :]
            )
            corner = jnp.where(same, self_score + self_bias, scores[:, low:])
            peak = jnp.max(corner, axis=1, keepdims=True)
            if low:
                peak = jnp.maximum(peak, jnp.max(scores[:, :low], axis=1, keepdims=True))
            corner = jnp.exp(corner - peak)
            mass = jnp.sum(corner, axis=1, keepdims=True)
            if low:
                weight = jnp.exp(scores[:, :low] - peak)
                mass += jnp.sum(weight, axis=1, keepdims=True)
                inverse = 1.0 / mass
                probs[pair, stacked, :low] = (weight * inverse).astype(jnp.bfloat16)
            else:
                inverse = 1.0 / mass
            probs[pair, stacked, low:high] = (corner * inverse).astype(jnp.bfloat16)
            both = merge_heads(
                plain_product(probs[pair, stacked, :high], projected[:high, values])
            )
            mixed[low:high, lanes] = both.astype(jnp.bfloat16)
            mixed_t[lanes, low:high] = both.T.astype(jnp.bfloat16)


def store_halves(place, value, keep, send, full):
    half = keep.shape[0]
    full[...] = value
    keep[...] = full[pl.ds(pl.multiple_of(place[1] * half, half), half), :]
    send[...] = full[pl.ds(pl.multiple_of((1 - place[1]) * half, half), half), :].astype(
        jnp.bfloat16
    )


def mix_kernel(place, own, near, far, last, out_w, gathered, d_mixed):
    rows = own.shape[0]
    for index, chunk in enumerate((own, near, far, last)):
        at = pl.ds(pl.multiple_of((place[0] ^ index) * rows, rows), rows)
        gathered[at, :] = chunk[...]
    d_mixed[...] = pair_product(gathered[...], out_w[...]).astype(jnp.bfloat16)


def output_kernel(place, gathered, mixed_t, keep, send, full):
    store_halves(place, plain_product(mixed_t[...], gathered[...]), keep, send, full)


def backward_kernel(
    pair, place, normed_t, projected, probs, mixed, d_mixed,
    d_own, keep, send,
    grads, key_sum, value_sum, full,
):
    total, width = mixed.shape
    rows = d_own.shape[0]
    scale = HEAD ** (-0.5)
    lanes, key_lanes, value_lanes = (
        slice(i * width + pair * LANES, i * width + (pair + 1) * LANES) for i in range(3)
    )
    for tile in reversed(range(total // LANES)):
        low, high = tile * LANES, (tile + 1) * LANES
        query = split_heads(projected[low:high, lanes])
        mix_grad = split_heads(d_mixed[low:high, lanes])
        mix = mixed[low:high, lanes].astype(jnp.float32)
        delta = jnp.sum(
            mix_grad.astype(jnp.float32) * jnp.concatenate([mix, mix], axis=0),
            axis=1,
            keepdims=True,
        )
        prob = probs[pair, 2 * low : 2 * high, :high]
        d_probs = pair_product(mix_grad, projected[:high, value_lanes])
        score_grad = (prob.astype(jnp.float32) * (d_probs - delta)).astype(jnp.bfloat16)
        grads[low:high, :LANES] = (
            merge_heads(plain_product(score_grad, projected[:high, key_lanes])) * scale
        ).astype(jnp.bfloat16)
        key_term = transposed_product(score_grad, query)
        value_term = transposed_product(prob, mix_grad)
        if high == total:
            key_sum[...] = key_term
            value_sum[...] = value_term
        else:
            key_sum[:high, :] += key_term
            value_sum[:high, :] += value_term
    grads[:, LANES : 2 * LANES] = (key_sum[...] * scale).astype(jnp.bfloat16)
    grads[:, 2 * LANES :] = value_sum[...].astype(jnp.bfloat16)
    store_halves(place, plain_product(normed_t[...], grads[...]), keep, send, full)
    d_own[...] = grads[pl.ds(pl.multiple_of(place[0] * rows, rows), rows), :]


def rows_kernel(place, own, grads_in, mixed, query_w, key_w, value_w, out_w, *rest):
    *d_own, updated, gradient = rest
    rows = updated.shape[0]
    width = mixed.shape[1]
    states, inverse, unit = normalize(own[:rows, :])
    here = pl.ds(pl.multiple_of(place[0] * rows, rows), rows)
    updated[...] = (states + plain_product(mixed[here, :], out_w[...])).astype(jnp.bfloat16)
    inner = jnp.zeros(updated.shape, jnp.float32)
    for pair, piece in enumerate(d_own):
        lanes = slice(pair * LANES, (pair + 1) * LANES)
        for i, weight in enumerate((query_w, key_w, value_w)):
            inner += pair_product(piece[:, i * LANES : (i + 1) * LANES], weight[:, lanes])
    gradient[...] = (
        grads_in[...].astype(jnp.float32)
        + inverse * (inner - unit * jnp.mean(inner * unit, axis=1, keepdims=True))
    ).astype(jnp.bfloat16)


def join_kernel(place, *refs):
    mine, other = refs[0:3], refs[3:6]
    total_query, total_key, total_value, total_out = refs[6:]
    for pieces, slot in ((mine, place[1]), (other, 1 - place[1])):
        half = pieces[0].shape[0]
        total_out[pl.ds(pl.multiple_of(slot * half, half), half), :] = pieces[0][...].astype(
            jnp.float32
        )
        half = pieces[1].shape[0]
        at = pl.ds(pl.multiple_of(slot * half, half), half)
        for pair, piece in enumerate(pieces[1:]):
            for i, total in enumerate((total_query, total_key, total_value)):
                total[at, pair * LANES : (pair + 1) * LANES] = piece[
                    :, i * LANES : (i + 1) * LANES
                ].astype(jnp.float32)


def run(kernel, outs, smem, arrays, scratch=(), cost=0):
    out_shape = tuple(jax.ShapeDtypeStruct(shape, dtype) for shape, dtype in outs)
    return pl.pallas_call(
        kernel,
        out_shape=out_shape,
        in_specs=[pl.BlockSpec(memory_space=pltpu.SMEM)] * len(smem)
        + [pl.BlockSpec(memory_space=pltpu.VMEM)] * len(arrays),
        out_specs=tuple([pl.BlockSpec(memory_space=pltpu.VMEM)] * len(outs)),
        scratch_shapes=list(scratch),
        compiler_params=pltpu.CompilerParams(vmem_limit_bytes=VMEM_LIMIT),
        cost_estimate=pl.CostEstimate(
            flops=cost * 1000000000, bytes_accessed=0, transcendentals=0
        ),
    )(*smem, *arrays)


def swap(array, axis, flip):
    return lax.ppermute(array, axis, [(i, i ^ flip) for i in range(lax.axis_size(axis))])


def sum_over_chips(keep, send):
    local = (keep + swap(send, "rep", 1).astype(jnp.float32)).astype(jnp.bfloat16)
    across = swap(local, "rep", 2)
    return local, across


def on_device_whole(
    node_states,
    cotangent,
    reach_blocks,
    reach_count,
    level_start,
    query_weight,
    key_weight,
    value_weight,
    out_weight,
    bias_table,
):
    states = node_states[0]
    grads_in = cotangent[0]
    blocks = reach_blocks[0]
    counts = reach_count[0]
    starts = level_start[0]
    rows, model = states.shape
    width = query_weight.shape[1]
    total = rows * lax.axis_size("node")
    place = jnp.stack([lax.axis_index("node"), lax.axis_index("rep") & 1]).astype(jnp.int32)
    half = jnp.bfloat16
    wide = jnp.float32

    local_blocks = blocks.shape[0]
    shape = (local_blocks, blocks.shape[1], HEADS * LANES)
    kinds = (lax.broadcasted_iota(jnp.int32, shape, 2) & (LANES - 1)) - LEVEL_PARTS * SLOTS
    slots = lax.broadcasted_iota(jnp.int32, shape, 1)
    match = (blocks[:, :, None] == kinds) & (slots < counts[:, None, None])
    match |= (kinds < 0) | (kinds >= SLOTS)
    hidden = (1.0 - jnp.max(match.astype(wide), axis=1)) * NEG
    own = jnp.concatenate(
        [states, jnp.pad(hidden.astype(half), ((0, SLOTS - local_blocks), (0, 0)))], axis=0
    )
    far = swap(own, "node", 2)
    near = swap(own, "node", 1)
    last = swap(far, "node", 1)
    grads_sent, near = lax.optimization_barrier((grads_in, near))
    grads_far = swap(grads_sent, "node", 2)
    grads_near = swap(grads_sent, "node", 1)
    scalars = jnp.pad(bias_table, ((0, HEADS), (0, LANES - DIST))) + jnp.pad(
        starts.astype(wide)[None, :], ((HEADS, HEADS - 1), (0, LANES - starts.shape[0]))
    )
    features, table, columns = run(
        functools.partial(tables_kernel, starts.shape[0] - 1),
        [
            ((2 * SLOTS, total), half),
            ((SLOTS, HEADS * LANES), half),
            ((total, LANES), half),
        ],
        [scalars],
        [],
        cost=10,
    )
    weights = [query_weight, key_weight, value_weight]
    table, *weights = lax.optimization_barrier((table, *weights))
    chunk_outs = [((model, rows), half), ((rows, 3 * width), half)]
    own_t, own_p = run(project_kernel, chunk_outs, [], [own, *weights])
    near_t, near_p = run(project_kernel, chunk_outs, [], [near, *weights])
    far_t, far_p = run(project_kernel, chunk_outs, [], [far, *weights])
    grads_far, own_p, near_p, far_p = lax.optimization_barrier((grads_far, own_p, near_p, far_p))
    grads_last = swap(grads_far, "node", 1)
    normed_t, projected, probs, mixed, mixed_t = run(
        forward_kernel,
        [
            ((model, total), half),
            ((total, 3 * width), half),
            ((HEADS // 2, 2 * total, total), half),
            ((total, width), half),
            ((width, total), half),
        ],
        [place, scalars],
        [
            own, own_t, own_p, near, near_t, near_p, far, far_t, far_p, last, *weights,
            features, table, columns,
        ],
        [
            pltpu.VMEM((total, HEADS * LANES), half),
            pltpu.VMEM((HEADS // 2, total, 2 * LANES), half),
            pltpu.VMEM((model, rows), half),
            pltpu.VMEM((rows, 3 * width), half),
        ],
        cost=5,
    )
    gathered, d_mixed = run(
        mix_kernel,
        [((total, model), half), ((total, width), half)],
        [place],
        [grads_in, grads_near, grads_far, grads_last, out_weight],
    )
    halves = []
    d_own = []
    for pair in range(HEADS // 2):
        if pair == 1:
            local, across = halves[0]
            gathered, keep = lax.optimization_barrier((gathered, keep))
            out_keep, out_send = run(
                output_kernel,
                [((width // 2, model), wide), ((width // 2, model), half)],
                [place],
                [gathered, mixed_t],
                [pltpu.VMEM((width, model), wide)],
            )
            d_mixed, local, out_send = lax.optimization_barrier((d_mixed, local, out_send))
            halves[0] = (local, across)
        own_grads, keep, send = run(
            functools.partial(backward_kernel, pair),
            [
                ((rows, 3 * LANES), half),
                ((model // 2, 3 * LANES), wide),
                ((model // 2, 3 * LANES), half),
            ],
            [place],
            [normed_t, projected, probs, mixed, d_mixed],
            [
                pltpu.VMEM((total, 3 * LANES), half),
                pltpu.VMEM((total, LANES), wide),
                pltpu.VMEM((total, LANES), wide),
                pltpu.VMEM((model, 3 * LANES), wide),
            ],
        )
        d_own.append(own_grads)
        halves.append(sum_over_chips(keep, send))
    halves.append(sum_over_chips(out_keep, out_send))
    d_own[-1], _ = lax.optimization_barrier((d_own[-1], halves[1][0]))
    updated, node_state_gradient = run(
        rows_kernel,
        [((rows, model), half)] * 2,
        [place],
        [own, grads_in, mixed, *weights, out_weight, *d_own],
    )
    first, node_state_gradient = lax.optimization_barrier((halves[0][1], node_state_gradient))
    halves[0] = (halves[0][0], first)
    mine = [
        (near_sum.astype(wide) + far_sum.astype(wide)).astype(half) for near_sum, far_sum in halves
    ]
    other = [swap(piece, "rep", 1) for piece in mine]
    total_query, total_key, total_value, total_out = run(
        join_kernel,
        [((model, width), wide)] * 3 + [((width, model), wide)],
        [place],
        [mine[-1], *mine[:-1], other[-1], *other[:-1]],
    )
    return (
        updated[None],
        node_state_gradient[None],
        total_query,
        total_key,
        total_value,
        total_out,
    )


def on_device(node_states, cotangent, reach_blocks, reach_count, level_start, *rest):
    nodes = lax.axis_size("node")
    total = node_states.shape[1] * nodes
    small = (
        nodes == 4
        and lax.axis_size("rep") == 4
        and node_states.shape[1] == LANES
        and total // BLOCK <= SLOTS
        and level_start.shape[1] - 1 <= SLOTS
    )
    path = on_device_whole if small else on_device_general
    return path(node_states, cotangent, reach_blocks, reach_count, level_start, *rest)


def solution(mesh):
    in_specs = (
        P(("groups", "rep"), "node", None),
        P(("groups", "rep"), "node", None),
        P(("groups", "rep"), "node", None),
        P(("groups", "rep"), "node"),
        P(("groups", "rep"), None),
        P(),
        P(),
        P(),
        P(),
        P(),
    )
    out_specs = (
        P(("groups", "rep"), "node", None),
        P(("groups", "rep"), "node", None),
        P("groups", None),
        P("groups", None),
        P("groups", None),
        P("groups", None),
    )
    return jax.shard_map(
        on_device, mesh=mesh, in_specs=in_specs, out_specs=out_specs, check_vma=False
    )
```

```python
import functools

import jax
import jax.numpy as jnp
from jax import lax
from jax.experimental import pallas as pl
from jax.experimental.pallas import tpu as pltpu
from jax.sharding import PartitionSpec as P

HEADS = 4
HEAD = 64
BLOCK = 64
DIST = 32


EPS = 1e-05
NEG = -1e30
HIGH = lax.Precision.HIGHEST
CONTRACT_ROWS = (((0,), (0,)), ((), ()))
CONTRACT_COLS = (((1,), (1,)), ((), ()))


def rows_product(left, right):
    return lax.dot_general(left, right, CONTRACT_ROWS, preferred_element_type=jnp.float32)


def cols_product(left, right):
    return lax.dot_general(left, right, CONTRACT_COLS, preferred_element_type=jnp.float32)


def expand(listed):
    return jnp.repeat(jnp.repeat(listed, BLOCK, axis=0), BLOCK, axis=1)


def level_tables(starts, total, bias_table):
    level_count = starts.shape[0] - 1
    places = jnp.arange(total, dtype=jnp.int32)
    inner = starts[1:level_count]
    levels = jnp.sum((places[:, None] >= inner[None, :]).astype(jnp.int32), axis=1)
    marks = jnp.arange(level_count, dtype=jnp.int32)
    onehot = (levels[:, None] == marks[None, :]).astype(jnp.float32)
    spread = jnp.clip(marks[:, None] - marks[None, :], 0, DIST - 1)
    picks = (spread[:, :, None] == jnp.arange(DIST, dtype=jnp.int32)[None, None, :]).astype(
        jnp.float32
    )
    level_bias = jnp.einsum("hd,abd->hab", bias_table, picks, precision=HIGH)
    return (levels, onehot, level_bias)


def bias_block(row_onehot, head_bias, col_onehot):
    row_part = jnp.dot(row_onehot, head_bias, precision=HIGH)
    return lax.dot_general(row_part, col_onehot, CONTRACT_COLS, precision=HIGH)


def on_device_general(
    node_states,
    cotangent,
    reach_blocks,
    reach_count,
    level_start,
    query_weight,
    key_weight,
    value_weight,
    out_weight,
    bias_table,
):
    states = node_states[0]
    grads_in = cotangent[0]
    blocks = reach_blocks[0]
    counts = reach_count[0]
    starts = level_start[0]
    rows_dev = states.shape[0]
    width = query_weight.shape[1]
    total = rows_dev * lax.axis_size("node")
    offset = lax.axis_index("node") * rows_dev
    scale = HEAD ** (-0.5)
    key_blocks = total // BLOCK
    states_single_float = states.astype(jnp.float32)
    inverse_norm_scale = lax.rsqrt(
        jnp.mean(states_single_float * states_single_float, axis=1, keepdims=True) + EPS
    )
    centered_states = states_single_float * inverse_norm_scale
    normalized_states = centered_states.astype(jnp.bfloat16)
    queries = jnp.dot(normalized_states, query_weight, preferred_element_type=jnp.float32).astype(
        jnp.bfloat16
    )
    keys = jnp.dot(normalized_states, key_weight, preferred_element_type=jnp.float32).astype(
        jnp.bfloat16
    )
    values = jnp.dot(normalized_states, value_weight, preferred_element_type=jnp.float32).astype(
        jnp.bfloat16
    )
    keys_all, values_all = (
        lax.all_gather(keys, "node", axis=0, tiled=True),
        lax.all_gather(values, "node", axis=0, tiled=True),
    )
    levels, onehot, level_bias = level_tables(starts, total, bias_table)
    positions = jnp.arange(total, dtype=jnp.int32)
    local = jnp.arange(rows_dev, dtype=jnp.int32)
    row_ids = offset + local
    row_levels = lax.dynamic_slice_in_dim(levels, offset, rows_dev, 0)
    row_onehot = lax.dynamic_slice_in_dim(onehot, offset, rows_dev, 0)
    slots = jnp.arange(blocks.shape[1], dtype=jnp.int32)
    live = slots[None, :] < counts[:, None]
    kinds = jnp.arange(key_blocks, dtype=jnp.int32)
    listed = jnp.any((blocks[:, :, None] == kinds[None, None, :]) & live[:, :, None], axis=1)
    visible = expand(listed) & (
        (levels[None, :] < row_levels[:, None]) | (positions[None, :] == row_ids[:, None])
    )
    prob_list = []
    lse_list = []
    mixed_list = []
    for head in range(HEADS):
        lower = head * HEAD
        scores = (
            cols_product(queries[:, lower : lower + HEAD], keys_all[:, lower : lower + HEAD])
            * scale
        )
        scores = scores + bias_block(row_onehot, level_bias[head], onehot)
        scores = jnp.where(visible, scores, NEG)
        peak = jnp.max(scores, axis=1, keepdims=True)
        mass = jnp.sum(jnp.where(visible, jnp.exp(scores - peak), 0.0), axis=1, keepdims=True)
        lse = peak + jnp.log(mass)
        probs = jnp.where(visible, jnp.exp(scores - lse), 0.0).astype(jnp.bfloat16)
        prob_list.append(probs)
        lse_list.append(lse)
        mixed_list.append(
            jnp.dot(probs, values_all[:, lower : lower + HEAD], preferred_element_type=jnp.float32)
        )
    mixed = jnp.concatenate(mixed_list, axis=1).astype(jnp.bfloat16)
    updated = (
        states_single_float + jnp.dot(mixed, out_weight, preferred_element_type=jnp.float32)
    ).astype(jnp.bfloat16)
    partial_out = rows_product(mixed, grads_in)
    d_mixed = cols_product(grads_in, out_weight).astype(jnp.bfloat16)
    score_grads = []
    delta_list = []
    query_grads = []
    for head in range(HEADS):
        lower = head * HEAD
        mixed_head = d_mixed[:, lower : lower + HEAD]
        delta = jnp.sum(
            mixed_head.astype(jnp.float32) * mixed[:, lower : lower + HEAD].astype(jnp.float32),
            axis=1,
            keepdims=True,
        )
        d_probs = cols_product(mixed_head, values_all[:, lower : lower + HEAD])
        d_scores = (prob_list[head].astype(jnp.float32) * (d_probs - delta)).astype(jnp.bfloat16)
        score_grads.append(d_scores)
        delta_list.append(delta)
        query_grads.append(
            jnp.dot(d_scores, keys_all[:, lower : lower + HEAD], preferred_element_type=jnp.float32)
            * scale
        )
    d_queries = jnp.concatenate(query_grads, axis=1).astype(jnp.bfloat16)
    key_pieces = []
    value_pieces = []
    for head in range(HEADS):
        lower = head * HEAD
        score_part = score_grads[head]
        prob_part = prob_list[head]
        key_pieces.append(rows_product(score_part, queries[:, lower : lower + HEAD]) * scale)
        value_pieces.append(rows_product(prob_part, d_mixed[:, lower : lower + HEAD]))
    key_value_grads = lax.psum_scatter(
        jnp.concatenate(key_pieces + value_pieces, axis=1).astype(jnp.bfloat16),
        "node",
        scatter_dimension=0,
        tiled=True,
    ).astype(jnp.float32)
    d_keys = key_value_grads[:, :width].astype(jnp.bfloat16)
    d_values = key_value_grads[:, width:].astype(jnp.bfloat16)
    normalized_gradient = (
        cols_product(d_queries, query_weight)
        + cols_product(d_keys, key_weight)
        + cols_product(d_values, value_weight)
    )
    node_state_gradient = (
        grads_in.astype(jnp.float32)
        + inverse_norm_scale
        * (
            normalized_gradient
            - centered_states
            * jnp.mean(normalized_gradient * centered_states, axis=1, keepdims=True)
        )
    ).astype(jnp.bfloat16)
    partial_query = rows_product(normalized_states, d_queries)
    partial_key = rows_product(normalized_states, d_keys)
    partial_value = rows_product(normalized_states, d_values)
    total_query, total_key, total_value, total_out = lax.psum(
        (partial_query, partial_key, partial_value, partial_out), ("node", "rep")
    )
    return (
        updated[None],
        node_state_gradient[None],
        total_query,
        total_key,
        total_value,
        total_out,
    )

LANES = 128
SLOTS = 16
LEVEL_PARTS = 3
TILE_ROWS = 8
VMEM_LIMIT = 24 * 1024 * 1024


def transposed_product(left, right):
    return lax.dot_general(left, right, CONTRACT_ROWS, preferred_element_type=jnp.float32)


def pair_product(left, right):
    return lax.dot_general(left, right, CONTRACT_COLS, preferred_element_type=jnp.float32)


def plain_product(left, right):
    return jnp.dot(left, right, preferred_element_type=jnp.float32)


def head_lanes(rows, half):
    lanes = lax.broadcasted_iota(jnp.int32, (rows, LANES), 1)
    return (lanes >= HEAD) if half else (lanes < HEAD)


def keep_lanes(array, mask):
    return jnp.where(mask, array, jnp.zeros_like(array))


def split_heads(array):
    rows = array.shape[0]
    return jnp.concatenate(
        [keep_lanes(array, head_lanes(rows, 0)), keep_lanes(array, head_lanes(rows, 1))], axis=0
    )


def merge_heads(array):
    rows = array.shape[0] // 2
    return jnp.where(head_lanes(rows, 0), array[:rows], array[rows:])


def normalize(states):
    wide = states.astype(jnp.float32)
    inverse = lax.rsqrt(jnp.mean(wide * wide, axis=1, keepdims=True) + EPS)
    return wide, inverse, wide * inverse


def level_tables_whole(scalars, levels, total):
    columns = lax.broadcasted_iota(jnp.int32, (SLOTS, total), 1)
    places = columns.astype(jnp.float32)
    slots = lax.broadcasted_iota(jnp.int32, (SLOTS, total), 0)
    level = jnp.zeros((SLOTS, total), jnp.int32)
    for entry in range(1, levels):
        level += (places >= scalars[HEADS, entry]).astype(jnp.int32)
    features = jnp.concatenate(
        [
            (level == slots).astype(jnp.float32),
            ((columns >> 6) == slots).astype(jnp.float32),
        ],
        axis=0,
    ).astype(jnp.bfloat16)
    own = lax.broadcasted_iota(jnp.int32, (SLOTS, LANES), 0)
    lanes = lax.broadcasted_iota(jnp.int32, (SLOTS, LANES), 1)
    part = lanes >> 4
    distance = own - (lanes & (SLOTS - 1))
    tables = []
    for head in range(HEADS):
        table = jnp.full((SLOTS, LANES), NEG, jnp.float32)
        for step in range(1, min(levels, DIST)):
            table = jnp.where(distance == step, scalars[head, step], table)
        high = table.astype(jnp.bfloat16).astype(jnp.float32)
        middle = (table - high).astype(jnp.bfloat16).astype(jnp.float32)
        low = table - high - middle
        split = jnp.where(part == 0, high, jnp.where(part == 1, middle, low))
        tables.append(jnp.where(part < LEVEL_PARTS, split, 0.0))
    table = jnp.concatenate(tables, axis=1).astype(jnp.bfloat16)
    picks_row = lax.broadcasted_iota(jnp.int32, (2 * SLOTS, LANES), 0)
    picks_lane = lax.broadcasted_iota(jnp.int32, (2 * SLOTS, LANES), 1)
    wanted = jnp.where(
        picks_lane < LEVEL_PARTS * SLOTS,
        picks_lane & (SLOTS - 1),
        picks_lane - (LEVEL_PARTS - 1) * SLOTS,
    )
    picks = (wanted == picks_row).astype(jnp.float32).astype(jnp.bfloat16)
    return features, table, transposed_product(features, picks).astype(jnp.bfloat16)


def project(chunk, weights, unit_t, projected):
    unit = normalize(chunk[: projected.shape[0], :])[2]
    unit_t[...] = unit.T.astype(jnp.bfloat16)
    unit = unit.astype(jnp.bfloat16)
    width = projected.shape[1] // 3
    for i, weight in enumerate(weights):
        projected[:, i * width : (i + 1) * width] = plain_product(unit, weight[...]).astype(
            jnp.bfloat16
        )


def tables_kernel(levels, scalars, features, table, column_features):
    rows, level_bias, columns = level_tables_whole(scalars, levels, features.shape[1])
    features[...] = rows
    table[...] = level_bias
    column_features[...] = columns


def project_kernel(chunk, query_w, key_w, value_w, unit_t, projected):
    project(chunk, (query_w, key_w, value_w), unit_t, projected)


def forward_kernel(
    place, scalars, own_states, own_t, own, near_states, near_t, near,
    far_states, far_t, far, last_states, query_w, key_w, value_w, features, table, column_features,
    normed_t, projected, probs, mixed, mixed_t,
    row_table, key_table, last_t, last,
):
    total, width = mixed.shape
    rows = own.shape[0]
    scale = HEAD ** (-0.5)
    project(last_states, (query_w, key_w, value_w), last_t, last)
    chunks = ((own_t, own), (near_t, near), (far_t, far), (last_t, last))
    for index, (unit_t, chunk) in enumerate(chunks):
        at = pl.ds(pl.multiple_of((place[0] ^ index) * rows, rows), rows)
        normed_t[:, at] = unit_t[...]
        projected[at, :] = chunk[...]
    slots = lax.broadcasted_iota(jnp.int32, (SLOTS, HEADS * LANES), 0)
    hidden = jnp.zeros((SLOTS, HEADS * LANES), jnp.float32)
    for index, part in enumerate((own_states, near_states, far_states, last_states)):
        tile = part[rows:, :].astype(jnp.float32)
        for block in range(rows // BLOCK):
            at = (place[0] ^ index) * (rows // BLOCK) + block
            hidden = jnp.where(slots == at, tile[block : block + 1, :], hidden)
    row_table[...] = transposed_product(
        features[...], jnp.concatenate([table[...], hidden.astype(jnp.bfloat16)], axis=0)
    ).astype(jnp.bfloat16)
    for pair in range(HEADS // 2):
        key_table[pair, :, :LANES] = projected[:, width + pair * LANES : width + (pair + 1) * LANES]
        key_table[pair, :, LANES:] = column_features[...]
    same = lax.broadcasted_iota(jnp.int32, (2 * LANES, LANES), 1) == (
        lax.broadcasted_iota(jnp.int32, (2 * LANES, LANES), 0) & (LANES - 1)
    )
    first_half = lax.broadcasted_iota(jnp.int32, (2 * LANES, 1), 0) < LANES
    for pair in range(HEADS // 2):
        lanes = slice(pair * LANES, (pair + 1) * LANES)
        values = slice(2 * width + pair * LANES, 2 * width + (pair + 1) * LANES)
        self_bias = jnp.where(
            first_half, scalars[2 * pair, 0], scalars[2 * pair + 1, 0]
        )
        for tile in range(total // LANES):
            low, high = tile * LANES, (tile + 1) * LANES
            stacked = slice(2 * low, 2 * high)
            query = split_heads(projected[low:high, lanes] * jnp.asarray(scale, jnp.bfloat16))
            key = key_table[pair, low:high, :LANES].astype(jnp.float32)
            self_score = jnp.sum(
                query.astype(jnp.float32) * jnp.concatenate([key, key], axis=0),
                axis=1,
                keepdims=True,
            )
            rest = jnp.concatenate(
                [
                    row_table[low:high, (2 * pair) * LANES : (2 * pair + 1) * LANES],
                    row_table[low:high, (2 * pair + 1) * LANES : (2 * pair + 2) * LANES],
                ],
                axis=0,
            )
            scores = pair_product(
                jnp.concatenate([query, rest], axis=1), key_table[pair, :high, :]
            )
            corner = jnp.where(same, self_score + self_bias, scores[:, low:])
            peak = jnp.max(corner, axis=1, keepdims=True)
            if low:
                peak = jnp.maximum(peak, jnp.max(scores[:, :low], axis=1, keepdims=True))
            corner = jnp.exp(corner - peak)
            mass = jnp.sum(corner, axis=1, keepdims=True)
            if low:
                weight = jnp.exp(scores[:, :low] - peak)
                mass += jnp.sum(weight, axis=1, keepdims=True)
                inverse = 1.0 / mass
                probs[pair, stacked, :low] = (weight * inverse).astype(jnp.bfloat16)
            else:
                inverse = 1.0 / mass
            probs[pair, stacked, low:high] = (corner * inverse).astype(jnp.bfloat16)
            both = merge_heads(
                plain_product(probs[pair, stacked, :high], projected[:high, values])
            )
            mixed[low:high, lanes] = both.astype(jnp.bfloat16)
            mixed_t[lanes, low:high] = both.T.astype(jnp.bfloat16)


def product_halves(place, left, right, keep, send):
    half = keep.shape[0]
    mine = pl.ds(pl.multiple_of(place[1] * half, half), half)
    other = pl.ds(pl.multiple_of((1 - place[1]) * half, half), half)
    send[...] = plain_product(left[other, :], right).astype(jnp.bfloat16)
    keep[...] = plain_product(left[mine, :], right)


def mix_kernel(place, own, near, far, last, out_w, gathered, d_mixed):
    rows = own.shape[0]
    for index, chunk in enumerate((own, near, far, last)):
        at = pl.ds(pl.multiple_of((place[0] ^ index) * rows, rows), rows)
        gathered[at, :] = chunk[...]
    d_mixed[...] = pair_product(gathered[...], out_w[...]).astype(jnp.bfloat16)


def output_kernel(place, gathered, mixed_t, keep, send):
    product_halves(place, mixed_t, gathered[...], keep, send)


def backward_kernel(
    pair, place, normed_t, projected, probs, mixed, d_mixed,
    d_own, keep, send,
    grads, key_sum, value_sum,
):
    total, width = mixed.shape
    rows = d_own.shape[0]
    scale = HEAD ** (-0.5)
    lanes, key_lanes, value_lanes = (
        slice(i * width + pair * LANES, i * width + (pair + 1) * LANES) for i in range(3)
    )
    for tile in reversed(range(total // LANES)):
        low, high = tile * LANES, (tile + 1) * LANES
        query = split_heads(projected[low:high, lanes])
        mix_grad = split_heads(d_mixed[low:high, lanes])
        mix = mixed[low:high, lanes].astype(jnp.float32)
        delta = jnp.sum(
            mix_grad.astype(jnp.float32) * jnp.concatenate([mix, mix], axis=0),
            axis=1,
            keepdims=True,
        )
        prob = probs[pair, 2 * low : 2 * high, :high]
        d_probs = pair_product(mix_grad, projected[:high, value_lanes])
        score_grad = (prob.astype(jnp.float32) * (d_probs - delta)).astype(jnp.bfloat16)
        grads[low:high, :LANES] = (
            merge_heads(plain_product(score_grad, projected[:high, key_lanes])) * scale
        ).astype(jnp.bfloat16)
        key_term = transposed_product(score_grad, query)
        value_term = transposed_product(prob, mix_grad)
        if high == total:
            key_sum[...] = key_term
            value_sum[...] = value_term
        else:
            key_sum[:high, :] += key_term
            value_sum[:high, :] += value_term
    grads[:, LANES : 2 * LANES] = (key_sum[...] * scale).astype(jnp.bfloat16)
    grads[:, 2 * LANES :] = value_sum[...].astype(jnp.bfloat16)
    product_halves(place, normed_t, grads[...], keep, send)
    d_own[...] = grads[pl.ds(pl.multiple_of(place[0] * rows, rows), rows), :]


def rows_kernel(place, own, grads_in, mixed, query_w, key_w, value_w, out_w, *rest):
    *d_own, updated, gradient = rest
    rows = updated.shape[0]
    width = mixed.shape[1]
    states, inverse, unit = normalize(own[:rows, :])
    here = pl.ds(pl.multiple_of(place[0] * rows, rows), rows)
    updated[...] = (states + plain_product(mixed[here, :], out_w[...])).astype(jnp.bfloat16)
    inner = jnp.zeros(updated.shape, jnp.float32)
    for pair, piece in enumerate(d_own):
        lanes = slice(pair * LANES, (pair + 1) * LANES)
        for i, weight in enumerate((query_w, key_w, value_w)):
            inner += pair_product(piece[:, i * LANES : (i + 1) * LANES], weight[:, lanes])
    gradient[...] = (
        grads_in[...].astype(jnp.float32)
        + inverse * (inner - unit * jnp.mean(inner * unit, axis=1, keepdims=True))
    ).astype(jnp.bfloat16)


def join_kernel(place, *refs):
    mine, other = refs[0:3], refs[3:6]
    total_query, total_key, total_value, total_out = refs[6:]
    for pieces, slot in ((mine, place[1]), (other, 1 - place[1])):
        half = pieces[0].shape[0]
        total_out[pl.ds(pl.multiple_of(slot * half, half), half), :] = pieces[0][...].astype(
            jnp.float32
        )
        half = pieces[1].shape[0]
        at = pl.ds(pl.multiple_of(slot * half, half), half)
        for pair, piece in enumerate(pieces[1:]):
            for i, total in enumerate((total_query, total_key, total_value)):
                total[at, pair * LANES : (pair + 1) * LANES] = piece[
                    :, i * LANES : (i + 1) * LANES
                ].astype(jnp.float32)


def run(kernel, outs, smem, arrays, scratch=(), cost=0):
    out_shape = tuple(jax.ShapeDtypeStruct(shape, dtype) for shape, dtype in outs)
    return pl.pallas_call(
        kernel,
        out_shape=out_shape,
        in_specs=[pl.BlockSpec(memory_space=pltpu.SMEM)] * len(smem)
        + [pl.BlockSpec(memory_space=pltpu.VMEM)] * len(arrays),
        out_specs=tuple([pl.BlockSpec(memory_space=pltpu.VMEM)] * len(outs)),
        scratch_shapes=list(scratch),
        compiler_params=pltpu.CompilerParams(vmem_limit_bytes=VMEM_LIMIT),
        cost_estimate=pl.CostEstimate(
            flops=cost * 1000000000, bytes_accessed=0, transcendentals=0
        ),
    )(*smem, *arrays)


def swap(array, axis, flip):
    return lax.ppermute(array, axis, [(i, i ^ flip) for i in range(lax.axis_size(axis))])


def sum_over_chips(keep, send):
    local = (keep + swap(send, "rep", 1).astype(jnp.float32)).astype(jnp.bfloat16)
    across = swap(local, "rep", 2)
    return local, across


def on_device_whole(
    node_states,
    cotangent,
    reach_blocks,
    reach_count,
    level_start,
    query_weight,
    key_weight,
    value_weight,
    out_weight,
    bias_table,
):
    states = node_states[0]
    grads_in = cotangent[0]
    blocks = reach_blocks[0]
    counts = reach_count[0]
    starts = level_start[0]
    rows, model = states.shape
    width = query_weight.shape[1]
    total = rows * lax.axis_size("node")
    place = jnp.stack([lax.axis_index("node"), lax.axis_index("rep") & 1]).astype(jnp.int32)
    half = jnp.bfloat16
    wide = jnp.float32

    local_blocks = blocks.shape[0]
    shape = (local_blocks, blocks.shape[1], HEADS * LANES)
    kinds = (lax.broadcasted_iota(jnp.int32, shape, 2) & (LANES - 1)) - LEVEL_PARTS * SLOTS
    slots = lax.broadcasted_iota(jnp.int32, shape, 1)
    match = (blocks[:, :, None] == kinds) & (slots < counts[:, None, None])
    match |= (kinds < 0) | (kinds >= SLOTS)
    hidden = (1.0 - jnp.max(match.astype(wide), axis=1)) * NEG
    own = jnp.concatenate(
        [states, jnp.pad(hidden.astype(half), ((0, TILE_ROWS - local_blocks), (0, 0)))], axis=0
    )
    far = swap(own, "node", 2)
    near = swap(own, "node", 1)
    last = swap(far, "node", 1)
    grads_sent, near = lax.optimization_barrier((grads_in, near))
    grads_far = swap(grads_sent, "node", 2)
    grads_near = swap(grads_sent, "node", 1)
    scalars = jnp.pad(bias_table, ((0, HEADS), (0, LANES - DIST))) + jnp.pad(
        starts.astype(wide)[None, :], ((HEADS, HEADS - 1), (0, LANES - starts.shape[0]))
    )
    features, table, columns = run(
        functools.partial(tables_kernel, starts.shape[0] - 1),
        [
            ((2 * SLOTS, total), half),
            ((SLOTS, HEADS * LANES), half),
            ((total, LANES), half),
        ],
        [scalars],
        [],
        cost=10,
    )
    weights = [query_weight, key_weight, value_weight]
    table, *weights = lax.optimization_barrier((table, *weights))
    chunk_outs = [((model, rows), half), ((rows, 3 * width), half)]
    own_t, own_p = run(project_kernel, chunk_outs, [], [own, *weights])
    near_t, near_p = run(project_kernel, chunk_outs, [], [near, *weights])
    far_t, far_p = run(project_kernel, chunk_outs, [], [far, *weights])
    grads_far, own_p, near_p, far_p = lax.optimization_barrier((grads_far, own_p, near_p, far_p))
    grads_last = swap(grads_far, "node", 1)
    normed_t, projected, probs, mixed, mixed_t = run(
        forward_kernel,
        [
            ((model, total), half),
            ((total, 3 * width), half),
            ((HEADS // 2, 2 * total, total), half),
            ((total, width), half),
            ((width, total), half),
        ],
        [place, scalars],
        [
            own, own_t, own_p, near, near_t, near_p, far, far_t, far_p, last, *weights,
            features, table, columns,
        ],
        [
            pltpu.VMEM((total, HEADS * LANES), half),
            pltpu.VMEM((HEADS // 2, total, 2 * LANES), half),
            pltpu.VMEM((model, rows), half),
            pltpu.VMEM((rows, 3 * width), half),
        ],
        cost=5,
    )
    gathered, d_mixed = run(
        mix_kernel,
        [((total, model), half), ((total, width), half)],
        [place],
        [grads_in, grads_near, grads_far, grads_last, out_weight],
    )
    halves = []
    d_own = []
    for pair in range(HEADS // 2):
        if pair == 1:
            local, across = halves[0]
            gathered, keep = lax.optimization_barrier((gathered, keep))
            out_keep, out_send = run(
                output_kernel,
                [((width // 2, model), wide), ((width // 2, model), half)],
                [place],
                [gathered, mixed_t],
            )
            d_mixed, local, out_send = lax.optimization_barrier((d_mixed, local, out_send))
            halves[0] = (local, across)
        own_grads, keep, send = run(
            functools.partial(backward_kernel, pair),
            [
                ((rows, 3 * LANES), half),
                ((model // 2, 3 * LANES), wide),
                ((model // 2, 3 * LANES), half),
            ],
            [place],
            [normed_t, projected, probs, mixed, d_mixed],
            [
                pltpu.VMEM((total, 3 * LANES), half),
                pltpu.VMEM((total, LANES), wide),
                pltpu.VMEM((total, LANES), wide),
            ],
        )
        d_own.append(own_grads)
        halves.append(sum_over_chips(keep, send))
    halves.append(sum_over_chips(out_keep, out_send))
    d_own[-1], _ = lax.optimization_barrier((d_own[-1], halves[1][0]))
    updated, node_state_gradient = run(
        rows_kernel,
        [((rows, model), half)] * 2,
        [place],
        [own, grads_in, mixed, *weights, out_weight, *d_own],
    )
    first, node_state_gradient = lax.optimization_barrier((halves[0][1], node_state_gradient))
    halves[0] = (halves[0][0], first)
    mine = [
        (near_sum.astype(wide) + far_sum.astype(wide)).astype(half) for near_sum, far_sum in halves
    ]
    other = [swap(piece, "rep", 1) for piece in mine]
    total_query, total_key, total_value, total_out = run(
        join_kernel,
        [((model, width), wide)] * 3 + [((width, model), wide)],
        [place],
        [mine[-1], *mine[:-1], other[-1], *other[:-1]],
    )
    return (
        updated[None],
        node_state_gradient[None],
        total_query,
        total_key,
        total_value,
        total_out,
    )


def on_device(node_states, cotangent, reach_blocks, reach_count, level_start, *rest):
    nodes = lax.axis_size("node")
    total = node_states.shape[1] * nodes
    small = (
        nodes == 4
        and lax.axis_size("rep") == 4
        and node_states.shape[1] == LANES
        and total // BLOCK <= SLOTS
        and level_start.shape[1] - 1 <= SLOTS
    )
    path = on_device_whole if small else on_device_general
    return path(node_states, cotangent, reach_blocks, reach_count, level_start, *rest)


def solution(mesh):
    in_specs = (
        P(("groups", "rep"), "node", None),
        P(("groups", "rep"), "node", None),
        P(("groups", "rep"), "node", None),
        P(("groups", "rep"), "node"),
        P(("groups", "rep"), None),
        P(),
        P(),
        P(),
        P(),
        P(),
    )
    out_specs = (
        P(("groups", "rep"), "node", None),
        P(("groups", "rep"), "node", None),
        P("groups", None),
        P("groups", None),
        P("groups", None),
        P("groups", None),
    )
    return jax.shard_map(
        on_device, mesh=mesh, in_specs=in_specs, out_specs=out_specs, check_vma=False
    )
```

```python
import functools

import jax
import jax.numpy as jnp
from jax import lax
from jax.experimental import pallas as pl
from jax.experimental.pallas import tpu as pltpu
from jax.sharding import PartitionSpec as P

HEADS = 4
HEAD = 64
BLOCK = 64
DIST = 32


EPS = 1e-05
NEG = -1e30
HIGH = lax.Precision.HIGHEST
CONTRACT_ROWS = (((0,), (0,)), ((), ()))
CONTRACT_COLS = (((1,), (1,)), ((), ()))


def rows_product(left, right):
    return lax.dot_general(left, right, CONTRACT_ROWS, preferred_element_type=jnp.float32)


def cols_product(left, right):
    return lax.dot_general(left, right, CONTRACT_COLS, preferred_element_type=jnp.float32)


def expand(listed):
    return jnp.repeat(jnp.repeat(listed, BLOCK, axis=0), BLOCK, axis=1)


def level_tables(starts, total, bias_table):
    level_count = starts.shape[0] - 1
    places = jnp.arange(total, dtype=jnp.int32)
    inner = starts[1:level_count]
    levels = jnp.sum((places[:, None] >= inner[None, :]).astype(jnp.int32), axis=1)
    marks = jnp.arange(level_count, dtype=jnp.int32)
    onehot = (levels[:, None] == marks[None, :]).astype(jnp.float32)
    spread = jnp.clip(marks[:, None] - marks[None, :], 0, DIST - 1)
    picks = (spread[:, :, None] == jnp.arange(DIST, dtype=jnp.int32)[None, None, :]).astype(
        jnp.float32
    )
    level_bias = jnp.einsum("hd,abd->hab", bias_table, picks, precision=HIGH)
    return (levels, onehot, level_bias)


def bias_block(row_onehot, head_bias, col_onehot):
    row_part = jnp.dot(row_onehot, head_bias, precision=HIGH)
    return lax.dot_general(row_part, col_onehot, CONTRACT_COLS, precision=HIGH)


def on_device_general(
    node_states,
    cotangent,
    reach_blocks,
    reach_count,
    level_start,
    query_weight,
    key_weight,
    value_weight,
    out_weight,
    bias_table,
):
    states = node_states[0]
    grads_in = cotangent[0]
    blocks = reach_blocks[0]
    counts = reach_count[0]
    starts = level_start[0]
    rows_dev = states.shape[0]
    width = query_weight.shape[1]
    total = rows_dev * lax.axis_size("node")
    offset = lax.axis_index("node") * rows_dev
    scale = HEAD ** (-0.5)
    key_blocks = total // BLOCK
    states_single_float = states.astype(jnp.float32)
    inverse_norm_scale = lax.rsqrt(
        jnp.mean(states_single_float * states_single_float, axis=1, keepdims=True) + EPS
    )
    centered_states = states_single_float * inverse_norm_scale
    normalized_states = centered_states.astype(jnp.bfloat16)
    queries = jnp.dot(normalized_states, query_weight, preferred_element_type=jnp.float32).astype(
        jnp.bfloat16
    )
    keys = jnp.dot(normalized_states, key_weight, preferred_element_type=jnp.float32).astype(
        jnp.bfloat16
    )
    values = jnp.dot(normalized_states, value_weight, preferred_element_type=jnp.float32).astype(
        jnp.bfloat16
    )
    keys_all, values_all = (
        lax.all_gather(keys, "node", axis=0, tiled=True),
        lax.all_gather(values, "node", axis=0, tiled=True),
    )
    levels, onehot, level_bias = level_tables(starts, total, bias_table)
    positions = jnp.arange(total, dtype=jnp.int32)
    local = jnp.arange(rows_dev, dtype=jnp.int32)
    row_ids = offset + local
    row_levels = lax.dynamic_slice_in_dim(levels, offset, rows_dev, 0)
    row_onehot = lax.dynamic_slice_in_dim(onehot, offset, rows_dev, 0)
    slots = jnp.arange(blocks.shape[1], dtype=jnp.int32)
    live = slots[None, :] < counts[:, None]
    kinds = jnp.arange(key_blocks, dtype=jnp.int32)
    listed = jnp.any((blocks[:, :, None] == kinds[None, None, :]) & live[:, :, None], axis=1)
    visible = expand(listed) & (
        (levels[None, :] < row_levels[:, None]) | (positions[None, :] == row_ids[:, None])
    )
    prob_list = []
    lse_list = []
    mixed_list = []
    for head in range(HEADS):
        lower = head * HEAD
        scores = (
            cols_product(queries[:, lower : lower + HEAD], keys_all[:, lower : lower + HEAD])
            * scale
        )
        scores = scores + bias_block(row_onehot, level_bias[head], onehot)
        scores = jnp.where(visible, scores, NEG)
        peak = jnp.max(scores, axis=1, keepdims=True)
        mass = jnp.sum(jnp.where(visible, jnp.exp(scores - peak), 0.0), axis=1, keepdims=True)
        lse = peak + jnp.log(mass)
        probs = jnp.where(visible, jnp.exp(scores - lse), 0.0).astype(jnp.bfloat16)
        prob_list.append(probs)
        lse_list.append(lse)
        mixed_list.append(
            jnp.dot(probs, values_all[:, lower : lower + HEAD], preferred_element_type=jnp.float32)
        )
    mixed = jnp.concatenate(mixed_list, axis=1).astype(jnp.bfloat16)
    updated = (
        states_single_float + jnp.dot(mixed, out_weight, preferred_element_type=jnp.float32)
    ).astype(jnp.bfloat16)
    partial_out = rows_product(mixed, grads_in)
    d_mixed = cols_product(grads_in, out_weight).astype(jnp.bfloat16)
    score_grads = []
    delta_list = []
    query_grads = []
    for head in range(HEADS):
        lower = head * HEAD
        mixed_head = d_mixed[:, lower : lower + HEAD]
        delta = jnp.sum(
            mixed_head.astype(jnp.float32) * mixed[:, lower : lower + HEAD].astype(jnp.float32),
            axis=1,
            keepdims=True,
        )
        d_probs = cols_product(mixed_head, values_all[:, lower : lower + HEAD])
        d_scores = (prob_list[head].astype(jnp.float32) * (d_probs - delta)).astype(jnp.bfloat16)
        score_grads.append(d_scores)
        delta_list.append(delta)
        query_grads.append(
            jnp.dot(d_scores, keys_all[:, lower : lower + HEAD], preferred_element_type=jnp.float32)
            * scale
        )
    d_queries = jnp.concatenate(query_grads, axis=1).astype(jnp.bfloat16)
    key_pieces = []
    value_pieces = []
    for head in range(HEADS):
        lower = head * HEAD
        score_part = score_grads[head]
        prob_part = prob_list[head]
        key_pieces.append(rows_product(score_part, queries[:, lower : lower + HEAD]) * scale)
        value_pieces.append(rows_product(prob_part, d_mixed[:, lower : lower + HEAD]))
    key_value_grads = lax.psum_scatter(
        jnp.concatenate(key_pieces + value_pieces, axis=1).astype(jnp.bfloat16),
        "node",
        scatter_dimension=0,
        tiled=True,
    ).astype(jnp.float32)
    d_keys = key_value_grads[:, :width].astype(jnp.bfloat16)
    d_values = key_value_grads[:, width:].astype(jnp.bfloat16)
    normalized_gradient = (
        cols_product(d_queries, query_weight)
        + cols_product(d_keys, key_weight)
        + cols_product(d_values, value_weight)
    )
    node_state_gradient = (
        grads_in.astype(jnp.float32)
        + inverse_norm_scale
        * (
            normalized_gradient
            - centered_states
            * jnp.mean(normalized_gradient * centered_states, axis=1, keepdims=True)
        )
    ).astype(jnp.bfloat16)
    partial_query = rows_product(normalized_states, d_queries)
    partial_key = rows_product(normalized_states, d_keys)
    partial_value = rows_product(normalized_states, d_values)
    total_query, total_key, total_value, total_out = lax.psum(
        (partial_query, partial_key, partial_value, partial_out), ("node", "rep")
    )
    return (
        updated[None],
        node_state_gradient[None],
        total_query,
        total_key,
        total_value,
        total_out,
    )

LANES = 128
SLOTS = 16
LEVEL_PARTS = 3
TILE_ROWS = 8
VMEM_LIMIT = 24 * 1024 * 1024


def transposed_product(left, right):
    return lax.dot_general(left, right, CONTRACT_ROWS, preferred_element_type=jnp.float32)


def pair_product(left, right):
    return lax.dot_general(left, right, CONTRACT_COLS, preferred_element_type=jnp.float32)


def plain_product(left, right):
    return jnp.dot(left, right, preferred_element_type=jnp.float32)


def head_lanes(rows, half):
    lanes = lax.broadcasted_iota(jnp.int32, (rows, LANES), 1)
    return (lanes >= HEAD) if half else (lanes < HEAD)


def keep_lanes(array, mask):
    return jnp.where(mask, array, jnp.zeros_like(array))


def split_heads(array):
    rows = array.shape[0]
    return jnp.concatenate(
        [keep_lanes(array, head_lanes(rows, 0)), keep_lanes(array, head_lanes(rows, 1))], axis=0
    )


def merge_heads(array):
    rows = array.shape[0] // 2
    return jnp.where(head_lanes(rows, 0), array[:rows], array[rows:])


def normalize(states):
    wide = states.astype(jnp.float32)
    inverse = lax.rsqrt(jnp.mean(wide * wide, axis=1, keepdims=True) + EPS)
    return wide, inverse, wide * inverse


def level_tables_whole(scalars, levels, total):
    columns = lax.broadcasted_iota(jnp.int32, (SLOTS, total), 1)
    places = columns.astype(jnp.float32)
    slots = lax.broadcasted_iota(jnp.int32, (SLOTS, total), 0)
    level = jnp.zeros((SLOTS, total), jnp.int32)
    for entry in range(1, levels):
        level += (places >= scalars[HEADS, entry]).astype(jnp.int32)
    features = jnp.concatenate(
        [
            (level == slots).astype(jnp.float32),
            ((columns >> 6) == slots).astype(jnp.float32),
        ],
        axis=0,
    ).astype(jnp.bfloat16)
    own = lax.broadcasted_iota(jnp.int32, (SLOTS, LANES), 0)
    lanes = lax.broadcasted_iota(jnp.int32, (SLOTS, LANES), 1)
    part = lanes >> 4
    distance = own - (lanes & (SLOTS - 1))
    tables = []
    for head in range(HEADS):
        table = jnp.full((SLOTS, LANES), NEG, jnp.float32)
        for step in range(1, min(levels, DIST)):
            table = jnp.where(distance == step, scalars[head, step], table)
        high = table.astype(jnp.bfloat16).astype(jnp.float32)
        middle = (table - high).astype(jnp.bfloat16).astype(jnp.float32)
        low = table - high - middle
        split = jnp.where(part == 0, high, jnp.where(part == 1, middle, low))
        tables.append(jnp.where(part < LEVEL_PARTS, split, 0.0))
    table = jnp.concatenate(tables, axis=1).astype(jnp.bfloat16)
    picks_row = lax.broadcasted_iota(jnp.int32, (2 * SLOTS, LANES), 0)
    picks_lane = lax.broadcasted_iota(jnp.int32, (2 * SLOTS, LANES), 1)
    wanted = jnp.where(
        picks_lane < LEVEL_PARTS * SLOTS,
        picks_lane & (SLOTS - 1),
        picks_lane - (LEVEL_PARTS - 1) * SLOTS,
    )
    picks = (wanted == picks_row).astype(jnp.float32).astype(jnp.bfloat16)
    return features, table, transposed_product(features, picks).astype(jnp.bfloat16)


def project(chunk, weights, unit_t, projected):
    unit = normalize(chunk[: projected.shape[0], :])[2]
    unit_t[...] = unit.T.astype(jnp.bfloat16)
    unit = unit.astype(jnp.bfloat16)
    width = projected.shape[1] // 3
    for i, weight in enumerate(weights):
        projected[:, i * width : (i + 1) * width] = plain_product(unit, weight[...]).astype(
            jnp.bfloat16
        )


def tables_kernel(levels, scalars, features, table, column_features):
    rows, level_bias, columns = level_tables_whole(scalars, levels, features.shape[1])
    features[...] = rows
    table[...] = level_bias
    column_features[...] = columns


def project_kernel(chunk, query_w, key_w, value_w, unit_t, projected):
    project(chunk, (query_w, key_w, value_w), unit_t, projected)


def forward_kernel(
    place, scalars, own_states, own_t, own, near_states, near_t, near,
    far_states, far_t, far, last_states, query_w, key_w, value_w, features, table, column_features,
    normed_t, projected, probs, mixed, mixed_t,
    row_table, key_table, last_t, last,
):
    total, width = mixed.shape
    rows = own.shape[0]
    scale = HEAD ** (-0.5)
    project(last_states, (query_w, key_w, value_w), last_t, last)
    chunks = ((own_t, own), (near_t, near), (far_t, far), (last_t, last))
    for index, (unit_t, chunk) in enumerate(chunks):
        at = pl.ds(pl.multiple_of((place[0] ^ index) * rows, rows), rows)
        normed_t[:, at] = unit_t[...]
        projected[at, :] = chunk[...]
    slots = lax.broadcasted_iota(jnp.int32, (SLOTS, HEADS * LANES), 0)
    hidden = jnp.zeros((SLOTS, HEADS * LANES), jnp.float32)
    for index, part in enumerate((own_states, near_states, far_states, last_states)):
        tile = part[rows:, :].astype(jnp.float32)
        for block in range(rows // BLOCK):
            at = (place[0] ^ index) * (rows // BLOCK) + block
            hidden = jnp.where(slots == at, tile[block : block + 1, :], hidden)
    row_table[...] = transposed_product(
        features[...], jnp.concatenate([table[...], hidden.astype(jnp.bfloat16)], axis=0)
    ).astype(jnp.bfloat16)
    for pair in range(HEADS // 2):
        key_table[pair, :, :LANES] = projected[:, width + pair * LANES : width + (pair + 1) * LANES]
        key_table[pair, :, LANES:] = column_features[...]
    same = lax.broadcasted_iota(jnp.int32, (2 * LANES, LANES), 1) == (
        lax.broadcasted_iota(jnp.int32, (2 * LANES, LANES), 0) & (LANES - 1)
    )
    first_half = lax.broadcasted_iota(jnp.int32, (2 * LANES, 1), 0) < LANES
    for pair in range(HEADS // 2):
        lanes = slice(pair * LANES, (pair + 1) * LANES)
        values = slice(2 * width + pair * LANES, 2 * width + (pair + 1) * LANES)
        self_bias = jnp.where(
            first_half, scalars[2 * pair, 0], scalars[2 * pair + 1, 0]
        )
        for tile in range(total // LANES):
            low, high = tile * LANES, (tile + 1) * LANES
            stacked = slice(2 * low, 2 * high)
            query = split_heads(projected[low:high, lanes] * jnp.asarray(scale, jnp.bfloat16))
            key = key_table[pair, low:high, :LANES].astype(jnp.float32)
            self_score = jnp.sum(
                query.astype(jnp.float32) * jnp.concatenate([key, key], axis=0),
                axis=1,
                keepdims=True,
            )
            rest = jnp.concatenate(
                [
                    row_table[low:high, (2 * pair) * LANES : (2 * pair + 1) * LANES],
                    row_table[low:high, (2 * pair + 1) * LANES : (2 * pair + 2) * LANES],
                ],
                axis=0,
            )
            scores = pair_product(
                jnp.concatenate([query, rest], axis=1), key_table[pair, :high, :]
            )
            corner = jnp.where(same, self_score + self_bias, scores[:, low:])
            peak = jnp.max(corner, axis=1, keepdims=True)
            if low:
                peak = jnp.maximum(peak, jnp.max(scores[:, :low], axis=1, keepdims=True))
            corner = jnp.exp(corner - peak)
            mass = jnp.sum(corner, axis=1, keepdims=True)
            if low:
                weight = jnp.exp(scores[:, :low] - peak)
                mass += jnp.sum(weight, axis=1, keepdims=True)
                inverse = 1.0 / mass
                probs[pair, stacked, :low] = (weight * inverse).astype(jnp.bfloat16)
            else:
                inverse = 1.0 / mass
            probs[pair, stacked, low:high] = (corner * inverse).astype(jnp.bfloat16)
            both = merge_heads(
                plain_product(probs[pair, stacked, :high], projected[:high, values])
            )
            mixed[low:high, lanes] = both.astype(jnp.bfloat16)
            mixed_t[lanes, low:high] = both.T.astype(jnp.bfloat16)


def product_halves(place, left, right, keep, send):
    half = keep.shape[0]
    mine = pl.ds(pl.multiple_of(place[1] * half, half), half)
    other = pl.ds(pl.multiple_of((1 - place[1]) * half, half), half)
    send[...] = plain_product(left[other, :], right).astype(jnp.bfloat16)
    keep[...] = plain_product(left[mine, :], right)


def mix_kernel(place, own, near, far, last, out_w, gathered, d_mixed):
    rows = own.shape[0]
    for index, chunk in enumerate((own, near, far, last)):
        at = pl.ds(pl.multiple_of((place[0] ^ index) * rows, rows), rows)
        gathered[at, :] = chunk[...]
    d_mixed[...] = pair_product(gathered[...], out_w[...]).astype(jnp.bfloat16)


def output_kernel(place, gathered, mixed_t, keep, send):
    product_halves(place, mixed_t, gathered[...], keep, send)


def backward_kernel(
    pair, place, normed_t, projected, probs, mixed, d_mixed,
    d_own, keep, send,
    grads, key_sum, value_sum,
):
    total, width = mixed.shape
    rows = d_own.shape[0]
    scale = HEAD ** (-0.5)
    lanes, key_lanes, value_lanes = (
        slice(i * width + pair * LANES, i * width + (pair + 1) * LANES) for i in range(3)
    )
    for tile in reversed(range(total // LANES)):
        low, high = tile * LANES, (tile + 1) * LANES
        query = split_heads(projected[low:high, lanes])
        mix_grad = split_heads(d_mixed[low:high, lanes])
        mix = mixed[low:high, lanes].astype(jnp.float32)
        delta = jnp.sum(
            mix_grad.astype(jnp.float32) * jnp.concatenate([mix, mix], axis=0),
            axis=1,
            keepdims=True,
        )
        prob = probs[pair, 2 * low : 2 * high, :high]
        d_probs = pair_product(mix_grad, projected[:high, value_lanes])
        score_grad = (prob.astype(jnp.float32) * (d_probs - delta)).astype(jnp.bfloat16)
        grads[low:high, :LANES] = (
            merge_heads(plain_product(score_grad, projected[:high, key_lanes])) * scale
        ).astype(jnp.bfloat16)
        key_term = transposed_product(score_grad, query)
        value_term = transposed_product(prob, mix_grad)
        if high == total:
            key_sum[...] = key_term
            value_sum[...] = value_term
        else:
            key_sum[:high, :] += key_term
            value_sum[:high, :] += value_term
    grads[:, LANES : 2 * LANES] = (key_sum[...] * scale).astype(jnp.bfloat16)
    grads[:, 2 * LANES :] = value_sum[...].astype(jnp.bfloat16)
    product_halves(place, normed_t, grads[...], keep, send)
    d_own[...] = grads[pl.ds(pl.multiple_of(place[0] * rows, rows), rows), :]


def rows_kernel(place, own, grads_in, mixed, query_w, key_w, value_w, out_w, *rest):
    *d_own, updated, gradient = rest
    rows = updated.shape[0]
    width = mixed.shape[1]
    states, inverse, unit = normalize(own[:rows, :])
    here = pl.ds(pl.multiple_of(place[0] * rows, rows), rows)
    updated[...] = (states + plain_product(mixed[here, :], out_w[...])).astype(jnp.bfloat16)
    inner = jnp.zeros(updated.shape, jnp.float32)
    for pair, piece in enumerate(d_own):
        lanes = slice(pair * LANES, (pair + 1) * LANES)
        for i, weight in enumerate((query_w, key_w, value_w)):
            inner += pair_product(piece[:, i * LANES : (i + 1) * LANES], weight[:, lanes])
    gradient[...] = (
        grads_in[...].astype(jnp.float32)
        + inverse * (inner - unit * jnp.mean(inner * unit, axis=1, keepdims=True))
    ).astype(jnp.bfloat16)


def join_kernel(place, *refs):
    mine, other = refs[0:3], refs[3:6]
    total_query, total_key, total_value, total_out = refs[6:]
    for pieces, slot in ((mine, place[1]), (other, 1 - place[1])):
        half = pieces[0].shape[0]
        total_out[pl.ds(pl.multiple_of(slot * half, half), half), :] = pieces[0][...].astype(
            jnp.float32
        )
        half = pieces[1].shape[0]
        at = pl.ds(pl.multiple_of(slot * half, half), half)
        for pair, piece in enumerate(pieces[1:]):
            for i, total in enumerate((total_query, total_key, total_value)):
                total[at, pair * LANES : (pair + 1) * LANES] = piece[
                    :, i * LANES : (i + 1) * LANES
                ].astype(jnp.float32)


def run(kernel, outs, smem, arrays, scratch=(), cost=0):
    out_shape = tuple(jax.ShapeDtypeStruct(shape, dtype) for shape, dtype in outs)
    return pl.pallas_call(
        kernel,
        out_shape=out_shape,
        in_specs=[pl.BlockSpec(memory_space=pltpu.SMEM)] * len(smem)
        + [pl.BlockSpec(memory_space=pltpu.VMEM)] * len(arrays),
        out_specs=tuple([pl.BlockSpec(memory_space=pltpu.VMEM)] * len(outs)),
        scratch_shapes=list(scratch),
        compiler_params=pltpu.CompilerParams(vmem_limit_bytes=VMEM_LIMIT),
        cost_estimate=pl.CostEstimate(
            flops=cost * 1000000000, bytes_accessed=0, transcendentals=0
        ),
    )(*smem, *arrays)


def swap(array, axis, flip):
    return lax.ppermute(array, axis, [(i, i ^ flip) for i in range(lax.axis_size(axis))])


def sum_over_chips(keep, send):
    local = (keep + swap(send, "rep", 1).astype(jnp.float32)).astype(jnp.bfloat16)
    across = swap(local, "rep", 2)
    return local, across


def on_device_whole(
    node_states,
    cotangent,
    reach_blocks,
    reach_count,
    level_start,
    query_weight,
    key_weight,
    value_weight,
    out_weight,
    bias_table,
):
    states = node_states[0]
    grads_in = cotangent[0]
    blocks = reach_blocks[0]
    counts = reach_count[0]
    starts = level_start[0]
    rows, model = states.shape
    width = query_weight.shape[1]
    total = rows * lax.axis_size("node")
    place = jnp.stack([lax.axis_index("node"), lax.axis_index("rep") & 1]).astype(jnp.int32)
    half = jnp.bfloat16
    wide = jnp.float32

    local_blocks = blocks.shape[0]
    shape = (local_blocks, blocks.shape[1], HEADS * LANES)
    kinds = (lax.broadcasted_iota(jnp.int32, shape, 2) & (LANES - 1)) - LEVEL_PARTS * SLOTS
    slots = lax.broadcasted_iota(jnp.int32, shape, 1)
    match = (blocks[:, :, None] == kinds) & (slots < counts[:, None, None])
    match |= (kinds < 0) | (kinds >= SLOTS)
    hidden = (1.0 - jnp.max(match.astype(wide), axis=1)) * NEG
    own = jnp.concatenate(
        [states, jnp.pad(hidden.astype(half), ((0, TILE_ROWS - local_blocks), (0, 0)))], axis=0
    )
    far = swap(own, "node", 2)
    near = swap(own, "node", 1)
    last = swap(far, "node", 1)
    grads_near = swap(grads_in, "node", 1)
    grads_sent, near = lax.optimization_barrier((grads_in, near))
    grads_far = swap(grads_sent, "node", 2)
    scalars = jnp.pad(bias_table, ((0, HEADS), (0, LANES - DIST))) + jnp.pad(
        starts.astype(wide)[None, :], ((HEADS, HEADS - 1), (0, LANES - starts.shape[0]))
    )
    features, table, columns = run(
        functools.partial(tables_kernel, starts.shape[0] - 1),
        [
            ((2 * SLOTS, total), half),
            ((SLOTS, HEADS * LANES), half),
            ((total, LANES), half),
        ],
        [scalars],
        [],
        cost=10,
    )
    weights = [query_weight, key_weight, value_weight]
    table, *weights = lax.optimization_barrier((table, *weights))
    chunk_outs = [((model, rows), half), ((rows, 3 * width), half)]
    own_t, own_p = run(project_kernel, chunk_outs, [], [own, *weights])
    near_t, near_p = run(project_kernel, chunk_outs, [], [near, *weights])
    far_t, far_p = run(project_kernel, chunk_outs, [], [far, *weights])
    grads_far, own_p, near_p, far_p = lax.optimization_barrier((grads_far, own_p, near_p, far_p))
    grads_last = swap(grads_far, "node", 1)
    normed_t, projected, probs, mixed, mixed_t = run(
        forward_kernel,
        [
            ((model, total), half),
            ((total, 3 * width), half),
            ((HEADS // 2, 2 * total, total), half),
            ((total, width), half),
            ((width, total), half),
        ],
        [place, scalars],
        [
            own, own_t, own_p, near, near_t, near_p, far, far_t, far_p, last, *weights,
            features, table, columns,
        ],
        [
            pltpu.VMEM((total, HEADS * LANES), half),
            pltpu.VMEM((HEADS // 2, total, 2 * LANES), half),
            pltpu.VMEM((model, rows), half),
            pltpu.VMEM((rows, 3 * width), half),
        ],
        cost=5,
    )
    gathered, d_mixed = run(
        mix_kernel,
        [((total, model), half), ((total, width), half)],
        [place],
        [grads_in, grads_near, grads_far, grads_last, out_weight],
    )
    halves = []
    d_own = []
    for pair in range(HEADS // 2):
        if pair == 1:
            local, across = halves[0]
            gathered, keep = lax.optimization_barrier((gathered, keep))
            out_keep, out_send = run(
                output_kernel,
                [((width // 2, model), wide), ((width // 2, model), half)],
                [place],
                [gathered, mixed_t],
            )
            d_mixed, local, out_send = lax.optimization_barrier((d_mixed, local, out_send))
            halves[0] = (local, across)
        own_grads, keep, send = run(
            functools.partial(backward_kernel, pair),
            [
                ((rows, 3 * LANES), half),
                ((model // 2, 3 * LANES), wide),
                ((model // 2, 3 * LANES), half),
            ],
            [place],
            [normed_t, projected, probs, mixed, d_mixed],
            [
                pltpu.VMEM((total, 3 * LANES), half),
                pltpu.VMEM((total, LANES), wide),
                pltpu.VMEM((total, LANES), wide),
            ],
        )
        d_own.append(own_grads)
        halves.append(sum_over_chips(keep, send))
    halves.append(sum_over_chips(out_keep, out_send))
    d_own[-1], _ = lax.optimization_barrier((d_own[-1], halves[1][0]))
    updated, node_state_gradient = run(
        rows_kernel,
        [((rows, model), half)] * 2,
        [place],
        [own, grads_in, mixed, *weights, out_weight, *d_own],
    )
    first, node_state_gradient = lax.optimization_barrier((halves[0][1], node_state_gradient))
    halves[0] = (halves[0][0], first)
    mine = [
        (near_sum.astype(wide) + far_sum.astype(wide)).astype(half) for near_sum, far_sum in halves
    ]
    other = [swap(piece, "rep", 1) for piece in mine]
    total_query, total_key, total_value, total_out = run(
        join_kernel,
        [((model, width), wide)] * 3 + [((width, model), wide)],
        [place],
        [mine[-1], *mine[:-1], other[-1], *other[:-1]],
    )
    return (
        updated[None],
        node_state_gradient[None],
        total_query,
        total_key,
        total_value,
        total_out,
    )


def on_device(node_states, cotangent, reach_blocks, reach_count, level_start, *rest):
    nodes = lax.axis_size("node")
    total = node_states.shape[1] * nodes
    small = (
        nodes == 4
        and lax.axis_size("rep") == 4
        and node_states.shape[1] == LANES
        and total // BLOCK <= SLOTS
        and level_start.shape[1] - 1 <= SLOTS
    )
    path = on_device_whole if small else on_device_general
    return path(node_states, cotangent, reach_blocks, reach_count, level_start, *rest)


def solution(mesh):
    in_specs = (
        P(("groups", "rep"), "node", None),
        P(("groups", "rep"), "node", None),
        P(("groups", "rep"), "node", None),
        P(("groups", "rep"), "node"),
        P(("groups", "rep"), None),
        P(),
        P(),
        P(),
        P(),
        P(),
    )
    out_specs = (
        P(("groups", "rep"), "node", None),
        P(("groups", "rep"), "node", None),
        P("groups", None),
        P("groups", None),
        P("groups", None),
        P("groups", None),
    )
    return jax.shard_map(
        on_device, mesh=mesh, in_specs=in_specs, out_specs=out_specs, check_vma=False
    )
```

```python
import functools

import jax
import jax.numpy as jnp
from jax import lax
from jax.experimental import pallas as pl
from jax.experimental.pallas import tpu as pltpu
from jax.sharding import PartitionSpec as P

HEADS = 4
HEAD = 64
BLOCK = 64
DIST = 32


EPS = 1e-05
NEG = -1e30
HIGH = lax.Precision.HIGHEST
CONTRACT_ROWS = (((0,), (0,)), ((), ()))
CONTRACT_COLS = (((1,), (1,)), ((), ()))


def rows_product(left, right):
    return lax.dot_general(left, right, CONTRACT_ROWS, preferred_element_type=jnp.float32)


def cols_product(left, right):
    return lax.dot_general(left, right, CONTRACT_COLS, preferred_element_type=jnp.float32)


def expand(listed):
    return jnp.repeat(jnp.repeat(listed, BLOCK, axis=0), BLOCK, axis=1)


def level_tables(starts, total, bias_table):
    level_count = starts.shape[0] - 1
    places = jnp.arange(total, dtype=jnp.int32)
    inner = starts[1:level_count]
    levels = jnp.sum((places[:, None] >= inner[None, :]).astype(jnp.int32), axis=1)
    marks = jnp.arange(level_count, dtype=jnp.int32)
    onehot = (levels[:, None] == marks[None, :]).astype(jnp.float32)
    spread = jnp.clip(marks[:, None] - marks[None, :], 0, DIST - 1)
    picks = (spread[:, :, None] == jnp.arange(DIST, dtype=jnp.int32)[None, None, :]).astype(
        jnp.float32
    )
    level_bias = jnp.einsum("hd,abd->hab", bias_table, picks, precision=HIGH)
    return (levels, onehot, level_bias)


def bias_block(row_onehot, head_bias, col_onehot):
    row_part = jnp.dot(row_onehot, head_bias, precision=HIGH)
    return lax.dot_general(row_part, col_onehot, CONTRACT_COLS, precision=HIGH)


def on_device_general(
    node_states,
    cotangent,
    reach_blocks,
    reach_count,
    level_start,
    query_weight,
    key_weight,
    value_weight,
    out_weight,
    bias_table,
):
    states = node_states[0]
    grads_in = cotangent[0]
    blocks = reach_blocks[0]
    counts = reach_count[0]
    starts = level_start[0]
    rows_dev = states.shape[0]
    width = query_weight.shape[1]
    total = rows_dev * lax.axis_size("node")
    offset = lax.axis_index("node") * rows_dev
    scale = HEAD ** (-0.5)
    key_blocks = total // BLOCK
    states_single_float = states.astype(jnp.float32)
    inverse_norm_scale = lax.rsqrt(
        jnp.mean(states_single_float * states_single_float, axis=1, keepdims=True) + EPS
    )
    centered_states = states_single_float * inverse_norm_scale
    normalized_states = centered_states.astype(jnp.bfloat16)
    queries = jnp.dot(normalized_states, query_weight, preferred_element_type=jnp.float32).astype(
        jnp.bfloat16
    )
    keys = jnp.dot(normalized_states, key_weight, preferred_element_type=jnp.float32).astype(
        jnp.bfloat16
    )
    values = jnp.dot(normalized_states, value_weight, preferred_element_type=jnp.float32).astype(
        jnp.bfloat16
    )
    keys_all, values_all = (
        lax.all_gather(keys, "node", axis=0, tiled=True),
        lax.all_gather(values, "node", axis=0, tiled=True),
    )
    levels, onehot, level_bias = level_tables(starts, total, bias_table)
    positions = jnp.arange(total, dtype=jnp.int32)
    local = jnp.arange(rows_dev, dtype=jnp.int32)
    row_ids = offset + local
    row_levels = lax.dynamic_slice_in_dim(levels, offset, rows_dev, 0)
    row_onehot = lax.dynamic_slice_in_dim(onehot, offset, rows_dev, 0)
    slots = jnp.arange(blocks.shape[1], dtype=jnp.int32)
    live = slots[None, :] < counts[:, None]
    kinds = jnp.arange(key_blocks, dtype=jnp.int32)
    listed = jnp.any((blocks[:, :, None] == kinds[None, None, :]) & live[:, :, None], axis=1)
    visible = expand(listed) & (
        (levels[None, :] < row_levels[:, None]) | (positions[None, :] == row_ids[:, None])
    )
    prob_list = []
    lse_list = []
    mixed_list = []
    for head in range(HEADS):
        lower = head * HEAD
        scores = (
            cols_product(queries[:, lower : lower + HEAD], keys_all[:, lower : lower + HEAD])
            * scale
        )
        scores = scores + bias_block(row_onehot, level_bias[head], onehot)
        scores = jnp.where(visible, scores, NEG)
        peak = jnp.max(scores, axis=1, keepdims=True)
        mass = jnp.sum(jnp.where(visible, jnp.exp(scores - peak), 0.0), axis=1, keepdims=True)
        lse = peak + jnp.log(mass)
        probs = jnp.where(visible, jnp.exp(scores - lse), 0.0).astype(jnp.bfloat16)
        prob_list.append(probs)
        lse_list.append(lse)
        mixed_list.append(
            jnp.dot(probs, values_all[:, lower : lower + HEAD], preferred_element_type=jnp.float32)
        )
    mixed = jnp.concatenate(mixed_list, axis=1).astype(jnp.bfloat16)
    updated = (
        states_single_float + jnp.dot(mixed, out_weight, preferred_element_type=jnp.float32)
    ).astype(jnp.bfloat16)
    partial_out = rows_product(mixed, grads_in)
    d_mixed = cols_product(grads_in, out_weight).astype(jnp.bfloat16)
    score_grads = []
    delta_list = []
    query_grads = []
    for head in range(HEADS):
        lower = head * HEAD
        mixed_head = d_mixed[:, lower : lower + HEAD]
        delta = jnp.sum(
            mixed_head.astype(jnp.float32) * mixed[:, lower : lower + HEAD].astype(jnp.float32),
            axis=1,
            keepdims=True,
        )
        d_probs = cols_product(mixed_head, values_all[:, lower : lower + HEAD])
        d_scores = (prob_list[head].astype(jnp.float32) * (d_probs - delta)).astype(jnp.bfloat16)
        score_grads.append(d_scores)
        delta_list.append(delta)
        query_grads.append(
            jnp.dot(d_scores, keys_all[:, lower : lower + HEAD], preferred_element_type=jnp.float32)
            * scale
        )
    d_queries = jnp.concatenate(query_grads, axis=1).astype(jnp.bfloat16)
    key_pieces = []
    value_pieces = []
    for head in range(HEADS):
        lower = head * HEAD
        score_part = score_grads[head]
        prob_part = prob_list[head]
        key_pieces.append(rows_product(score_part, queries[:, lower : lower + HEAD]) * scale)
        value_pieces.append(rows_product(prob_part, d_mixed[:, lower : lower + HEAD]))
    key_value_grads = lax.psum_scatter(
        jnp.concatenate(key_pieces + value_pieces, axis=1).astype(jnp.bfloat16),
        "node",
        scatter_dimension=0,
        tiled=True,
    ).astype(jnp.float32)
    d_keys = key_value_grads[:, :width].astype(jnp.bfloat16)
    d_values = key_value_grads[:, width:].astype(jnp.bfloat16)
    normalized_gradient = (
        cols_product(d_queries, query_weight)
        + cols_product(d_keys, key_weight)
        + cols_product(d_values, value_weight)
    )
    node_state_gradient = (
        grads_in.astype(jnp.float32)
        + inverse_norm_scale
        * (
            normalized_gradient
            - centered_states
            * jnp.mean(normalized_gradient * centered_states, axis=1, keepdims=True)
        )
    ).astype(jnp.bfloat16)
    partial_query = rows_product(normalized_states, d_queries)
    partial_key = rows_product(normalized_states, d_keys)
    partial_value = rows_product(normalized_states, d_values)
    total_query, total_key, total_value, total_out = lax.psum(
        (partial_query, partial_key, partial_value, partial_out), ("node", "rep")
    )
    return (
        updated[None],
        node_state_gradient[None],
        total_query,
        total_key,
        total_value,
        total_out,
    )

LANES = 128
SLOTS = 16
LEVEL_PARTS = 3
TILE_ROWS = 8
VMEM_LIMIT = 24 * 1024 * 1024


def transposed_product(left, right):
    return lax.dot_general(left, right, CONTRACT_ROWS, preferred_element_type=jnp.float32)


def pair_product(left, right):
    return lax.dot_general(left, right, CONTRACT_COLS, preferred_element_type=jnp.float32)


def plain_product(left, right):
    return jnp.dot(left, right, preferred_element_type=jnp.float32)


def head_lanes(rows, half):
    lanes = lax.broadcasted_iota(jnp.int32, (rows, LANES), 1)
    return (lanes >= HEAD) if half else (lanes < HEAD)


def keep_lanes(array, mask):
    return jnp.where(mask, array, jnp.zeros_like(array))


def split_heads(array):
    rows = array.shape[0]
    return jnp.concatenate(
        [keep_lanes(array, head_lanes(rows, 0)), keep_lanes(array, head_lanes(rows, 1))], axis=0
    )


def merge_heads(array):
    rows = array.shape[0] // 2
    return jnp.where(head_lanes(rows, 0), array[:rows], array[rows:])


def normalize(states):
    wide = states.astype(jnp.float32)
    inverse = lax.rsqrt(jnp.mean(wide * wide, axis=1, keepdims=True) + EPS)
    return wide, inverse, wide * inverse


def level_tables_whole(scalars, levels, total):
    columns = lax.broadcasted_iota(jnp.int32, (SLOTS, total), 1)
    places = columns.astype(jnp.float32)
    slots = lax.broadcasted_iota(jnp.int32, (SLOTS, total), 0)
    level = jnp.zeros((SLOTS, total), jnp.int32)
    for entry in range(1, levels):
        level += (places >= scalars[HEADS, entry]).astype(jnp.int32)
    features = jnp.concatenate(
        [
            (level == slots).astype(jnp.float32),
            ((columns >> 6) == slots).astype(jnp.float32),
        ],
        axis=0,
    ).astype(jnp.bfloat16)
    own = lax.broadcasted_iota(jnp.int32, (SLOTS, LANES), 0)
    lanes = lax.broadcasted_iota(jnp.int32, (SLOTS, LANES), 1)
    part = lanes >> 4
    distance = own - (lanes & (SLOTS - 1))
    tables = []
    for head in range(HEADS):
        table = jnp.full((SLOTS, LANES), NEG, jnp.float32)
        for step in range(1, min(levels, DIST)):
            table = jnp.where(distance == step, scalars[head, step], table)
        high = table.astype(jnp.bfloat16).astype(jnp.float32)
        middle = (table - high).astype(jnp.bfloat16).astype(jnp.float32)
        low = table - high - middle
        split = jnp.where(part == 0, high, jnp.where(part == 1, middle, low))
        tables.append(jnp.where(part < LEVEL_PARTS, split, 0.0))
    table = jnp.concatenate(tables, axis=1).astype(jnp.bfloat16)
    picks_row = lax.broadcasted_iota(jnp.int32, (2 * SLOTS, LANES), 0)
    picks_lane = lax.broadcasted_iota(jnp.int32, (2 * SLOTS, LANES), 1)
    wanted = jnp.where(
        picks_lane < LEVEL_PARTS * SLOTS,
        picks_lane & (SLOTS - 1),
        picks_lane - (LEVEL_PARTS - 1) * SLOTS,
    )
    picks = (wanted == picks_row).astype(jnp.float32).astype(jnp.bfloat16)
    return features, table, transposed_product(features, picks).astype(jnp.bfloat16)


def project(chunk, weights, unit_t, projected):
    unit = normalize(chunk[: projected.shape[0], :])[2]
    unit_t[...] = unit.T.astype(jnp.bfloat16)
    unit = unit.astype(jnp.bfloat16)
    width = projected.shape[1] // 3
    for i, weight in enumerate(weights):
        projected[:, i * width : (i + 1) * width] = plain_product(unit, weight[...]).astype(
            jnp.bfloat16
        )


def tables_kernel(levels, scalars, features, table, column_features):
    rows, level_bias, columns = level_tables_whole(scalars, levels, features.shape[1])
    features[...] = rows
    table[...] = level_bias
    column_features[...] = columns


def project_kernel(chunk, query_w, key_w, value_w, unit_t, projected):
    project(chunk, (query_w, key_w, value_w), unit_t, projected)


def forward_kernel(
    place, scalars, own_states, own_t, own, near_states, near_t, near,
    far_states, far_t, far, last_states, query_w, key_w, value_w, features, table, column_features,
    normed_t, projected, probs, mixed, mixed_t,
    row_table, key_table, last_t, last,
):
    total, width = mixed.shape
    rows = own.shape[0]
    scale = HEAD ** (-0.5)
    project(last_states, (query_w, key_w, value_w), last_t, last)
    chunks = ((own_t, own), (near_t, near), (far_t, far), (last_t, last))
    for index, (unit_t, chunk) in enumerate(chunks):
        at = pl.ds(pl.multiple_of((place[0] ^ index) * rows, rows), rows)
        normed_t[:, at] = unit_t[...]
        projected[at, :] = chunk[...]
    slots = lax.broadcasted_iota(jnp.int32, (SLOTS, HEADS * LANES), 0)
    hidden = jnp.zeros((SLOTS, HEADS * LANES), jnp.float32)
    for index, part in enumerate((own_states, near_states, far_states, last_states)):
        tile = part[rows:, :].astype(jnp.float32)
        for block in range(rows // BLOCK):
            at = (place[0] ^ index) * (rows // BLOCK) + block
            hidden = jnp.where(slots == at, tile[block : block + 1, :], hidden)
    row_table[...] = transposed_product(
        features[...], jnp.concatenate([table[...], hidden.astype(jnp.bfloat16)], axis=0)
    ).astype(jnp.bfloat16)
    for pair in range(HEADS // 2):
        key_table[pair, :, :LANES] = projected[:, width + pair * LANES : width + (pair + 1) * LANES]
        key_table[pair, :, LANES:] = column_features[...]
    same = lax.broadcasted_iota(jnp.int32, (2 * LANES, LANES), 1) == (
        lax.broadcasted_iota(jnp.int32, (2 * LANES, LANES), 0) & (LANES - 1)
    )
    first_half = lax.broadcasted_iota(jnp.int32, (2 * LANES, 1), 0) < LANES
    for pair in range(HEADS // 2):
        lanes = slice(pair * LANES, (pair + 1) * LANES)
        values = slice(2 * width + pair * LANES, 2 * width + (pair + 1) * LANES)
        self_bias = jnp.where(
            first_half, scalars[2 * pair, 0], scalars[2 * pair + 1, 0]
        )
        for tile in range(total // LANES):
            low, high = tile * LANES, (tile + 1) * LANES
            stacked = slice(2 * low, 2 * high)
            query = split_heads(projected[low:high, lanes] * jnp.asarray(scale, jnp.bfloat16))
            key = key_table[pair, low:high, :LANES].astype(jnp.float32)
            self_score = jnp.sum(
                query.astype(jnp.float32) * jnp.concatenate([key, key], axis=0),
                axis=1,
                keepdims=True,
            )
            rest = jnp.concatenate(
                [
                    row_table[low:high, (2 * pair) * LANES : (2 * pair + 1) * LANES],
                    row_table[low:high, (2 * pair + 1) * LANES : (2 * pair + 2) * LANES],
                ],
                axis=0,
            )
            scores = pair_product(
                jnp.concatenate([query, rest], axis=1), key_table[pair, :high, :]
            )
            corner = jnp.where(same, self_score + self_bias, scores[:, low:])
            peak = jnp.max(corner, axis=1, keepdims=True)
            if low:
                peak = jnp.maximum(peak, jnp.max(scores[:, :low], axis=1, keepdims=True))
            corner = jnp.exp(corner - peak)
            mass = jnp.sum(corner, axis=1, keepdims=True)
            if low:
                weight = jnp.exp(scores[:, :low] - peak)
                mass += jnp.sum(weight, axis=1, keepdims=True)
                inverse = 1.0 / mass
                probs[pair, stacked, :low] = (weight * inverse).astype(jnp.bfloat16)
            else:
                inverse = 1.0 / mass
            probs[pair, stacked, low:high] = (corner * inverse).astype(jnp.bfloat16)
            both = merge_heads(
                plain_product(probs[pair, stacked, :high], projected[:high, values])
            )
            mixed[low:high, lanes] = both.astype(jnp.bfloat16)
            mixed_t[lanes, low:high] = both.T.astype(jnp.bfloat16)


def product_halves(place, left, right, keep, send):
    half = keep.shape[0]
    mine = pl.ds(pl.multiple_of(place[1] * half, half), half)
    other = pl.ds(pl.multiple_of((1 - place[1]) * half, half), half)
    send[...] = plain_product(left[other, :], right).astype(jnp.bfloat16)
    keep[...] = plain_product(left[mine, :], right)


def mix_kernel(place, own, near, far, last, out_w, d_mixed):
    rows = own.shape[0]
    for index, chunk in enumerate((own, near, far, last)):
        at = pl.ds(pl.multiple_of((place[0] ^ index) * rows, rows), rows)
        d_mixed[at, :] = pair_product(chunk[...], out_w[...]).astype(jnp.bfloat16)


def output_kernel(place, own, near, far, last, mixed_t, keep, send, gathered):
    rows = own.shape[0]
    for index, chunk in enumerate((own, near, far, last)):
        at = pl.ds(pl.multiple_of((place[0] ^ index) * rows, rows), rows)
        gathered[at, :] = chunk[...]
    product_halves(place, mixed_t, gathered[...], keep, send)


def backward_kernel(
    pair, place, normed_t, projected, probs, mixed, d_mixed,
    d_own, keep, send,
    grads, key_sum, value_sum,
):
    total, width = mixed.shape
    rows = d_own.shape[0]
    scale = HEAD ** (-0.5)
    lanes, key_lanes, value_lanes = (
        slice(i * width + pair * LANES, i * width + (pair + 1) * LANES) for i in range(3)
    )
    for tile in reversed(range(total // LANES)):
        low, high = tile * LANES, (tile + 1) * LANES
        query = split_heads(projected[low:high, lanes])
        mix_grad = split_heads(d_mixed[low:high, lanes])
        mix = mixed[low:high, lanes].astype(jnp.float32)
        delta = jnp.sum(
            mix_grad.astype(jnp.float32) * jnp.concatenate([mix, mix], axis=0),
            axis=1,
            keepdims=True,
        )
        prob = probs[pair, 2 * low : 2 * high, :high]
        d_probs = pair_product(mix_grad, projected[:high, value_lanes])
        score_grad = (prob.astype(jnp.float32) * (d_probs - delta)).astype(jnp.bfloat16)
        grads[low:high, :LANES] = (
            merge_heads(plain_product(score_grad, projected[:high, key_lanes])) * scale
        ).astype(jnp.bfloat16)
        key_term = transposed_product(score_grad, query)
        value_term = transposed_product(prob, mix_grad)
        if high == total:
            key_sum[...] = key_term
            value_sum[...] = value_term
        else:
            key_sum[:high, :] += key_term
            value_sum[:high, :] += value_term
    grads[:, LANES : 2 * LANES] = (key_sum[...] * scale).astype(jnp.bfloat16)
    grads[:, 2 * LANES :] = value_sum[...].astype(jnp.bfloat16)
    product_halves(place, normed_t, grads[...], keep, send)
    d_own[...] = grads[pl.ds(pl.multiple_of(place[0] * rows, rows), rows), :]


def rows_kernel(place, own, grads_in, mixed, query_w, key_w, value_w, out_w, *rest):
    *d_own, updated, gradient = rest
    rows = updated.shape[0]
    width = mixed.shape[1]
    states, inverse, unit = normalize(own[:rows, :])
    here = pl.ds(pl.multiple_of(place[0] * rows, rows), rows)
    updated[...] = (states + plain_product(mixed[here, :], out_w[...])).astype(jnp.bfloat16)
    inner = jnp.zeros(updated.shape, jnp.float32)
    for pair, piece in enumerate(d_own):
        lanes = slice(pair * LANES, (pair + 1) * LANES)
        for i, weight in enumerate((query_w, key_w, value_w)):
            inner += pair_product(piece[:, i * LANES : (i + 1) * LANES], weight[:, lanes])
    gradient[...] = (
        grads_in[...].astype(jnp.float32)
        + inverse * (inner - unit * jnp.mean(inner * unit, axis=1, keepdims=True))
    ).astype(jnp.bfloat16)


def join_kernel(place, *refs):
    mine, other = refs[0:3], refs[3:6]
    total_query, total_key, total_value, total_out = refs[6:]
    for pieces, slot in ((mine, place[1]), (other, 1 - place[1])):
        half = pieces[0].shape[0]
        total_out[pl.ds(pl.multiple_of(slot * half, half), half), :] = pieces[0][...].astype(
            jnp.float32
        )
        half = pieces[1].shape[0]
        at = pl.ds(pl.multiple_of(slot * half, half), half)
        for pair, piece in enumerate(pieces[1:]):
            for i, total in enumerate((total_query, total_key, total_value)):
                total[at, pair * LANES : (pair + 1) * LANES] = piece[
                    :, i * LANES : (i + 1) * LANES
                ].astype(jnp.float32)


def run(kernel, outs, smem, arrays, scratch=(), cost=0):
    out_shape = tuple(jax.ShapeDtypeStruct(shape, dtype) for shape, dtype in outs)
    return pl.pallas_call(
        kernel,
        out_shape=out_shape,
        in_specs=[pl.BlockSpec(memory_space=pltpu.SMEM)] * len(smem)
        + [pl.BlockSpec(memory_space=pltpu.VMEM)] * len(arrays),
        out_specs=tuple([pl.BlockSpec(memory_space=pltpu.VMEM)] * len(outs)),
        scratch_shapes=list(scratch),
        compiler_params=pltpu.CompilerParams(vmem_limit_bytes=VMEM_LIMIT),
        cost_estimate=pl.CostEstimate(
            flops=cost * 1000000000, bytes_accessed=0, transcendentals=0
        ),
    )(*smem, *arrays)


def swap(array, axis, flip):
    return lax.ppermute(array, axis, [(i, i ^ flip) for i in range(lax.axis_size(axis))])


def sum_over_chips(keep, send):
    local = (keep + swap(send, "rep", 1).astype(jnp.float32)).astype(jnp.bfloat16)
    across = swap(local, "rep", 2)
    return local, across


def on_device_whole(
    node_states,
    cotangent,
    reach_blocks,
    reach_count,
    level_start,
    query_weight,
    key_weight,
    value_weight,
    out_weight,
    bias_table,
):
    states = node_states[0]
    grads_in = cotangent[0]
    blocks = reach_blocks[0]
    counts = reach_count[0]
    starts = level_start[0]
    rows, model = states.shape
    width = query_weight.shape[1]
    total = rows * lax.axis_size("node")
    place = jnp.stack([lax.axis_index("node"), lax.axis_index("rep") & 1]).astype(jnp.int32)
    half = jnp.bfloat16
    wide = jnp.float32

    local_blocks = blocks.shape[0]
    shape = (local_blocks, blocks.shape[1], HEADS * LANES)
    kinds = (lax.broadcasted_iota(jnp.int32, shape, 2) & (LANES - 1)) - LEVEL_PARTS * SLOTS
    slots = lax.broadcasted_iota(jnp.int32, shape, 1)
    match = (blocks[:, :, None] == kinds) & (slots < counts[:, None, None])
    match |= (kinds < 0) | (kinds >= SLOTS)
    hidden = (1.0 - jnp.max(match.astype(wide), axis=1)) * NEG
    own = jnp.concatenate(
        [states, jnp.pad(hidden.astype(half), ((0, TILE_ROWS - local_blocks), (0, 0)))], axis=0
    )
    far = swap(own, "node", 2)
    near = swap(own, "node", 1)
    last = swap(far, "node", 1)
    grads_near = swap(grads_in, "node", 1)
    grads_sent, near = lax.optimization_barrier((grads_in, near))
    grads_far = swap(grads_sent, "node", 2)
    scalars = jnp.pad(bias_table, ((0, HEADS), (0, LANES - DIST))) + jnp.pad(
        starts.astype(wide)[None, :], ((HEADS, HEADS - 1), (0, LANES - starts.shape[0]))
    )
    features, table, columns = run(
        functools.partial(tables_kernel, starts.shape[0] - 1),
        [
            ((2 * SLOTS, total), half),
            ((SLOTS, HEADS * LANES), half),
            ((total, LANES), half),
        ],
        [scalars],
        [],
        cost=10,
    )
    weights = [query_weight, key_weight, value_weight]
    table, *weights = lax.optimization_barrier((table, *weights))
    chunk_outs = [((model, rows), half), ((rows, 3 * width), half)]
    own_t, own_p = run(project_kernel, chunk_outs, [], [own, *weights])
    near_t, near_p = run(project_kernel, chunk_outs, [], [near, *weights])
    far_t, far_p = run(project_kernel, chunk_outs, [], [far, *weights])
    grads_far, own_p, near_p, far_p = lax.optimization_barrier((grads_far, own_p, near_p, far_p))
    grads_last = swap(grads_far, "node", 1)
    normed_t, projected, probs, mixed, mixed_t = run(
        forward_kernel,
        [
            ((model, total), half),
            ((total, 3 * width), half),
            ((HEADS // 2, 2 * total, total), half),
            ((total, width), half),
            ((width, total), half),
        ],
        [place, scalars],
        [
            own, own_t, own_p, near, near_t, near_p, far, far_t, far_p, last, *weights,
            features, table, columns,
        ],
        [
            pltpu.VMEM((total, HEADS * LANES), half),
            pltpu.VMEM((HEADS // 2, total, 2 * LANES), half),
            pltpu.VMEM((model, rows), half),
            pltpu.VMEM((rows, 3 * width), half),
        ],
        cost=5,
    )
    d_mixed = run(
        mix_kernel,
        [((total, width), half)],
        [place],
        [grads_in, grads_near, grads_far, grads_last, out_weight],
    )[0]
    halves = []
    d_own = []
    for pair in range(HEADS // 2):
        if pair == 1:
            local, across = halves[0]
            grads_last, keep = lax.optimization_barrier((grads_last, keep))
            out_keep, out_send = run(
                output_kernel,
                [((width // 2, model), wide), ((width // 2, model), half)],
                [place],
                [grads_in, grads_near, grads_far, grads_last, mixed_t],
                [pltpu.VMEM((total, model), half)],
            )
            d_mixed, local, out_send = lax.optimization_barrier((d_mixed, local, out_send))
            halves[0] = (local, across)
        own_grads, keep, send = run(
            functools.partial(backward_kernel, pair),
            [
                ((rows, 3 * LANES), half),
                ((model // 2, 3 * LANES), wide),
                ((model // 2, 3 * LANES), half),
            ],
            [place],
            [normed_t, projected, probs, mixed, d_mixed],
            [
                pltpu.VMEM((total, 3 * LANES), half),
                pltpu.VMEM((total, LANES), wide),
                pltpu.VMEM((total, LANES), wide),
            ],
        )
        d_own.append(own_grads)
        halves.append(sum_over_chips(keep, send))
    halves.append(sum_over_chips(out_keep, out_send))
    d_own[-1], _ = lax.optimization_barrier((d_own[-1], halves[1][0]))
    updated, node_state_gradient = run(
        rows_kernel,
        [((rows, model), half)] * 2,
        [place],
        [own, grads_in, mixed, *weights, out_weight, *d_own],
    )
    first, node_state_gradient = lax.optimization_barrier((halves[0][1], node_state_gradient))
    halves[0] = (halves[0][0], first)
    mine = [
        (near_sum.astype(wide) + far_sum.astype(wide)).astype(half) for near_sum, far_sum in halves
    ]
    other = [swap(piece, "rep", 1) for piece in mine]
    total_query, total_key, total_value, total_out = run(
        join_kernel,
        [((model, width), wide)] * 3 + [((width, model), wide)],
        [place],
        [mine[-1], *mine[:-1], other[-1], *other[:-1]],
    )
    return (
        updated[None],
        node_state_gradient[None],
        total_query,
        total_key,
        total_value,
        total_out,
    )


def on_device(node_states, cotangent, reach_blocks, reach_count, level_start, *rest):
    nodes = lax.axis_size("node")
    total = node_states.shape[1] * nodes
    small = (
        nodes == 4
        and lax.axis_size("rep") == 4
        and node_states.shape[1] == LANES
        and total // BLOCK <= SLOTS
        and level_start.shape[1] - 1 <= SLOTS
    )
    path = on_device_whole if small else on_device_general
    return path(node_states, cotangent, reach_blocks, reach_count, level_start, *rest)


def solution(mesh):
    in_specs = (
        P(("groups", "rep"), "node", None),
        P(("groups", "rep"), "node", None),
        P(("groups", "rep"), "node", None),
        P(("groups", "rep"), "node"),
        P(("groups", "rep"), None),
        P(),
        P(),
        P(),
        P(),
        P(),
    )
    out_specs = (
        P(("groups", "rep"), "node", None),
        P(("groups", "rep"), "node", None),
        P("groups", None),
        P("groups", None),
        P("groups", None),
        P("groups", None),
    )
    return jax.shard_map(
        on_device, mesh=mesh, in_specs=in_specs, out_specs=out_specs, check_vma=False
    )
```
